32 devices in a mesh: dp: 2 (over x), seq: 4 (over z), tensor: 4 (over y, core).
Axes of the slice: x: 2, y: 2, z: 4, core: 2. Of those that a mesh axis runs over, the one named last changes fastest.
Arguments:
- tokens: bfloat16 [2, 4, 1024, 768], P('dp', 'seq'), may hold values from -6 to 6
- branch: int32 [2, 4], P('dp', 'seq'), may hold values from 1024 to 2048, as said below
- w_attn: bfloat16 [3, 768, 768], P(None, None, 'tensor'), may hold values from -0.3125 to 0.3125
- w_proj: bfloat16 [768, 768], P('tensor'), may hold values from -6 to 6
- w_expand: bfloat16 [768, 3072], P(None, 'tensor'), may hold values from -0.21875 to 0.21875
- w_contract: bfloat16 [3072, 768], P('tensor'), may hold values from -0.4375 to 0.4375
- attn_bias: float32 [2, 768], P(None, 'tensor'), may hold values from -3 to 3
- branch_bias: float32 [2, 768], replicated, may hold values from -4 to 4
- expand_bias: float32 [3072], P('tensor'), may hold values from -3 to 3
- norm_gains: float32 [2, 768], replicated, may hold values from 0.5 to 1.5
- norm_shifts: float32 [2, 768], replicated, may hold values from -3 to 3
- cotangent: bfloat16 [2, 4, 1024, 768], P('dp', 'seq'), may hold values from -6 to 6
Outputs:
- layer_out: bfloat16 [2, 4, 1024, 768], P('dp', 'seq', 'tensor')
- grad_tokens: bfloat16 [2, 4, 1024, 768], P('dp', 'seq', 'tensor')
- grad_attn: float32 [3, 768, 768], P(None, ('dp', 'seq'), 'tensor')
- grad_proj: float32 [768, 768], P('tensor', ('dp', 'seq'))
- grad_expand: float32 [768, 3072], P(('dp', 'seq'), 'tensor')
- grad_contract: float32 [3072, 768], P('tensor', ('dp', 'seq'))
- grad_attn_bias: float32 [2, 768], P(None, 'tensor')
- grad_branch_bias: float32 [2, 768], replicated
- grad_expand_bias: float32 [3072], P('tensor')
- grad_norm_gains: float32 [2, 768], replicated
- grad_norm_shifts: float32 [2, 768], replicated
The draws below stay inside these ranges and needn't reach their ends.
Inputs may be any that keep to these rules, and one draw needn't show every extreme that they name: branch[g, 0] equals 2048 in every group: the first continuation sees the whole prompt.
All inputs are finite; a program needn't handle non-finite values.
Results may differ from the reference program's by a relative error of at most 0.013.
The reference program's roundings to bfloat16 on the way count: a program that leaves them out, or rounds other values in their place, can miss the bound.
Values may be sent and summed in bfloat16 or wider, within the bound.
A program may use at most 192 MiB of HBM per device.

```python
import math
import jax
import jax.numpy as jnp
from jax import lax

D = 768
HEADS = 12
HEAD_DIM = 64
FF = 3072
LAYERS = 12
PCH = 512
CLEN = 512
GROUPS = 2
PROMPT = 2048
ROWS = 1024
N_SEQ = 4


def draw_branch(key, part):
    starts = jax.random.randint(key, (GROUPS, N_SEQ), PROMPT // 2, PROMPT + 1)
    columns = jnp.arange(N_SEQ)[None, :]
    return jnp.where(columns == 0, PROMPT, starts).astype(jnp.int32)


def raised(values, key, source, target, parts, factor):
    def block_of(axis_at):
        return (jnp.arange(values.shape[axis_at]) // (values.shape[axis_at] // parts)).reshape((-1,) + (1,) * (values.ndim - 1 - axis_at))

    near = jax.random.permutation(key, parts)[block_of(target)]
    other_side = (block_of(target) + parts // 2) % parts
    return jnp.where((block_of(source) == near) | (block_of(source) == other_side), factor * values, values)


def shard_levels(rng, dims, cuts, low, high):
    def one(axis_at, blocks):
        heights = jax.random.uniform(jax.random.fold_in(jax.random.fold_in(rng, 6), axis_at), (blocks,), jnp.float32, low / len(cuts), high / len(cuts))
        return jnp.repeat(jnp.exp(heights), dims[axis_at] // blocks).reshape((-1,) + (1,) * (len(dims) - axis_at - 1))

    level = one(*cuts[0])
    for cut in cuts[1:]:
        level = level * one(*cut)
    return level


def bell_draw(rng, shape, scale, most, pieces=(), kind=jnp.bfloat16):
    drawn = scale * jax.random.normal(rng, shape, jnp.float32)
    if pieces:
        drawn = drawn * shard_levels(rng, shape, pieces, -0.22, 0.18)
    return jnp.clip(drawn, -most, most).astype(kind)


def gaussian_with(rng, extent, scale, reach, shards, heavy, dtype=jnp.bfloat16):
    drawn = scale * jax.random.normal(rng, extent, jnp.float32)
    if shards:
        drawn = drawn * shard_levels(rng, extent, shards, -0.22, 0.18)
    return jnp.clip(raised(drawn, jax.random.fold_in(rng, 3), *heavy), -reach, reach).astype(dtype)


def setup_inputs(seed: int = 0) -> dict:
    key_list = jax.random.split(jax.random.key(seed), 13)
    return {
        "tokens": bell_draw(key_list[0], (GROUPS, N_SEQ, ROWS, D), 1.0, 6.0, ((0, 2), (1, 4))),
        "branch": draw_branch(jax.random.fold_in(key_list[12], 71), 0),
        "w_attn": bell_draw(key_list[2], (3, D, D), (D // 2) ** -0.5, 0.3125, ((2, 4),)),
        "w_proj": bell_draw(key_list[3], (D, D), (max(D // 1024, 1)) ** -0.5, 6.0, ((0, 4),)),
        "w_expand": bell_draw(key_list[4], (D, FF), D ** -0.5, 0.21875, ((1, 4),)),
        "w_contract": bell_draw(key_list[5], (FF, D), (FF // 16) ** -0.5, 0.4375, ((0, 4),)),
        "attn_bias": bell_draw(key_list[6], (2, D), 0.5, 3.0, ((1, 4),), jnp.float32),
        "branch_bias": bell_draw(key_list[7], (2, D), 1.0, 4.0, (), jnp.float32),
        "expand_bias": bell_draw(key_list[8], (FF,), 0.5, 3.0, ((0, 4),), jnp.float32),
        "norm_gains": jnp.clip(1.0 + 0.1 * jax.random.normal(key_list[9], (2, D), jnp.float32), 0.5, 1.5),
        "norm_shifts": bell_draw(key_list[10], (2, D), 0.5, 3.0, (), jnp.float32),
        "cotangent": gaussian_with(key_list[11], (GROUPS, N_SEQ, ROWS, D), 1.0, 6.0, ((0, 2), (1, 4)), (0, 3, 2, 2.0)),
    }


@jax.custom_vjp
def low(v):
    return lax.optimization_barrier(v.astype(jnp.bfloat16)).astype(jnp.float32)

@jax.custom_vjp
def low_back(v):
    return v

def low_keep(v):
    return (low(v), None)

def low_pass(kept, grad):
    return (grad,)

def back_keep(v):
    return (v, None)

def back_low(kept, grad):
    return (low(grad),)
low.defvjp(low_keep, low_pass)
low_back.defvjp(back_keep, back_low)
norm_eps = 1e-05
big_negative = -1000000000.0
highest = lax.Precision.HIGHEST

def layer_norm(value, gain, shift):
    centre = lax.optimization_barrier(jnp.mean(value, axis=-1, keepdims=True))
    centred = value - centre
    spread = lax.optimization_barrier(jnp.mean(centred * centred, axis=-1, keepdims=True))
    return centred * lax.rsqrt(spread + norm_eps) * gain + shift

def softmax_rows(scores):
    highest_score = lax.optimization_barrier(jnp.max(scores, axis=-1, keepdims=True))
    exponent = jnp.exp(scores - highest_score)
    return exponent / lax.optimization_barrier(jnp.sum(exponent, axis=-1, keepdims=True))

def group_layer(params, group_tokens, group_branch):
    w_attn, w_proj, w_expand, w_contract, attn_bias, branch_bias, expand_bias, norm_gains, norm_shifts = params
    blocks = group_tokens.shape[0]
    prompt = blocks * PCH
    layer_scale = 1.0 / math.sqrt(LAYERS)
    score_scale = 1.0 / math.sqrt(HEAD_DIM)
    flat_rows = group_tokens.reshape(blocks * (PCH + CLEN), D)
    normed_one = low(layer_norm(flat_rows, norm_gains[0], norm_shifts[0]))
    queries = low(low_back(jnp.dot(normed_one, w_attn[0], precision=highest) + attn_bias[0]))
    keys = low(low_back(jnp.dot(normed_one, w_attn[1], precision=highest)))
    values = low(low_back(jnp.dot(normed_one, w_attn[2], precision=highest) + attn_bias[1]))

    def split_rows(inner):
        inner = inner.reshape(blocks, PCH + CLEN, HEADS, HEAD_DIM)
        return (inner[:, :PCH].reshape(prompt, HEADS, HEAD_DIM), inner[:, PCH:])
    query_prompt, query_cont = split_rows(queries)
    key_prompt, key_cont = split_rows(keys)
    value_prompt, value_cont = split_rows(values)
    places = jnp.arange(prompt)
    allowed_prompt = places[None, :] <= places[:, None]
    scores_prompt = low_back(jnp.einsum('ihd,jhd->hij', query_prompt, key_prompt, precision=highest) * score_scale)
    probs_prompt = low(softmax_rows(jnp.where(allowed_prompt[None], scores_prompt, big_negative)))
    out_prompt = jnp.einsum('hij,jhd->ihd', probs_prompt, value_prompt, precision=highest).reshape(blocks, PCH, D)
    cross = jnp.einsum('cihd,jhd->chij', query_cont, key_prompt, precision=highest)
    own = jnp.einsum('cihd,cjhd->chij', query_cont, key_cont, precision=highest)
    scores_cont = low_back(jnp.concatenate([cross, own], axis=-1) * score_scale)
    cont_places = jnp.arange(CLEN)
    seen_prompt = places[None, None, :] < group_branch[:, None, None]
    seen_prompt = jnp.broadcast_to(seen_prompt, (blocks, CLEN, prompt))
    seen_own = jnp.broadcast_to(cont_places[None, :] <= cont_places[:, None], (blocks, CLEN, CLEN))
    allowed_cont = jnp.concatenate([seen_prompt, seen_own], axis=-1)[:, None]
    probs_cont = low(softmax_rows(jnp.where(allowed_cont, scores_cont, big_negative)))
    out_cont = jnp.einsum('chij,jhd->cihd', probs_cont[..., :prompt], value_prompt, precision=highest)
    out_cont = out_cont + jnp.einsum('chij,cjhd->cihd', probs_cont[..., prompt:], value_cont, precision=highest)
    out_cont = out_cont.reshape(blocks, CLEN, D)
    attended = jnp.concatenate([out_prompt, out_cont], axis=1).reshape(blocks * (PCH + CLEN), D)
    attended = low(low_back(attended))
    attn_branch = low_back(jnp.dot(attended, w_proj, precision=highest) + branch_bias[0])
    hidden = flat_rows + layer_scale * attn_branch
    normed_two = low(layer_norm(hidden, norm_gains[1], norm_shifts[1]))
    preact = low_back(jnp.dot(normed_two, w_expand, precision=highest) + expand_bias)
    activated = low(jax.nn.gelu(preact, approximate=True))
    mlp_branch = low_back(jnp.dot(activated, w_contract, precision=highest) + branch_bias[1])
    result = hidden + layer_scale * mlp_branch
    return result.reshape(group_tokens.shape)

def reference(tokens, branch, w_attn, w_proj, w_expand, w_contract, attn_bias, branch_bias, expand_bias, norm_gains, norm_shifts, cotangent):
    params = tuple((item.astype(jnp.float32) for item in (w_attn, w_proj, w_expand, w_contract, attn_bias, branch_bias, expand_bias, norm_gains, norm_shifts)))
    inputs = tokens.astype(jnp.float32)
    checked = jax.checkpoint(group_layer)

    def forward(weights, layer_in):
        return lax.map(lambda pair: checked(weights, pair[0], pair[1]), (layer_in, branch))
    result, pullback = jax.vjp(forward, params, inputs)
    grads, grad_in = pullback(cotangent.astype(jnp.float32))
    return (result.astype(jnp.bfloat16), grad_in.astype(jnp.bfloat16), grads[0], grads[1], grads[2], grads[3], grads[4], grads[5], grads[6], grads[7], grads[8])
```

```python
import math

import jax
import jax.numpy as jnp
from jax import lax
from jax.sharding import PartitionSpec as P

HEAD_DIM = 64
LAYERS = 12
PCH = 512
CLEN = 512
F32 = jnp.float32
BF16 = jnp.bfloat16


norm_eps = 1e-05
big_negative = -1000000000.0


def layer_norm_parts(value):
    centre = jnp.mean(value, axis=-1, keepdims=True)
    centred = value - centre
    spread = jnp.mean(centred * centred, axis=-1, keepdims=True)
    inverse = lax.rsqrt(spread + norm_eps)
    return centred * inverse, inverse


def layer_norm_back(grad, gain, xhat, inverse):
    e = grad * gain
    return inverse * (
        e
        - jnp.mean(e, axis=-1, keepdims=True)
        - xhat * jnp.mean(e * xhat, axis=-1, keepdims=True)
    )


def scores_of(queries, all_keys, allowed, score_scale):
    raw = jnp.einsum("ihd,jhd->hij", queries, all_keys, preferred_element_type=F32) * score_scale
    return jnp.where(allowed[None], raw, big_negative)


def attend(queries, all_keys, all_values, allowed, score_scale):
    scores = scores_of(queries, all_keys, allowed, score_scale)
    highest_score = jnp.max(scores, axis=-1, keepdims=True)
    exponent = jnp.exp(scores - highest_score)
    totals = jnp.sum(exponent, axis=-1, keepdims=True)
    chances = (exponent / totals).astype(BF16)
    result = jnp.einsum("hij,jhd->ihd", chances, all_values, preferred_element_type=F32)
    return (result, highest_score + jnp.log(totals))


def attend_back(queries, all_keys, all_values, allowed, score_scale, logsum, grad_result):
    scores = scores_of(queries, all_keys, allowed, score_scale)
    chances = jnp.exp(scores - logsum)
    grad_chances = jnp.einsum("ihd,jhd->hij", grad_result, all_values, preferred_element_type=F32)
    row_dot = jnp.sum(chances * grad_chances, axis=-1, keepdims=True)
    grad_scores = (chances * (grad_chances - row_dot)).astype(BF16)
    grad_values = jnp.einsum(
        "hij,ihd->jhd", chances.astype(BF16), grad_result, preferred_element_type=F32
    )
    grad_queries = (
        jnp.einsum("hij,jhd->ihd", grad_scores, all_keys, preferred_element_type=F32) * score_scale
    )
    grad_keys = (
        jnp.einsum("hij,ihd->jhd", grad_scores, queries, preferred_element_type=F32) * score_scale
    )
    return (grad_queries, grad_keys, grad_values)


def gelu_tanh(inner):
    return jax.nn.gelu(inner, approximate=True)


def swap(value, axis, bit):
    size = lax.axis_size(axis)
    return lax.ppermute(value, axis, [(i, i ^ bit) for i in range(size)])


def bits_of(axis):
    size = lax.axis_size(axis)
    return [1 << k for k in range(size.bit_length() - 1)]


def halve(value, axis, bit):
    mine = (lax.axis_index(axis) // bit) % 2
    kept = lax.dynamic_index_in_dim(value, mine, 1, keepdims=False)
    sent = lax.dynamic_index_in_dim(value, 1 - mine, 1, keepdims=False)
    return kept + swap(sent.astype(BF16), axis, bit).astype(F32)


def scatter_sum(value, steps):
    axes = ("dp", "seq")
    bits = [(axis, bit) for axis in axes for bit in reversed(bits_of(axis))]
    bits = [b for b in bits if b in steps]
    rows, columns = value.shape
    left = list(bits)
    for step in steps:
        place = left.index(step)
        pre, post = 1 << place, 1 << (len(left) - place - 1)
        block = rows >> len(left)
        rows //= 2
        value = halve(value.reshape(pre, 2, post * block, columns), *step)
        left.remove(step)
        value = value.reshape(rows, columns)
    return value


def total_over(value, axes):
    for axis in axes:
        for bit in bits_of(axis):
            value = value + swap(value, axis, bit)
    return value


def gather_line(value, axis):
    size = lax.axis_size(axis)
    index = lax.axis_index(axis)
    up = [(i, i + 1) for i in range(size - 1)]
    down = [(i + 1, i) for i in range(size - 1)]
    whole = jnp.zeros((size,) + value.shape, value.dtype)
    whole = lax.dynamic_update_index_in_dim(whole, value, index, 0)
    from_below = from_above = value
    for step in range(1, size):
        from_below = lax.ppermute(from_below, axis, up[step - 1 :])
        from_above = lax.ppermute(from_above, axis, down[: size - step])
        place = jnp.maximum(index - step, 0)
        old = lax.dynamic_index_in_dim(whole, place, 0, keepdims=False)
        whole = lax.dynamic_update_index_in_dim(
            whole, jnp.where(index >= step, from_below, old), place, 0
        )
        place = jnp.minimum(index + step, size - 1)
        old = lax.dynamic_index_in_dim(whole, place, 0, keepdims=False)
        whole = lax.dynamic_update_index_in_dim(
            whole, jnp.where(index + step < size, from_above, old), place, 0
        )
    return whole


def tensor_scatter(part):
    far = swap(part(3).astype(BF16), "tensor", 1).astype(F32)
    across = swap((part(2) + far).astype(BF16), "tensor", 2).astype(F32)
    near = swap(part(1).astype(BF16), "tensor", 1).astype(F32)
    return part(0) + near + across


def tensor_gather(own):
    across = swap(own, "tensor", 2)
    near = swap(own, "tensor", 1)
    far = swap(across, "tensor", 1)
    return jnp.concatenate([own, near, across, far], axis=0)


def shards(
    tokens,
    branch,
    w_attn,
    w_proj,
    w_expand,
    w_contract,
    attn_bias,
    branch_bias,
    expand_bias,
    norm_gains,
    norm_shifts,
    cotangent,
):
    seq_count = lax.axis_size("seq")
    seq_index = lax.axis_index("seq")
    tensor_count = lax.axis_size("tensor")
    tensor_index = lax.axis_index("tensor")
    width = tokens.shape[3]
    row_count = tokens.shape[2]
    share = row_count // tensor_count
    local_width = w_attn.shape[2]
    local_heads = local_width // HEAD_DIM
    prompt = PCH * seq_count
    score_scale = 1.0 / math.sqrt(HEAD_DIM)
    layer_scale = 1.0 / math.sqrt(LAYERS)

    def slot(whole, k):
        start = jnp.bitwise_xor(tensor_index, k) * share
        return lax.dynamic_slice_in_dim(whole, start, share, 0)

    def relative(whole):
        return jnp.concatenate([slot(whole, k) for k in range(tensor_count)], axis=0)

    def rows_at(whole, k):
        return whole[k * share : (k + 1) * share]

    token_rows = tokens.reshape(row_count, width)
    cotangent_rows = cotangent.reshape(row_count, width)
    flat_rows = token_rows.astype(F32)
    normed_one = (
        layer_norm_parts(flat_rows)[0] * norm_gains[0] + norm_shifts[0]
    ).astype(BF16)
    projected = jnp.einsum("rd,cde->cre", normed_one, w_attn, preferred_element_type=F32)
    bias_rows = jnp.stack([attn_bias[0], jnp.zeros_like(attn_bias[0]), attn_bias[1]])
    projected = (projected + bias_rows[:, None, :]).astype(BF16)
    query_flat, key_flat, value_flat = (projected[0], projected[1], projected[2])
    gathered = gather_line(jnp.stack([key_flat[:PCH], value_flat[:PCH]]), "seq")
    gathered_keys = gathered[:, 0].reshape(prompt, local_width)
    gathered_values = gathered[:, 1].reshape(prompt, local_width)

    grad_mlp = (relative(cotangent_rows).astype(F32) * layer_scale).astype(BF16)
    grad_activated = jnp.einsum("rd,fd->rf", grad_mlp, w_contract, preferred_element_type=F32)

    def heads_of(flat):
        return flat.reshape(flat.shape[0], local_heads, HEAD_DIM)

    query_prompt = heads_of(query_flat[:PCH])
    query_cont = heads_of(query_flat[PCH:])
    places = jnp.arange(prompt)
    positions = seq_index * PCH + jnp.arange(PCH)
    allowed_prompt = places[None, :] <= positions[:, None]
    cont_places = jnp.arange(CLEN)
    branch_end = branch[0, 0]
    allowed_cont = jnp.concatenate(
        [
            jnp.broadcast_to(places[None, :] < branch_end, (CLEN, prompt)),
            cont_places[None, :] <= cont_places[:, None],
        ],
        axis=1,
    )
    keys_prompt = heads_of(gathered_keys)
    values_prompt = heads_of(gathered_values)
    keys_cont = jnp.concatenate([keys_prompt, heads_of(key_flat[PCH:])], axis=0)
    values_cont = jnp.concatenate([values_prompt, heads_of(value_flat[PCH:])], axis=0)
    out_prompt, logsum_prompt = attend(
        query_prompt, keys_prompt, values_prompt, allowed_prompt, score_scale
    )
    out_cont, logsum_cont = attend(query_cont, keys_cont, values_cont, allowed_cont, score_scale)
    attended = (
        jnp.concatenate([out_prompt, out_cont], axis=0)
        .reshape(row_count, local_width)
        .astype(BF16)
    )
    attended = relative(attended)
    attn_summed = tensor_scatter(
        lambda k: jnp.dot(rows_at(attended, k), w_proj, preferred_element_type=F32)
    )
    own_tokens = slot(token_rows, 0).astype(F32)
    own_cotangent = slot(cotangent_rows, 0).astype(F32)
    hidden = own_tokens + layer_scale * (attn_summed + branch_bias[0])
    xhat_two, inverse_two = layer_norm_parts(hidden)
    own_normed_two = (xhat_two * norm_gains[1] + norm_shifts[1]).astype(BF16)
    normed_two = tensor_gather(own_normed_two)
    preact = jnp.dot(normed_two, w_expand, preferred_element_type=F32) + expand_bias
    gelu_value, gelu_back = jax.vjp(gelu_tanh, preact)
    activated = gelu_value.astype(BF16)
    grad_preact = gelu_back(grad_activated)[0].astype(BF16)
    grad_mixed = tensor_scatter(
        lambda k: jnp.einsum(
            "rf,df->rd", rows_at(grad_preact, k), w_expand, preferred_element_type=F32
        )
    )
    grad_hidden = own_cotangent + layer_norm_back(
        grad_mixed, norm_gains[1], xhat_two, inverse_two
    )
    own_grad_att = (grad_hidden * layer_scale).astype(BF16)
    grad_att = tensor_gather(own_grad_att)
    grad_attended = jnp.einsum("rd,ed->re", grad_att, w_proj, preferred_element_type=F32).astype(
        BF16
    )
    grad_attended = heads_of(relative(grad_attended))

    mlp_summed = tensor_scatter(
        lambda k: jnp.dot(rows_at(activated, k), w_contract, preferred_element_type=F32)
    )
    layer_out = (hidden + layer_scale * (mlp_summed + branch_bias[1])).astype(BF16)

    bits = [("dp", b) for b in bits_of("dp")]
    seq_bits = [("seq", b) for b in bits_of("seq")]
    grad_contract = jnp.einsum("rf,rd->df", activated, grad_mlp, preferred_element_type=F32)
    grad_contract = scatter_sum(grad_contract, bits + seq_bits).T
    grad_expand = jnp.einsum("rd,rf->df", normed_two, grad_preact, preferred_element_type=F32)
    grad_expand = scatter_sum(grad_expand, seq_bits + bits)
    grad_proj = jnp.einsum("re,rd->de", attended, grad_att, preferred_element_type=F32)
    grad_proj = scatter_sum(grad_proj, seq_bits + bits).T

    grad_query_prompt, grad_key_pp, grad_value_pp = attend_back(
        query_prompt,
        keys_prompt,
        values_prompt,
        allowed_prompt,
        score_scale,
        logsum_prompt,
        grad_attended[:PCH],
    )
    grad_query_cont, grad_key_cont, grad_value_cont = attend_back(
        query_cont,
        keys_cont,
        values_cont,
        allowed_cont,
        score_scale,
        logsum_cont,
        grad_attended[PCH:],
    )
    prompt_terms = jnp.concatenate(
        [
            (grad_key_pp + grad_key_cont[:prompt]).reshape(prompt, local_width),
            (grad_value_pp + grad_value_cont[:prompt]).reshape(prompt, local_width),
        ],
        axis=1,
    )
    own_terms = scatter_sum(prompt_terms, seq_bits)
    own_keys, own_values = own_terms[:, :local_width], own_terms[:, local_width:]
    grad_keys = jnp.concatenate(
        [own_keys, grad_key_cont[prompt:].reshape(CLEN, local_width)], axis=0
    ).astype(BF16)
    grad_values = jnp.concatenate(
        [own_values, grad_value_cont[prompt:].reshape(CLEN, local_width)], axis=0
    ).astype(BF16)
    grad_queries = (
        jnp.concatenate([grad_query_prompt, grad_query_cont], axis=0)
        .reshape(row_count, local_width)
        .astype(BF16)
    )
    stacked = jnp.concatenate([grad_queries, grad_keys, grad_values], axis=1)
    w_flat = jnp.transpose(w_attn, (1, 0, 2)).reshape(width, 3 * local_width)
    stacked_slots = relative(stacked)
    grad_normed = tensor_scatter(
        lambda k: jnp.einsum(
            "re,de->rd", rows_at(stacked_slots, k), w_flat, preferred_element_type=F32
        )
    )
    grad_attn = jnp.einsum("rd,re->de", normed_one, stacked, preferred_element_type=F32)
    grad_attn = scatter_sum(grad_attn, bits + seq_bits)
    grad_attn = jnp.transpose(grad_attn.reshape(-1, 3, local_width), (1, 0, 2))
    xhat_one, inverse_one = layer_norm_parts(own_tokens)
    grad_tokens = (
        grad_hidden + layer_norm_back(grad_normed, norm_gains[0], xhat_one, inverse_one)
    ).astype(BF16)

    everywhere = ("dp", "seq", "tensor")
    early = total_over(
        jnp.stack(
            [
                jnp.sum(own_grad_att.astype(F32), axis=0),
                jnp.sum(rows_at(grad_mlp, 0).astype(F32), axis=0),
                jnp.sum(grad_mixed * xhat_two, axis=0),
                jnp.sum(grad_mixed, axis=0),
            ]
        ),
        everywhere,
    )
    late = total_over(
        jnp.stack([jnp.sum(grad_normed * xhat_one, axis=0), jnp.sum(grad_normed, axis=0)]),
        everywhere,
    )
    expand_terms = total_over(jnp.sum(grad_preact.astype(F32), axis=0), ("dp", "seq"))
    bias_terms = total_over(
        jnp.stack(
            [
                jnp.sum(grad_queries.astype(F32), axis=0),
                jnp.sum(grad_values.astype(F32), axis=0),
            ]
        ),
        ("dp", "seq"),
    )
    out_shape = (1, 1, share, width)
    return (
        layer_out.reshape(out_shape),
        grad_tokens.reshape(out_shape),
        grad_attn,
        grad_proj,
        grad_expand,
        grad_contract,
        bias_terms,
        early[:2],
        expand_terms,
        jnp.stack([late[0], early[2]]),
        jnp.stack([late[1], early[3]]),
    )


def solution(mesh):
    placed = (
        P("dp", "seq", None, None),
        P("dp", "seq"),
        P(None, None, "tensor"),
        P("tensor", None),
        P(None, "tensor"),
        P("tensor", None),
        P(None, "tensor"),
        P(),
        P("tensor"),
        P(),
        P(),
        P("dp", "seq", None, None),
    )
    return jax.shard_map(
        shards,
        mesh=mesh,
        in_specs=placed,
        out_specs=(
            P("dp", "seq", "tensor", None),
            P("dp", "seq", "tensor", None),
            P(None, ("dp", "seq"), "tensor"),
            P("tensor", ("dp", "seq")),
            P(("dp", "seq"), "tensor"),
            P("tensor", ("dp", "seq")),
            P(None, "tensor"),
            P(),
            P("tensor"),
            P(),
            P(),
        ),
        check_vma=False,
    )
```

```python
import functools
import math

import jax
import jax.numpy as jnp
from jax import lax
from jax.experimental import pallas as pl
from jax.experimental.pallas import tpu as pltpu
from jax.sharding import PartitionSpec as P

HEAD_DIM = 64
LAYERS = 12
PCH = 512
CLEN = 512
F32 = jnp.float32
BF16 = jnp.bfloat16


norm_eps = 1e-05
big_negative = -1000000000.0


def layer_norm_parts(value):
    centre = jnp.mean(value, axis=-1, keepdims=True)
    centred = value - centre
    spread = jnp.mean(centred * centred, axis=-1, keepdims=True)
    inverse = lax.rsqrt(spread + norm_eps)
    return centred * inverse, inverse


def layer_norm_back(grad, gain, xhat, inverse):
    e = grad * gain
    return inverse * (
        e
        - jnp.mean(e, axis=-1, keepdims=True)
        - xhat * jnp.mean(e * xhat, axis=-1, keepdims=True)
    )


def forward_kernel(n, heads, q_ref, kv_ref, branch_ref, o_ref, of_ref, lse_ref, kv_all, m_sc, l_sc, acc, up_send, up_recv, down_send, down_recv):
    z = lax.axis_index("seq")
    feats = heads * HEAD_DIM
    barrier = pltpu.get_barrier_semaphore()
    has_up, has_down = z < n - 1, z > 0

    def meet(to):
        pl.semaphore_signal(barrier, inc=1, device_id={"seq": to}, device_id_type=pl.DeviceIdType.MESH)

    @pl.when(has_up)
    def _(): meet(z + 1)
    @pl.when(has_down)
    def _(): meet(z - 1)
    pl.semaphore_wait(barrier, has_up.astype(jnp.int32) + has_down.astype(jnp.int32))

    own = kv_ref.at[:, 0:PCH]

    def hop(src, block, step, to, send, recv):
        return pltpu.make_async_remote_copy(src_ref=src, dst_ref=kv_all.at[block], send_sem=send.at[step], recv_sem=recv.at[step], device_id={"seq": to}, device_id_type=pl.DeviceIdType.MESH)

    @pl.when(has_up)
    def _(): hop(own, z, 0, z + 1, up_send, up_recv).start()
    @pl.when(has_down)
    def _(): hop(own, z, 0, z - 1, down_send, down_recv).start()

    def load_q(h, c):
        return q_ref[pl.ds(pl.multiple_of(h * HEAD_DIM, HEAD_DIM), HEAD_DIM), pl.ds(pl.multiple_of(c * PCH, PCH), PCH)]

    def scores(k, q):
        return lax.dot_general(k, q, (((0,), (0,)), ((), ())), preferred_element_type=F32)

    def diag(i, carry):
        c, h = i // heads, i % heads
        rows = pl.ds(pl.multiple_of(h * HEAD_DIM, HEAD_DIM), HEAD_DIM)
        vrows = pl.ds(pl.multiple_of(feats + h * HEAD_DIM, HEAD_DIM), HEAD_DIM)
        cols = pl.ds(pl.multiple_of(c * PCH, PCH), PCH)
        s = scores(kv_ref[rows, cols], load_q(h, c))
        key = lax.broadcasted_iota(jnp.int32, s.shape, 0)
        query = lax.broadcasted_iota(jnp.int32, s.shape, 1)
        s = jnp.where(key <= query, s, big_negative)
        m = jnp.max(s, axis=0, keepdims=True)
        p = jnp.exp(s - m)
        m_sc[h, :, cols] = m
        l_sc[h, :, cols] = jnp.sum(p, axis=0, keepdims=True)
        acc[rows, cols] = jnp.dot(kv_ref[vrows, cols], p.astype(BF16), preferred_element_type=F32)
        return carry
    lax.fori_loop(0, 2 * heads, diag, 0)

    branch = branch_ref[0, 0]

    def full(source, c, block):
        limit = jnp.where(c == 0, n * PCH, branch) - block * PCH
        def body(h, carry):
            rows = pl.ds(pl.multiple_of(h * HEAD_DIM, HEAD_DIM), HEAD_DIM)
            vrows = pl.ds(pl.multiple_of(feats + h * HEAD_DIM, HEAD_DIM), HEAD_DIM)
            cols = pl.ds(pl.multiple_of(c * PCH, PCH), PCH)
            s = scores(source[rows, :], load_q(h, c))
            key = lax.broadcasted_iota(jnp.int32, (PCH, 1), 0)
            s = s + jnp.where(key < limit, 0.0, big_negative)
            m_old = m_sc[h, :, cols]
            m = jnp.maximum(m_old, jnp.max(s, axis=0, keepdims=True))
            p = jnp.exp(s - m)
            alpha = jnp.exp(m_old - m)
            m_sc[h, :, cols] = m
            l_sc[h, :, cols] = l_sc[h, :, cols] * alpha + jnp.sum(p, axis=0, keepdims=True)
            acc[rows, cols] = acc[rows, cols] * alpha + jnp.dot(source[vrows, :], p.astype(BF16), preferred_element_type=F32)
            return carry
        lax.fori_loop(0, heads, body, 0)

    full(own, 1, z)

    def step_body(step, carry):
        @pl.when(z >= step)
        def _():
            hop(own, z - step, step - 1, z, up_send, up_recv).wait_recv()
            @pl.when(has_up & (step < n - 1))
            def _(): hop(kv_all.at[z - step], z - step, step, z + 1, up_send, up_recv).start()
        @pl.when(z + step < n)
        def _():
            hop(own, z + step, step - 1, z, down_send, down_recv).wait_recv()
            @pl.when(has_down & (step < n - 1))
            def _(): hop(kv_all.at[z + step], z + step, step, z - 1, down_send, down_recv).start()
        @pl.when(z >= step)
        def _():
            def both(c, carry):
                full(kv_all.at[z - step], c, z - step)
                return carry
            lax.fori_loop(0, 2, both, 0)
        @pl.when(z + step < n)
        def _(): full(kv_all.at[z + step], 1, z + step)
        return carry
    lax.fori_loop(1, n, step_body, 0)

    for h in range(heads):
        rows = slice(h * HEAD_DIM, (h + 1) * HEAD_DIM)
        total = l_sc[h]
        out = acc[rows, :] / total
        of_ref[rows, :] = out
        o_ref[rows, :] = out.astype(BF16)
        lse_ref[h:h + 1, :] = m_sc[h] + jnp.log(total)

    for step in range(n - 1):
        @pl.when(has_up & (z >= step))
        def _(): hop(own, z, step, z + 1, up_send, up_recv).wait_send()
        @pl.when(has_down & (z + step < n))
        def _(): hop(own, z, step, z - 1, down_send, down_recv).wait_send()

def attend_forward(n, q, kv, branch):
    feats, rows = q.shape
    heads = feats // HEAD_DIM
    vm = pl.BlockSpec(memory_space=pltpu.VMEM)
    return pl.pallas_call(
        functools.partial(forward_kernel, n, heads),
        out_shape=(jax.ShapeDtypeStruct((feats, rows), BF16), jax.ShapeDtypeStruct((feats, rows), F32), jax.ShapeDtypeStruct((heads, rows), F32), jax.ShapeDtypeStruct((n, 2 * feats, PCH), BF16)),
        in_specs=[vm, vm, pl.BlockSpec(memory_space=pltpu.SMEM)],
        out_specs=(vm, vm, vm, vm),
        scratch_shapes=[
            pltpu.VMEM((heads, 1, rows), F32),
            pltpu.VMEM((heads, 1, rows), F32),
            pltpu.VMEM((feats, rows), F32),
            pltpu.SemaphoreType.DMA((n - 1,)), pltpu.SemaphoreType.DMA((n - 1,)),
            pltpu.SemaphoreType.DMA((n - 1,)), pltpu.SemaphoreType.DMA((n - 1,)),
        ],
        compiler_params=pltpu.CompilerParams(collective_id=1, has_side_effects=True, vmem_limit_bytes=40 * 2**20),
        name="attend_forward",
    )(q, kv, branch)


def backward_kernel(n, heads, q_ref, kv_ref, all_ref, branch_ref, do_ref, of_ref, lse_ref, dq_ref, dkv_ref, dq_acc, own_acc, far_acc, lse_sc, dot_sc, up_out, up_in, down_out, down_in, up_send, up_recv, down_send, down_recv):
    z = lax.axis_index("seq")
    feats = heads * HEAD_DIM
    barrier = pltpu.get_barrier_semaphore()
    has_up, has_down = z < n - 1, z > 0

    def meet(to):
        pl.semaphore_signal(barrier, inc=1, device_id={"seq": to}, device_id_type=pl.DeviceIdType.MESH)

    @pl.when(has_up)
    def _(): meet(z + 1)
    @pl.when(has_down)
    def _(): meet(z - 1)
    pl.semaphore_wait(barrier, has_up.astype(jnp.int32) + has_down.astype(jnp.int32))

    def hop(out, inn, d, to, send, recv):
        return pltpu.make_async_remote_copy(src_ref=out.at[d], dst_ref=inn.at[d], send_sem=send.at[d], recv_sem=recv.at[d], device_id={"seq": to}, device_id_type=pl.DeviceIdType.MESH)

    dq_acc[...] = jnp.zeros_like(dq_acc)
    for h in range(heads):
        rows = slice(h * HEAD_DIM, (h + 1) * HEAD_DIM)
        lse_sc[h] = lse_ref[h:h + 1, :]
        dot_sc[h] = jnp.sum(do_ref[rows, :].astype(F32) * of_ref[rows, :], axis=0, keepdims=True)

    nt = (((1,), (1,)), ((), ()))
    tn = (((0,), (0,)), ((), ()))

    def tile(h, cols, k, v, mask):
        rows = pl.ds(pl.multiple_of(h * HEAD_DIM, HEAD_DIM), HEAD_DIM)
        q, do = q_ref[rows, cols], do_ref[rows, cols]
        s = mask(lax.dot_general(k, q, tn, preferred_element_type=F32))
        p = jnp.exp(s - lse_sc[h, :, cols])
        dp = lax.dot_general(v, do, tn, preferred_element_type=F32)
        ds = (p * (dp - dot_sc[h, :, cols])).astype(BF16)
        p = p.astype(BF16)
        dv = lax.dot_general(do, p, nt, preferred_element_type=F32)
        dk = lax.dot_general(q, ds, nt, preferred_element_type=F32)
        dq_acc[rows, cols] += jnp.dot(k, ds, preferred_element_type=F32)
        return dk, dv

    def head_rows(h):
        return (pl.ds(pl.multiple_of(h * HEAD_DIM, HEAD_DIM), HEAD_DIM),
                pl.ds(pl.multiple_of(feats + h * HEAD_DIM, HEAD_DIM), HEAD_DIM))

    def columns(c):
        return pl.ds(pl.multiple_of(c * PCH, PCH), PCH)

    branch = branch_ref[0, 0]

    def full(source, c, block, total):
        limit = jnp.where(c == 0, n * PCH, branch) - block * PCH
        def mask(s):
            key = lax.broadcasted_iota(jnp.int32, (PCH, 1), 0)
            return s + jnp.where(key < limit, 0.0, big_negative)
        def body(h, carry):
            rows, vrows = head_rows(h)
            dk, dv = tile(h, columns(c), source[rows, :], source[vrows, :], mask)
            total[rows, :] += dk
            total[vrows, :] += dv
            return carry
        lax.fori_loop(0, heads, body, 0)

    def diag(i, carry):
        c, h = i // heads, i % heads
        rows, vrows = head_rows(h)
        cols = columns(c)
        def mask(s):
            key = lax.broadcasted_iota(jnp.int32, s.shape, 0)
            query = lax.broadcasted_iota(jnp.int32, s.shape, 1)
            return jnp.where(key <= query, s, big_negative)
        dk, dv = tile(h, cols, kv_ref[rows, cols], kv_ref[vrows, cols], mask)
        own_acc[rows, cols] = dk
        own_acc[vrows, cols] = dv
        return carry

    own_step = jnp.where(has_up & has_down, 0, n - 1)

    def step_body(step, carry):
        d = n - 1 - step

        @pl.when(step == own_step)
        def _():
            lax.fori_loop(0, 2 * heads, diag, 0)
            full(kv_ref.at[:, 0:PCH], 1, z, own_acc.at[:, 0:PCH])

        @pl.when((d >= 1) & (z + d < n))
        def _():
            far_acc[...] = jnp.zeros_like(far_acc)
            full(all_ref.at[z + d], 1, z + d, far_acc)
            @pl.when(has_down & (d < n - 1))
            def _():
                hop(up_out, up_in, d, z, up_send, up_recv).wait_recv()
                far_acc[...] += up_in[d].astype(F32)
            up_out[d - 1] = far_acc[...].astype(BF16)
            hop(up_out, up_in, d - 1, z + 1, up_send, up_recv).start()

        @pl.when((d >= 1) & (z >= d))
        def _():
            far_acc[...] = jnp.zeros_like(far_acc)
            def both(c, carry):
                full(all_ref.at[z - d], c, z - d, far_acc)
                return carry
            lax.fori_loop(0, 2, both, 0)
            @pl.when(has_up & (d < n - 1))
            def _():
                hop(down_out, down_in, d, z, down_send, down_recv).wait_recv()
                far_acc[...] += down_in[d].astype(F32)
            down_out[d - 1] = far_acc[...].astype(BF16)
            hop(down_out, down_in, d - 1, z - 1, down_send, down_recv).start()
        return carry
    lax.fori_loop(0, n, step_body, 0)

    dq_ref[...] = (dq_acc[...] * (1.0 / math.sqrt(HEAD_DIM))).astype(BF16)
    dkv_ref[:, PCH:] = own_acc[:, PCH:].astype(BF16)

    @pl.when(has_down)
    def _():
        hop(up_out, up_in, 0, z, up_send, up_recv).wait_recv()
        own_acc[:, 0:PCH] += up_in[0].astype(F32)
    @pl.when(has_up)
    def _():
        hop(down_out, down_in, 0, z, down_send, down_recv).wait_recv()
        own_acc[:, 0:PCH] += down_in[0].astype(F32)
    dkv_ref[:, 0:PCH] = own_acc[:, 0:PCH].astype(BF16)
    for d in range(1, n):
        @pl.when(z + d < n)
        def _(): hop(up_out, up_in, d - 1, z + 1, up_send, up_recv).wait_send()
        @pl.when(z >= d)
        def _(): hop(down_out, down_in, d - 1, z - 1, down_send, down_recv).wait_send()

def attend_backward(n, q, kv, kv_all, branch, do, of, lse):
    feats, rows = q.shape
    heads = feats // HEAD_DIM
    vm = pl.BlockSpec(memory_space=pltpu.VMEM)
    slots = pltpu.VMEM((n - 1, 2 * feats, PCH), BF16)
    sems = pltpu.SemaphoreType.DMA((n - 1,))
    return pl.pallas_call(
        functools.partial(backward_kernel, n, heads),
        out_shape=(jax.ShapeDtypeStruct((feats, rows), BF16), jax.ShapeDtypeStruct((2 * feats, rows), BF16)),
        in_specs=[vm, vm, vm, pl.BlockSpec(memory_space=pltpu.SMEM), vm, vm, vm],
        out_specs=(vm, vm),
        scratch_shapes=[
            pltpu.VMEM((feats, rows), F32),
            pltpu.VMEM((2 * feats, rows), F32),
            pltpu.VMEM((2 * feats, PCH), F32),
            pltpu.VMEM((heads, 1, rows), F32),
            pltpu.VMEM((heads, 1, rows), F32),
            slots, slots, slots, slots, sems, sems, sems, sems,
        ],
        compiler_params=pltpu.CompilerParams(collective_id=2, has_side_effects=True, vmem_limit_bytes=48 * 2**20),
        name="attend_backward",
    )(q, kv, kv_all, branch, do, of, lse)


def gelu_tanh(inner):
    return jax.nn.gelu(inner, approximate=True)


def swap(value, axis, bit):
    size = lax.axis_size(axis)
    return lax.ppermute(value, axis, [(i, i ^ bit) for i in range(size)])


def bits_of(axis):
    size = lax.axis_size(axis)
    return [1 << k for k in range(size.bit_length() - 1)]


def halve(value, axis, bit):
    mine = (lax.axis_index(axis) // bit) % 2
    kept = lax.dynamic_index_in_dim(value, mine, 1, keepdims=False)
    sent = lax.dynamic_index_in_dim(value, 1 - mine, 1, keepdims=False)
    return kept + swap(sent.astype(BF16), axis, bit).astype(F32)


def scatter_sum(value, steps):
    axes = ("dp", "seq")
    bits = [(axis, bit) for axis in axes for bit in reversed(bits_of(axis))]
    bits = [b for b in bits if b in steps]
    rows, columns = value.shape
    left = list(bits)
    for step in steps:
        place = left.index(step)
        pre, post = 1 << place, 1 << (len(left) - place - 1)
        block = rows >> len(left)
        rows //= 2
        value = halve(value.reshape(pre, 2, post * block, columns), *step)
        left.remove(step)
        value = value.reshape(rows, columns)
    return value


def total_over(value, axes):
    for axis in axes:
        for bit in bits_of(axis):
            value = value + swap(value, axis, bit)
    return value


def tensor_scatter(part):
    far = swap(part(3).astype(BF16), "tensor", 1).astype(F32)
    across = swap((part(2) + far).astype(BF16), "tensor", 2).astype(F32)
    near = swap(part(1).astype(BF16), "tensor", 1).astype(F32)
    return part(0) + near + across


def tensor_gather(own):
    across = swap(own, "tensor", 2)
    near = swap(own, "tensor", 1)
    far = swap(across, "tensor", 1)
    return jnp.concatenate([own, near, across, far], axis=0)


def shards(
    tokens,
    branch,
    w_attn,
    w_proj,
    w_expand,
    w_contract,
    attn_bias,
    branch_bias,
    expand_bias,
    norm_gains,
    norm_shifts,
    cotangent,
):
    seq_count = lax.axis_size("seq")
    seq_index = lax.axis_index("seq")
    tensor_count = lax.axis_size("tensor")
    tensor_index = lax.axis_index("tensor")
    width = tokens.shape[3]
    row_count = tokens.shape[2]
    share = row_count // tensor_count
    local_width = w_attn.shape[2]
    score_scale = 1.0 / math.sqrt(HEAD_DIM)
    layer_scale = 1.0 / math.sqrt(LAYERS)

    def slot(whole, k, axis=0):
        start = jnp.bitwise_xor(tensor_index, k) * share
        return lax.dynamic_slice_in_dim(whole, start, share, axis)

    def relative(whole, axis=0):
        return jnp.concatenate([slot(whole, k, axis) for k in range(tensor_count)], axis=axis)

    def rows_at(whole, k):
        return whole[k * share : (k + 1) * share]

    def columns_at(whole, k):
        return whole[:, k * share : (k + 1) * share]

    token_rows = tokens.reshape(row_count, width)
    cotangent_rows = cotangent.reshape(row_count, width)
    flat_rows = token_rows.astype(F32)
    normed_one = (
        layer_norm_parts(flat_rows)[0] * norm_gains[0] + norm_shifts[0]
    ).astype(BF16)
    projected = jnp.einsum("cde,rd->cer", w_attn, normed_one, preferred_element_type=F32)
    bias_rows = jnp.stack([attn_bias[0], jnp.zeros_like(attn_bias[0]), attn_bias[1]])
    projected = (projected + bias_rows[:, :, None]).astype(BF16)
    queries = projected[0] * jnp.asarray(score_scale, BF16)
    own_kv = projected[1:].reshape(2 * local_width, row_count)

    grad_mlp = (relative(cotangent_rows).astype(F32) * layer_scale).astype(BF16)
    grad_activated = jnp.einsum("rd,fd->rf", grad_mlp, w_contract, preferred_element_type=F32)

    attended, attended_wide, logsum, all_kv = attend_forward(seq_count, queries, own_kv, branch)
    attended = relative(attended, 1)
    attn_summed = tensor_scatter(
        lambda k: jnp.einsum(
            "er,ed->rd", columns_at(attended, k), w_proj, preferred_element_type=F32
        )
    )
    own_tokens = slot(token_rows, 0).astype(F32)
    own_cotangent = slot(cotangent_rows, 0).astype(F32)
    hidden = own_tokens + layer_scale * (attn_summed + branch_bias[0])
    xhat_two, inverse_two = layer_norm_parts(hidden)
    own_normed_two = (xhat_two * norm_gains[1] + norm_shifts[1]).astype(BF16)
    normed_two = tensor_gather(own_normed_two)
    preact = jnp.dot(normed_two, w_expand, preferred_element_type=F32) + expand_bias
    gelu_value, gelu_back = jax.vjp(gelu_tanh, preact)
    activated = gelu_value.astype(BF16)
    grad_preact = gelu_back(grad_activated)[0].astype(BF16)
    grad_mixed = tensor_scatter(
        lambda k: jnp.einsum(
            "rf,df->rd", rows_at(grad_preact, k), w_expand, preferred_element_type=F32
        )
    )
    grad_hidden = own_cotangent + layer_norm_back(
        grad_mixed, norm_gains[1], xhat_two, inverse_two
    )
    own_grad_att = (grad_hidden * layer_scale).astype(BF16)
    grad_att = tensor_gather(own_grad_att)
    grad_attended = jnp.einsum("rd,ed->er", grad_att, w_proj, preferred_element_type=F32).astype(
        BF16
    )
    grad_attended = relative(grad_attended, 1)

    mlp_summed = tensor_scatter(
        lambda k: jnp.dot(rows_at(activated, k), w_contract, preferred_element_type=F32)
    )
    layer_out = (hidden + layer_scale * (mlp_summed + branch_bias[1])).astype(BF16)

    bits = [("dp", b) for b in bits_of("dp")]
    seq_bits = [("seq", b) for b in bits_of("seq")]
    grad_contract = jnp.einsum("rf,rd->df", activated, grad_mlp, preferred_element_type=F32)
    grad_contract = scatter_sum(grad_contract, bits + seq_bits).T
    grad_expand = jnp.einsum("rd,rf->df", normed_two, grad_preact, preferred_element_type=F32)
    grad_expand = scatter_sum(grad_expand, seq_bits + bits)
    grad_proj = jnp.einsum("er,rd->de", attended, grad_att, preferred_element_type=F32)
    grad_proj = scatter_sum(grad_proj, seq_bits + bits).T

    grad_queries, grad_kv = attend_backward(
        seq_count, queries, own_kv, all_kv, branch, grad_attended, attended_wide, logsum
    )
    grad_values = grad_kv[local_width:]
    stacked = jnp.concatenate([grad_queries, grad_kv], axis=0)
    stacked_slots = relative(stacked, 1).reshape(3, local_width, row_count)
    grad_normed = tensor_scatter(
        lambda k: jnp.einsum(
            "cer,cde->rd",
            stacked_slots[:, :, k * share : (k + 1) * share],
            w_attn,
            preferred_element_type=F32,
        )
    )
    grad_attn = jnp.einsum("rd,er->de", normed_one, stacked, preferred_element_type=F32)
    grad_attn = scatter_sum(grad_attn, bits + seq_bits)
    grad_attn = jnp.transpose(grad_attn.reshape(-1, 3, local_width), (1, 0, 2))
    xhat_one, inverse_one = layer_norm_parts(own_tokens)
    grad_tokens = (
        grad_hidden + layer_norm_back(grad_normed, norm_gains[0], xhat_one, inverse_one)
    ).astype(BF16)

    everywhere = ("dp", "seq", "tensor")
    early = total_over(
        jnp.stack(
            [
                jnp.sum(own_grad_att.astype(F32), axis=0),
                jnp.sum(rows_at(grad_mlp, 0).astype(F32), axis=0),
                jnp.sum(grad_mixed * xhat_two, axis=0),
                jnp.sum(grad_mixed, axis=0),
            ]
        ),
        everywhere,
    )
    late = total_over(
        jnp.stack([jnp.sum(grad_normed * xhat_one, axis=0), jnp.sum(grad_normed, axis=0)]),
        everywhere,
    )
    expand_terms = total_over(jnp.sum(grad_preact.astype(F32), axis=0), ("dp", "seq"))
    bias_terms = total_over(
        jnp.stack(
            [
                jnp.sum(grad_queries.astype(F32), axis=1),
                jnp.sum(grad_values.astype(F32), axis=1),
            ]
        ),
        ("dp", "seq"),
    )
    out_shape = (1, 1, share, width)
    return (
        layer_out.reshape(out_shape),
        grad_tokens.reshape(out_shape),
        grad_attn,
        grad_proj,
        grad_expand,
        grad_contract,
        bias_terms,
        early[:2],
        expand_terms,
        jnp.stack([late[0], early[2]]),
        jnp.stack([late[1], early[3]]),
    )


def solution(mesh):
    placed = (
        P("dp", "seq", None, None),
        P("dp", "seq"),
        P(None, None, "tensor"),
        P("tensor", None),
        P(None, "tensor"),
        P("tensor", None),
        P(None, "tensor"),
        P(),
        P("tensor"),
        P(),
        P(),
        P("dp", "seq", None, None),
    )
    return jax.shard_map(
        shards,
        mesh=mesh,
        in_specs=placed,
        out_specs=(
            P("dp", "seq", "tensor", None),
            P("dp", "seq", "tensor", None),
            P(None, ("dp", "seq"), "tensor"),
            P("tensor", ("dp", "seq")),
            P(("dp", "seq"), "tensor"),
            P("tensor", ("dp", "seq")),
            P(None, "tensor"),
            P(),
            P("tensor"),
            P(),
            P(),
        ),
        check_vma=False,
    )
```

```python
import functools
import math

import jax
import jax.numpy as jnp
from jax import lax
from jax.experimental import pallas as pl
from jax.experimental.pallas import tpu as pltpu
from jax.sharding import PartitionSpec as P

HEAD_DIM = 64
LAYERS = 12
PCH = 512
CLEN = 512
F32 = jnp.float32
BF16 = jnp.bfloat16


norm_eps = 1e-05
big_negative = -1000000000.0


def layer_norm_parts(value):
    centre = jnp.mean(value, axis=-1, keepdims=True)
    centred = value - centre
    spread = jnp.mean(centred * centred, axis=-1, keepdims=True)
    inverse = lax.rsqrt(spread + norm_eps)
    return centred * inverse, inverse


def layer_norm_back(grad, gain, xhat, inverse):
    e = grad * gain
    return inverse * (
        e
        - jnp.mean(e, axis=-1, keepdims=True)
        - xhat * jnp.mean(e * xhat, axis=-1, keepdims=True)
    )


def forward_kernel(n, heads, q_ref, kv_ref, branch_ref, o_ref, of_ref, lse_ref, kv_all, m_sc, l_sc, acc, up_send, up_recv, down_send, down_recv):
    z = lax.axis_index("seq")
    feats = heads * HEAD_DIM
    barrier = pltpu.get_barrier_semaphore()
    has_up, has_down = z < n - 1, z > 0

    def meet(to):
        pl.semaphore_signal(barrier, inc=1, device_id={"seq": to}, device_id_type=pl.DeviceIdType.MESH)

    @pl.when(has_up)
    def _(): meet(z + 1)
    @pl.when(has_down)
    def _(): meet(z - 1)
    pl.semaphore_wait(barrier, has_up.astype(jnp.int32) + has_down.astype(jnp.int32))

    own = kv_ref.at[:, 0:PCH]

    def hop(src, block, step, to, send, recv):
        return pltpu.make_async_remote_copy(src_ref=src, dst_ref=kv_all.at[block], send_sem=send.at[step], recv_sem=recv.at[step], device_id={"seq": to}, device_id_type=pl.DeviceIdType.MESH)

    @pl.when(has_up)
    def _(): hop(own, z, 0, z + 1, up_send, up_recv).start()
    @pl.when(has_down)
    def _(): hop(own, z, 0, z - 1, down_send, down_recv).start()

    def load_q(h, c):
        return q_ref[pl.ds(pl.multiple_of(h * HEAD_DIM, HEAD_DIM), HEAD_DIM), pl.ds(pl.multiple_of(c * PCH, PCH), PCH)]

    def scores(k, q):
        return lax.dot_general(k, q, (((0,), (0,)), ((), ())), preferred_element_type=F32)

    def diag(i, carry):
        c, h = i // heads, i % heads
        rows = pl.ds(pl.multiple_of(h * HEAD_DIM, HEAD_DIM), HEAD_DIM)
        vrows = pl.ds(pl.multiple_of(feats + h * HEAD_DIM, HEAD_DIM), HEAD_DIM)
        cols = pl.ds(pl.multiple_of(c * PCH, PCH), PCH)
        s = scores(kv_ref[rows, cols], load_q(h, c))
        key = lax.broadcasted_iota(jnp.int32, s.shape, 0)
        query = lax.broadcasted_iota(jnp.int32, s.shape, 1)
        s = jnp.where(key <= query, s, big_negative)
        m = jnp.max(s, axis=0, keepdims=True)
        p = jnp.exp(s - m)
        m_sc[h, :, cols] = m
        l_sc[h, :, cols] = jnp.sum(p, axis=0, keepdims=True)
        acc[rows, cols] = jnp.dot(kv_ref[vrows, cols], p.astype(BF16), preferred_element_type=F32)
        return carry
    lax.fori_loop(0, 2 * heads, diag, 0)

    branch = branch_ref[0, 0]

    def full(source, c, block):
        limit = jnp.where(c == 0, n * PCH, branch) - block * PCH
        def body(h, carry):
            rows = pl.ds(pl.multiple_of(h * HEAD_DIM, HEAD_DIM), HEAD_DIM)
            vrows = pl.ds(pl.multiple_of(feats + h * HEAD_DIM, HEAD_DIM), HEAD_DIM)
            cols = pl.ds(pl.multiple_of(c * PCH, PCH), PCH)
            s = scores(source[rows, :], load_q(h, c))
            key = lax.broadcasted_iota(jnp.int32, (PCH, 1), 0)
            s = s + jnp.where(key < limit, 0.0, big_negative)
            m_old = m_sc[h, :, cols]
            m = jnp.maximum(m_old, jnp.max(s, axis=0, keepdims=True))
            p = jnp.exp(s - m)
            alpha = jnp.exp(m_old - m)
            m_sc[h, :, cols] = m
            l_sc[h, :, cols] = l_sc[h, :, cols] * alpha + jnp.sum(p, axis=0, keepdims=True)
            acc[rows, cols] = acc[rows, cols] * alpha + jnp.dot(source[vrows, :], p.astype(BF16), preferred_element_type=F32)
            return carry
        lax.fori_loop(0, heads, body, 0)

    full(own, 1, z)

    def step_body(step, carry):
        @pl.when(z >= step)
        def _():
            hop(own, z - step, step - 1, z, up_send, up_recv).wait_recv()
            @pl.when(has_up & (step < n - 1))
            def _(): hop(kv_all.at[z - step], z - step, step, z + 1, up_send, up_recv).start()
        @pl.when(z + step < n)
        def _():
            hop(own, z + step, step - 1, z, down_send, down_recv).wait_recv()
            @pl.when(has_down & (step < n - 1))
            def _(): hop(kv_all.at[z + step], z + step, step, z - 1, down_send, down_recv).start()
        @pl.when(z >= step)
        def _():
            def both(c, carry):
                full(kv_all.at[z - step], c, z - step)
                return carry
            lax.fori_loop(0, 2, both, 0)
        @pl.when(z + step < n)
        def _(): full(kv_all.at[z + step], 1, z + step)
        return carry
    lax.fori_loop(1, n, step_body, 0)

    for h in range(heads):
        rows = slice(h * HEAD_DIM, (h + 1) * HEAD_DIM)
        total = l_sc[h]
        out = acc[rows, :] / total
        of_ref[rows, :] = out
        o_ref[rows, :] = out.astype(BF16)
        lse_ref[h:h + 1, :] = m_sc[h] + jnp.log(total)

    for step in range(n - 1):
        @pl.when(has_up & (z >= step))
        def _(): hop(own, z, step, z + 1, up_send, up_recv).wait_send()
        @pl.when(has_down & (z + step < n))
        def _(): hop(own, z, step, z - 1, down_send, down_recv).wait_send()

def attend_forward(n, q, kv, branch):
    feats, rows = q.shape
    heads = feats // HEAD_DIM
    vm = pl.BlockSpec(memory_space=pltpu.VMEM)
    return pl.pallas_call(
        functools.partial(forward_kernel, n, heads),
        out_shape=(jax.ShapeDtypeStruct((feats, rows), BF16), jax.ShapeDtypeStruct((feats, rows), F32), jax.ShapeDtypeStruct((heads, rows), F32), jax.ShapeDtypeStruct((n, 2 * feats, PCH), BF16)),
        in_specs=[vm, vm, pl.BlockSpec(memory_space=pltpu.SMEM)],
        out_specs=(vm, vm, vm, vm),
        scratch_shapes=[
            pltpu.VMEM((heads, 1, rows), F32),
            pltpu.VMEM((heads, 1, rows), F32),
            pltpu.VMEM((feats, rows), F32),
            pltpu.SemaphoreType.DMA((n - 1,)), pltpu.SemaphoreType.DMA((n - 1,)),
            pltpu.SemaphoreType.DMA((n - 1,)), pltpu.SemaphoreType.DMA((n - 1,)),
        ],
        compiler_params=pltpu.CompilerParams(collective_id=1, has_side_effects=True, vmem_limit_bytes=40 * 2**20),
        cost_estimate=pl.CostEstimate(flops=4 * 10**10, bytes_accessed=10**7, transcendentals=0),
        name="attend_forward",
    )(q, kv, branch)


def backward_kernel(n, heads, q_ref, kv_ref, all_ref, branch_ref, do_ref, of_ref, lse_ref, dq_ref, dkv_ref, dq_acc, own_acc, far_acc, lse_sc, dot_sc, up_out, up_in, down_out, down_in, up_send, up_recv, down_send, down_recv):
    z = lax.axis_index("seq")
    feats = heads * HEAD_DIM
    barrier = pltpu.get_barrier_semaphore()
    has_up, has_down = z < n - 1, z > 0

    def meet(to):
        pl.semaphore_signal(barrier, inc=1, device_id={"seq": to}, device_id_type=pl.DeviceIdType.MESH)

    @pl.when(has_up)
    def _(): meet(z + 1)
    @pl.when(has_down)
    def _(): meet(z - 1)
    pl.semaphore_wait(barrier, has_up.astype(jnp.int32) + has_down.astype(jnp.int32))

    def hop(out, inn, d, to, send, recv):
        return pltpu.make_async_remote_copy(src_ref=out.at[d], dst_ref=inn.at[d], send_sem=send.at[d], recv_sem=recv.at[d], device_id={"seq": to}, device_id_type=pl.DeviceIdType.MESH)

    dq_acc[...] = jnp.zeros_like(dq_acc)
    for h in range(heads):
        rows = slice(h * HEAD_DIM, (h + 1) * HEAD_DIM)
        lse_sc[h] = lse_ref[h:h + 1, :]
        dot_sc[h] = jnp.sum(do_ref[rows, :].astype(F32) * of_ref[rows, :], axis=0, keepdims=True)

    nt = (((1,), (1,)), ((), ()))
    tn = (((0,), (0,)), ((), ()))

    def tile(h, cols, k, v, mask):
        rows = pl.ds(pl.multiple_of(h * HEAD_DIM, HEAD_DIM), HEAD_DIM)
        q, do = q_ref[rows, cols], do_ref[rows, cols]
        s = mask(lax.dot_general(k, q, tn, preferred_element_type=F32))
        p = jnp.exp(s - lse_sc[h, :, cols])
        dp = lax.dot_general(v, do, tn, preferred_element_type=F32)
        ds = (p * (dp - dot_sc[h, :, cols])).astype(BF16)
        p = p.astype(BF16)
        dv = lax.dot_general(do, p, nt, preferred_element_type=F32)
        dk = lax.dot_general(q, ds, nt, preferred_element_type=F32)
        dq_acc[rows, cols] += jnp.dot(k, ds, preferred_element_type=F32)
        return dk, dv

    def head_rows(h):
        return (pl.ds(pl.multiple_of(h * HEAD_DIM, HEAD_DIM), HEAD_DIM),
                pl.ds(pl.multiple_of(feats + h * HEAD_DIM, HEAD_DIM), HEAD_DIM))

    def columns(c):
        return pl.ds(pl.multiple_of(c * PCH, PCH), PCH)

    branch = branch_ref[0, 0]

    def full(source, c, block, total):
        limit = jnp.where(c == 0, n * PCH, branch) - block * PCH
        def mask(s):
            key = lax.broadcasted_iota(jnp.int32, (PCH, 1), 0)
            return s + jnp.where(key < limit, 0.0, big_negative)
        def body(h, carry):
            rows, vrows = head_rows(h)
            dk, dv = tile(h, columns(c), source[rows, :], source[vrows, :], mask)
            total[rows, :] += dk
            total[vrows, :] += dv
            return carry
        lax.fori_loop(0, heads, body, 0)

    def diag(i, carry):
        c, h = i // heads, i % heads
        rows, vrows = head_rows(h)
        cols = columns(c)
        def mask(s):
            key = lax.broadcasted_iota(jnp.int32, s.shape, 0)
            query = lax.broadcasted_iota(jnp.int32, s.shape, 1)
            return jnp.where(key <= query, s, big_negative)
        dk, dv = tile(h, cols, kv_ref[rows, cols], kv_ref[vrows, cols], mask)
        own_acc[rows, cols] = dk
        own_acc[vrows, cols] = dv
        return carry

    own_step = jnp.where(has_up & has_down, 0, n - 1)

    def step_body(step, carry):
        d = n - 1 - step

        @pl.when(step == own_step)
        def _():
            lax.fori_loop(0, 2 * heads, diag, 0)
            full(kv_ref.at[:, 0:PCH], 1, z, own_acc.at[:, 0:PCH])

        @pl.when((d >= 1) & (z + d < n))
        def _():
            far_acc[...] = jnp.zeros_like(far_acc)
            full(all_ref.at[z + d], 1, z + d, far_acc)
            @pl.when(has_down & (d < n - 1))
            def _():
                hop(up_out, up_in, d, z, up_send, up_recv).wait_recv()
                far_acc[...] += up_in[d].astype(F32)
            up_out[d - 1] = far_acc[...].astype(BF16)
            hop(up_out, up_in, d - 1, z + 1, up_send, up_recv).start()

        @pl.when((d >= 1) & (z >= d))
        def _():
            far_acc[...] = jnp.zeros_like(far_acc)
            def both(c, carry):
                full(all_ref.at[z - d], c, z - d, far_acc)
                return carry
            lax.fori_loop(0, 2, both, 0)
            @pl.when(has_up & (d < n - 1))
            def _():
                hop(down_out, down_in, d, z, down_send, down_recv).wait_recv()
                far_acc[...] += down_in[d].astype(F32)
            down_out[d - 1] = far_acc[...].astype(BF16)
            hop(down_out, down_in, d - 1, z - 1, down_send, down_recv).start()
        return carry
    lax.fori_loop(0, n, step_body, 0)

    dq_ref[...] = (dq_acc[...] * (1.0 / math.sqrt(HEAD_DIM))).astype(BF16)
    dkv_ref[:, PCH:] = own_acc[:, PCH:].astype(BF16)

    @pl.when(has_down)
    def _():
        hop(up_out, up_in, 0, z, up_send, up_recv).wait_recv()
        own_acc[:, 0:PCH] += up_in[0].astype(F32)
    @pl.when(has_up)
    def _():
        hop(down_out, down_in, 0, z, down_send, down_recv).wait_recv()
        own_acc[:, 0:PCH] += down_in[0].astype(F32)
    dkv_ref[:, 0:PCH] = own_acc[:, 0:PCH].astype(BF16)
    for d in range(1, n):
        @pl.when(z + d < n)
        def _(): hop(up_out, up_in, d - 1, z + 1, up_send, up_recv).wait_send()
        @pl.when(z >= d)
        def _(): hop(down_out, down_in, d - 1, z - 1, down_send, down_recv).wait_send()

def attend_backward(n, q, kv, kv_all, branch, do, of, lse):
    feats, rows = q.shape
    heads = feats // HEAD_DIM
    vm = pl.BlockSpec(memory_space=pltpu.VMEM)
    slots = pltpu.VMEM((n - 1, 2 * feats, PCH), BF16)
    sems = pltpu.SemaphoreType.DMA((n - 1,))
    return pl.pallas_call(
        functools.partial(backward_kernel, n, heads),
        out_shape=(jax.ShapeDtypeStruct((feats, rows), BF16), jax.ShapeDtypeStruct((2 * feats, rows), BF16)),
        in_specs=[vm, vm, vm, pl.BlockSpec(memory_space=pltpu.SMEM), vm, vm, vm],
        out_specs=(vm, vm),
        scratch_shapes=[
            pltpu.VMEM((feats, rows), F32),
            pltpu.VMEM((2 * feats, rows), F32),
            pltpu.VMEM((2 * feats, PCH), F32),
            pltpu.VMEM((heads, 1, rows), F32),
            pltpu.VMEM((heads, 1, rows), F32),
            slots, slots, slots, slots, sems, sems, sems, sems,
        ],
        compiler_params=pltpu.CompilerParams(collective_id=2, has_side_effects=True, vmem_limit_bytes=48 * 2**20),
        cost_estimate=pl.CostEstimate(flops=4 * 10**10, bytes_accessed=10**7, transcendentals=0),
        name="attend_backward",
    )(q, kv, kv_all, branch, do, of, lse)


def middle_kernel(
    layer_scale, o_ref, tok_ref, cot_ref, wp_ref, we_ref, wc_ref, bb_ref, eb_ref, gain_ref, shift_ref,
    hidden_ref, ghid_ref, near_ref, far_ref, gatt_ref, gproj_ref, gexp_ref, gcon_ref, sums_ref, esum_ref,
    ga_sc, mix_sc, n2, gm, act, gp, att, own_sc, xhat_sc, inv_sc, proj_sc,
    core_out, core_in, y_out, y_in, core_send, core_recv, y_send, y_recv, n2_send, n2_recv, att_send, att_recv,
):
    t = lax.axis_index("tensor")
    y, c = t // 2, t % 2
    sibling = y * 2 + (1 - c)
    partner = (1 - y) * 2 + c
    share = own_sc.shape[0]

    def block(k):
        if isinstance(k, int):
            return ((1 - y) if k >= 2 else y) * 2 + ((1 - c) if k % 2 else c)
        return jnp.where(k >= 2, 1 - y, y) * 2 + jnp.where(k % 2 == 1, 1 - c, c)

    def place(k):
        return pl.ds(pl.multiple_of(block(k) * share, share), share)

    barrier = pltpu.get_barrier_semaphore()
    for to in (sibling, partner):
        pl.semaphore_signal(barrier, inc=1, device_id={"tensor": to}, device_id_type=pl.DeviceIdType.MESH)
    pl.semaphore_wait(barrier, 2)

    def copy(src, dst, send, recv, to):
        return pltpu.make_async_remote_copy(
            src_ref=src, dst_ref=dst, send_sem=send, recv_sem=recv,
            device_id={"tensor": to}, device_id_type=pl.DeviceIdType.MESH,
        )

    def core_copy(i):
        return copy(core_out.at[i], core_in.at[i], core_send.at[i], core_recv.at[i], sibling)

    def y_copy(i):
        return copy(y_out.at[i], y_in.at[i], y_send.at[i], y_recv.at[i], partner)

    def gather(ref, send, recv):
        return (
            copy(ref.at[0], ref.at[2], send.at[0], recv.at[0], partner),
            copy(ref.at[0], ref.at[1], send.at[1], recv.at[1], sibling),
            copy(ref.at[2], ref.at[3], send.at[2], recv.at[2], sibling),
        )

    tn = (((0,), (0,)), ((), ()))
    nt = (((1,), (1,)), ((), ()))

    def project(k):
        return lax.dot_general(o_ref[:, place(k)], wp_ref[...], tn, preferred_element_type=F32)

    core_out[0] = project(3).astype(BF16)
    core_copy(0).start()
    own_sc[...] = project(2)
    core_out[1] = project(1).astype(BF16)
    core_copy(1).start()
    core_copy(0).wait_recv()
    y_out[0] = (own_sc[...] + core_in[0].astype(F32)).astype(BF16)
    y_copy(0).start()
    own_sc[...] = project(0)

    def before(k, carry):
        g = (cot_ref[place(k), :].astype(F32) * layer_scale).astype(BF16)
        gm[k] = g
        ga_sc[k] = lax.dot_general(g, wc_ref[...], nt, preferred_element_type=F32)
        return carry

    lax.fori_loop(0, 4, before, 0)
    core_copy(1).wait_recv()
    own_sc[...] += core_in[1].astype(F32)
    y_copy(0).wait_recv()

    hidden = tok_ref[place(0), :].astype(F32) + layer_scale * (
        own_sc[...] + y_in[0].astype(F32) + bb_ref[0:1, :]
    )
    hidden_ref[...] = hidden
    centred = hidden - jnp.mean(hidden, axis=-1, keepdims=True)
    inverse = lax.rsqrt(jnp.mean(centred * centred, axis=-1, keepdims=True) + norm_eps)
    xhat = centred * inverse
    n2[0] = (xhat * gain_ref[1:2, :] + shift_ref[1:2, :]).astype(BF16)
    across, near, on = gather(n2, n2_send, n2_recv)
    across.start()
    near.start()
    xhat_sc[...] = xhat
    inv_sc[...] = jnp.broadcast_to(inverse, inv_sc.shape)
    esum_ref[...] = jnp.zeros_like(esum_ref)

    def process(k, carry):
        @pl.when(k == 1)
        def _():
            near.wait_recv()

        @pl.when(k == 2)
        def _():
            across.wait_recv()
            on.start()

        @pl.when(k == 3)
        def _():
            on.wait_recv()

        v = jnp.dot(n2[k], we_ref[...], preferred_element_type=F32) + eb_ref[...]
        square = v * v
        th = jnp.tanh(math.sqrt(2.0 / math.pi) * (v + 0.044715 * (v * square)))
        cdf = 0.5 * (1.0 + th)
        act[k] = (v * cdf).astype(BF16)
        slope = cdf + 0.5 * v * (1.0 - th * th) * (
            math.sqrt(2.0 / math.pi) * (1.0 + 3 * 0.044715 * square)
        )
        g = (slope * ga_sc[k]).astype(BF16)
        gp[k] = g
        esum_ref[...] += jnp.sum(g.astype(F32), axis=0, keepdims=True)
        mix_sc[k] = lax.dot_general(g, we_ref[...], nt, preferred_element_type=F32)
        return carry

    lax.fori_loop(0, 4, process, 0)
    core_out[2] = mix_sc[3].astype(BF16)
    core_copy(2).start()
    core_out[3] = mix_sc[1].astype(BF16)
    core_copy(3).start()
    core_copy(2).wait_recv()
    y_out[1] = (mix_sc[2] + core_in[2].astype(F32)).astype(BF16)
    y_copy(1).start()

    rows = 4 * share
    width = gm.shape[2]
    gcon_ref[...] = lax.dot_general(
        gm[...].reshape(rows, width), act[...].reshape(rows, -1), tn, preferred_element_type=F32
    )
    gexp_ref[...] = lax.dot_general(
        n2[...].reshape(rows, width), gp[...].reshape(rows, -1), tn, preferred_element_type=F32
    )

    def contract(k):
        return jnp.dot(act[k], wc_ref[...], preferred_element_type=F32)

    core_out[4] = contract(3).astype(BF16)
    core_copy(4).start()
    core_out[5] = contract(1).astype(BF16)
    core_copy(5).start()
    near_ref[...] = contract(0)
    last = contract(2)
    core_copy(4).wait_recv()
    far_ref[...] = (last + core_in[4].astype(F32)).astype(BF16)
    core_copy(5).wait_recv()
    near_ref[...] += core_in[5].astype(F32)

    core_copy(3).wait_recv()
    mixed = mix_sc[0] + core_in[3].astype(F32)
    y_copy(1).wait_recv()
    mixed = mixed + y_in[1].astype(F32)
    e = mixed * gain_ref[1:2, :]
    xhat = xhat_sc[...]
    grad_hidden = cot_ref[place(0), :].astype(F32) + inv_sc[:, 0:1] * (
        e - jnp.mean(e, axis=-1, keepdims=True) - xhat * jnp.mean(e * xhat, axis=-1, keepdims=True)
    )
    g = (grad_hidden * layer_scale).astype(BF16)
    att[0] = g
    across_b, near_b, on_b = gather(att, att_send, att_recv)
    across_b.start()
    near_b.start()
    ghid_ref[...] = grad_hidden
    sums_ref[0:1, :] = jnp.sum(g.astype(F32), axis=0, keepdims=True)
    sums_ref[1:2, :] = jnp.sum(gm[0].astype(F32), axis=0, keepdims=True)
    sums_ref[2:3, :] = jnp.sum(mixed * xhat, axis=0, keepdims=True)
    sums_ref[3:4, :] = jnp.sum(mixed, axis=0, keepdims=True)

    proj_sc[...] = jnp.zeros_like(proj_sc)

    def after(k, carry):
        @pl.when(k == 1)
        def _():
            near_b.wait_recv()

        @pl.when(k == 2)
        def _():
            across_b.wait_recv()
            on_b.start()

        @pl.when(k == 3)
        def _():
            on_b.wait_recv()

        gatt_ref[:, place(k)] = lax.dot_general(
            wp_ref[...], att[k], nt, preferred_element_type=F32
        ).astype(BF16)
        proj_sc[...] += jnp.dot(o_ref[:, place(k)], att[k], preferred_element_type=F32)
        return carry

    lax.fori_loop(0, 4, after, 0)
    gproj_ref[...] = proj_sc[...].T
    for i in range(6):
        core_copy(i).wait_send()
    for i in range(2):
        y_copy(i).wait_send()
    for one in (across, near, on, across_b, near_b, on_b):
        one.wait_send()


def middle(
    layer_scale, attended, token_rows, cotangent_rows, w_proj, w_expand, w_contract,
    branch_bias, expand_bias, norm_gains, norm_shifts,
):
    rows, width = token_rows.shape
    feats, hidden_units = w_proj.shape[0], w_expand.shape[1]
    share = rows // 4
    vm = pl.BlockSpec(memory_space=pltpu.VMEM)
    shape = jax.ShapeDtypeStruct
    slots = lambda columns, kind: pltpu.VMEM((4, share, columns), kind)
    sems = lambda count: pltpu.SemaphoreType.DMA((count,))
    return pl.pallas_call(
        functools.partial(middle_kernel, layer_scale),
        out_shape=(
            shape((share, width), F32),
            shape((share, width), F32),
            shape((share, width), F32),
            shape((share, width), BF16),
            shape((feats, rows), BF16),
            shape((width, feats), F32),
            shape((width, hidden_units), F32),
            shape((width, hidden_units), F32),
            shape((4, width), F32),
            shape((1, hidden_units), F32),
        ),
        in_specs=[vm] * 10,
        out_specs=(vm,) * 10,
        scratch_shapes=[
            slots(hidden_units, F32),
            slots(width, F32),
            slots(width, BF16),
            slots(width, BF16),
            slots(hidden_units, BF16),
            slots(hidden_units, BF16),
            slots(width, BF16),
            pltpu.VMEM((share, width), F32),
            pltpu.VMEM((share, width), F32),
            pltpu.VMEM((share, 128), F32),
            pltpu.VMEM((feats, width), F32),
            pltpu.VMEM((6, share, width), BF16),
            pltpu.VMEM((6, share, width), BF16),
            pltpu.VMEM((2, share, width), BF16),
            pltpu.VMEM((2, share, width), BF16),
            sems(6), sems(6), sems(2), sems(2), sems(3), sems(3), sems(3), sems(3),
        ],
        compiler_params=pltpu.CompilerParams(
            collective_id=3, has_side_effects=True, vmem_limit_bytes=56 * 2**20
        ),
        cost_estimate=pl.CostEstimate(flops=5 * 10**10, bytes_accessed=2 * 10**7, transcendentals=0),
        name="middle",
    )(
        attended, token_rows, cotangent_rows, w_proj, w_expand, w_contract,
        branch_bias, expand_bias, norm_gains, norm_shifts,
    )


def swap(value, axis, bit):
    size = lax.axis_size(axis)
    return lax.ppermute(value, axis, [(i, i ^ bit) for i in range(size)])


def bits_of(axis):
    size = lax.axis_size(axis)
    return [1 << k for k in range(size.bit_length() - 1)]


def halve(value, axis, bit):
    mine = (lax.axis_index(axis) // bit) % 2
    kept = lax.dynamic_index_in_dim(value, mine, 1, keepdims=False)
    sent = lax.dynamic_index_in_dim(value, 1 - mine, 1, keepdims=False)
    return kept + swap(sent.astype(BF16), axis, bit).astype(F32)


def scatter_sum(value, steps):
    axes = ("dp", "seq")
    bits = [(axis, bit) for axis in axes for bit in reversed(bits_of(axis))]
    bits = [b for b in bits if b in steps]
    rows, columns = value.shape
    left = list(bits)
    for step in steps:
        place = left.index(step)
        pre, post = 1 << place, 1 << (len(left) - place - 1)
        block = rows >> len(left)
        rows //= 2
        value = halve(value.reshape(pre, 2, post * block, columns), *step)
        left.remove(step)
        value = value.reshape(rows, columns)
    return value


def total_over(value, axes):
    for axis in axes:
        for bit in bits_of(axis):
            value = value + swap(value, axis, bit)
    return value


def tensor_scatter(part):
    far = swap(part(3).astype(BF16), "tensor", 1).astype(F32)
    across = swap((part(2) + far).astype(BF16), "tensor", 2).astype(F32)
    near = swap(part(1).astype(BF16), "tensor", 1).astype(F32)
    return part(0) + near + across


def shards(
    tokens,
    branch,
    w_attn,
    w_proj,
    w_expand,
    w_contract,
    attn_bias,
    branch_bias,
    expand_bias,
    norm_gains,
    norm_shifts,
    cotangent,
):
    seq_count = lax.axis_size("seq")
    seq_index = lax.axis_index("seq")
    tensor_count = lax.axis_size("tensor")
    tensor_index = lax.axis_index("tensor")
    width = tokens.shape[3]
    row_count = tokens.shape[2]
    share = row_count // tensor_count
    local_width = w_attn.shape[2]
    score_scale = 1.0 / math.sqrt(HEAD_DIM)
    layer_scale = 1.0 / math.sqrt(LAYERS)

    def slot(whole, k, axis=0):
        start = jnp.bitwise_xor(tensor_index, k) * share
        return lax.dynamic_slice_in_dim(whole, start, share, axis)

    def relative(whole, axis=0):
        return jnp.concatenate([slot(whole, k, axis) for k in range(tensor_count)], axis=axis)

    token_rows = tokens.reshape(row_count, width)
    cotangent_rows = cotangent.reshape(row_count, width)
    flat_rows = token_rows.astype(F32)
    normed_one = (
        layer_norm_parts(flat_rows)[0] * norm_gains[0] + norm_shifts[0]
    ).astype(BF16)
    projected = jnp.einsum("cde,rd->cer", w_attn, normed_one, preferred_element_type=F32)
    bias_rows = jnp.stack([attn_bias[0], jnp.zeros_like(attn_bias[0]), attn_bias[1]])
    projected = (projected + bias_rows[:, :, None]).astype(BF16)
    queries = projected[0] * jnp.asarray(score_scale, BF16)
    own_kv = projected[1:].reshape(2 * local_width, row_count)

    attended, attended_wide, logsum, all_kv = attend_forward(seq_count, queries, own_kv, branch)
    (
        hidden, grad_hidden, mlp_near, mlp_far, grad_attended,
        grad_proj, grad_expand, grad_contract, early, expand_terms,
    ) = middle(
        layer_scale, attended, token_rows, cotangent_rows, w_proj, w_expand, w_contract,
        branch_bias, expand_bias.reshape(1, -1), norm_gains, norm_shifts,
    )
    mlp_summed = mlp_near + swap(mlp_far, "tensor", 2).astype(F32)
    layer_out = (hidden + layer_scale * (mlp_summed + branch_bias[1])).astype(BF16)

    bits = [("dp", b) for b in bits_of("dp")]
    seq_bits = [("seq", b) for b in bits_of("seq")]
    weights = scatter_sum(jnp.concatenate([grad_contract, grad_expand, grad_proj], axis=1), bits + seq_bits)
    units = grad_contract.shape[1]
    grad_contract = weights[:, :units].T
    grad_expand = weights[:, units : 2 * units]
    grad_proj = weights[:, 2 * units :].T

    grad_queries, grad_kv = attend_backward(
        seq_count, queries, own_kv, all_kv, branch, grad_attended, attended_wide, logsum
    )
    grad_values = grad_kv[local_width:]
    stacked = jnp.concatenate([grad_queries, grad_kv], axis=0)
    stacked_slots = relative(stacked, 1).reshape(3, local_width, row_count)
    grad_normed = tensor_scatter(
        lambda k: jnp.einsum(
            "cer,cde->rd",
            stacked_slots[:, :, k * share : (k + 1) * share],
            w_attn,
            preferred_element_type=F32,
        )
    )
    grad_attn = jnp.einsum("rd,er->de", normed_one, stacked, preferred_element_type=F32)
    grad_attn = scatter_sum(grad_attn, bits + seq_bits)
    grad_attn = jnp.transpose(grad_attn.reshape(-1, 3, local_width), (1, 0, 2))
    xhat_one, inverse_one = layer_norm_parts(slot(token_rows, 0).astype(F32))
    grad_tokens = (
        grad_hidden + layer_norm_back(grad_normed, norm_gains[0], xhat_one, inverse_one)
    ).astype(BF16)

    everywhere = ("dp", "seq", "tensor")
    early = total_over(early, everywhere)
    late = total_over(
        jnp.stack([jnp.sum(grad_normed * xhat_one, axis=0), jnp.sum(grad_normed, axis=0)]),
        everywhere,
    )
    expand_terms = total_over(expand_terms, ("dp", "seq")).reshape(-1)
    bias_terms = total_over(
        jnp.stack(
            [
                jnp.sum(grad_queries.astype(F32), axis=1),
                jnp.sum(grad_values.astype(F32), axis=1),
            ]
        ),
        ("dp", "seq"),
    )
    out_shape = (1, 1, share, width)
    return (
        layer_out.reshape(out_shape),
        grad_tokens.reshape(out_shape),
        grad_attn,
        grad_proj,
        grad_expand,
        grad_contract,
        bias_terms,
        early[:2],
        expand_terms,
        jnp.stack([late[0], early[2]]),
        jnp.stack([late[1], early[3]]),
    )


def solution(mesh):
    placed = (
        P("dp", "seq", None, None),
        P("dp", "seq"),
        P(None, None, "tensor"),
        P("tensor", None),
        P(None, "tensor"),
        P("tensor", None),
        P(None, "tensor"),
        P(),
        P("tensor"),
        P(),
        P(),
        P("dp", "seq", None, None),
    )
    return jax.shard_map(
        shards,
        mesh=mesh,
        in_specs=placed,
        out_specs=(
            P("dp", "seq", "tensor", None),
            P("dp", "seq", "tensor", None),
            P(None, ("dp", "seq"), "tensor"),
            P("tensor", ("dp", "seq")),
            P(("dp", "seq"), "tensor"),
            P("tensor", ("dp", "seq")),
            P(None, "tensor"),
            P(),
            P("tensor"),
            P(),
            P(),
        ),
        check_vma=False,
    )
```

```python
import functools
import math

import jax
import jax.numpy as jnp
from jax import lax
from jax.experimental import pallas as pl
from jax.experimental.pallas import tpu as pltpu
from jax.sharding import PartitionSpec as P

HEAD_DIM = 64
LAYERS = 12
PCH = 512
CLEN = 512
F32 = jnp.float32
BF16 = jnp.bfloat16


norm_eps = 1e-05
big_negative = -1000000000.0


def layer_norm_parts(value):
    centre = jnp.mean(value, axis=-1, keepdims=True)
    centred = value - centre
    spread = jnp.mean(centred * centred, axis=-1, keepdims=True)
    inverse = lax.rsqrt(spread + norm_eps)
    return centred * inverse, inverse


def forward_kernel(n, heads, q_ref, kv_ref, branch_ref, o_ref, of_ref, lse_ref, kv_all, m_sc, l_sc, acc, up_send, up_recv, down_send, down_recv):
    z = lax.axis_index("seq")
    feats = heads * HEAD_DIM
    barrier = pltpu.get_barrier_semaphore()
    has_up, has_down = z < n - 1, z > 0

    def meet(to):
        pl.semaphore_signal(barrier, inc=1, device_id={"seq": to}, device_id_type=pl.DeviceIdType.MESH)

    @pl.when(has_up)
    def _(): meet(z + 1)
    @pl.when(has_down)
    def _(): meet(z - 1)
    pl.semaphore_wait(barrier, has_up.astype(jnp.int32) + has_down.astype(jnp.int32))

    own = kv_ref.at[:, 0:PCH]

    def hop(src, block, step, to, send, recv):
        return pltpu.make_async_remote_copy(src_ref=src, dst_ref=kv_all.at[block], send_sem=send.at[step], recv_sem=recv.at[step], device_id={"seq": to}, device_id_type=pl.DeviceIdType.MESH)

    @pl.when(has_up)
    def _(): hop(own, z, 0, z + 1, up_send, up_recv).start()
    @pl.when(has_down)
    def _(): hop(own, z, 0, z - 1, down_send, down_recv).start()

    def load_q(h, c):
        return q_ref[pl.ds(pl.multiple_of(h * HEAD_DIM, HEAD_DIM), HEAD_DIM), pl.ds(pl.multiple_of(c * PCH, PCH), PCH)]

    def scores(k, q):
        return lax.dot_general(k, q, (((0,), (0,)), ((), ())), preferred_element_type=F32)

    def diag(i, carry):
        c, h = i // heads, i % heads
        rows = pl.ds(pl.multiple_of(h * HEAD_DIM, HEAD_DIM), HEAD_DIM)
        vrows = pl.ds(pl.multiple_of(feats + h * HEAD_DIM, HEAD_DIM), HEAD_DIM)
        cols = pl.ds(pl.multiple_of(c * PCH, PCH), PCH)
        s = scores(kv_ref[rows, cols], load_q(h, c))
        key = lax.broadcasted_iota(jnp.int32, s.shape, 0)
        query = lax.broadcasted_iota(jnp.int32, s.shape, 1)
        s = jnp.where(key <= query, s, big_negative)
        m = jnp.max(s, axis=0, keepdims=True)
        p = jnp.exp(s - m)
        m_sc[h, :, cols] = m
        l_sc[h, :, cols] = jnp.sum(p, axis=0, keepdims=True)
        acc[rows, cols] = jnp.dot(kv_ref[vrows, cols], p.astype(BF16), preferred_element_type=F32)
        return carry
    lax.fori_loop(0, 2 * heads, diag, 0)

    branch = branch_ref[0, 0]

    def full(source, c, block):
        limit = jnp.where(c == 0, n * PCH, branch) - block * PCH
        def body(h, carry):
            rows = pl.ds(pl.multiple_of(h * HEAD_DIM, HEAD_DIM), HEAD_DIM)
            vrows = pl.ds(pl.multiple_of(feats + h * HEAD_DIM, HEAD_DIM), HEAD_DIM)
            cols = pl.ds(pl.multiple_of(c * PCH, PCH), PCH)
            s = scores(source[rows, :], load_q(h, c))
            key = lax.broadcasted_iota(jnp.int32, (PCH, 1), 0)
            s = s + jnp.where(key < limit, 0.0, big_negative)
            m_old = m_sc[h, :, cols]
            m = jnp.maximum(m_old, jnp.max(s, axis=0, keepdims=True))
            p = jnp.exp(s - m)
            alpha = jnp.exp(m_old - m)
            m_sc[h, :, cols] = m
            l_sc[h, :, cols] = l_sc[h, :, cols] * alpha + jnp.sum(p, axis=0, keepdims=True)
            acc[rows, cols] = acc[rows, cols] * alpha + jnp.dot(source[vrows, :], p.astype(BF16), preferred_element_type=F32)
            return carry
        lax.fori_loop(0, heads, body, 0)

    full(own, 1, z)

    def step_body(step, carry):
        @pl.when(z >= step)
        def _():
            hop(own, z - step, step - 1, z, up_send, up_recv).wait_recv()
            @pl.when(has_up & (step < n - 1))
            def _(): hop(kv_all.at[z - step], z - step, step, z + 1, up_send, up_recv).start()
        @pl.when(z + step < n)
        def _():
            hop(own, z + step, step - 1, z, down_send, down_recv).wait_recv()
            @pl.when(has_down & (step < n - 1))
            def _(): hop(kv_all.at[z + step], z + step, step, z - 1, down_send, down_recv).start()
        @pl.when(z >= step)
        def _():
            def both(c, carry):
                full(kv_all.at[z - step], c, z - step)
                return carry
            lax.fori_loop(0, 2, both, 0)
        @pl.when(z + step < n)
        def _(): full(kv_all.at[z + step], 1, z + step)
        return carry
    lax.fori_loop(1, n, step_body, 0)

    for h in range(heads):
        rows = slice(h * HEAD_DIM, (h + 1) * HEAD_DIM)
        total = l_sc[h]
        out = acc[rows, :] / total
        of_ref[rows, :] = out
        o_ref[rows, :] = out.astype(BF16)
        lse_ref[h:h + 1, :] = m_sc[h] + jnp.log(total)

    for step in range(n - 1):
        @pl.when(has_up & (z >= step))
        def _(): hop(own, z, step, z + 1, up_send, up_recv).wait_send()
        @pl.when(has_down & (z + step < n))
        def _(): hop(own, z, step, z - 1, down_send, down_recv).wait_send()

def attend_forward(n, q, kv, branch):
    feats, rows = q.shape
    heads = feats // HEAD_DIM
    vm = pl.BlockSpec(memory_space=pltpu.VMEM)
    return pl.pallas_call(
        functools.partial(forward_kernel, n, heads),
        out_shape=(jax.ShapeDtypeStruct((feats, rows), BF16), jax.ShapeDtypeStruct((feats, rows), F32), jax.ShapeDtypeStruct((heads, rows), F32), jax.ShapeDtypeStruct((n, 2 * feats, PCH), BF16)),
        in_specs=[vm, vm, pl.BlockSpec(memory_space=pltpu.SMEM)],
        out_specs=(vm, vm, vm, vm),
        scratch_shapes=[
            pltpu.VMEM((heads, 1, rows), F32),
            pltpu.VMEM((heads, 1, rows), F32),
            pltpu.VMEM((feats, rows), F32),
            pltpu.SemaphoreType.DMA((n - 1,)), pltpu.SemaphoreType.DMA((n - 1,)),
            pltpu.SemaphoreType.DMA((n - 1,)), pltpu.SemaphoreType.DMA((n - 1,)),
        ],
        compiler_params=pltpu.CompilerParams(collective_id=1, has_side_effects=True, vmem_limit_bytes=40 * 2**20),
        cost_estimate=pl.CostEstimate(flops=4 * 10**10, bytes_accessed=10**7, transcendentals=0),
        name="attend_forward",
    )(q, kv, branch)


def flip(index, bit):
    return index + bit * (1 - 2 * lax.rem(lax.div(index, bit), 2))


def log_bits(size):
    return [1 << k for k in range(size.bit_length() - 1)]


def finish_kernel(
    n, dp_count, heads, layer_scale,
    q_ref, kv_ref, all_ref, branch_ref, do_ref, of_ref, lse_ref, near_ref, far_ref,
    con_ref, exp_ref, proj_ref, early_ref, esum_ref, wa_ref, normed_ref, tok_ref, ghid_ref, gain_ref,
    lout_ref, gtok_ref, con_out, exp_out, proj_out, attn_out, sums_ref,
    dq_acc, own_acc, far_acc, lse_sc, dot_sc, up_out, up_in, down_out, down_in,
    stacked, mix, attn_flat, attn_sc, xhat_sc, inv_sc,
    con_xo, con_xi, con_acc, con_zo, con_zi,
    exp_xo, exp_xi, exp_acc, exp_zo, exp_zi,
    proj_xo, proj_xi, proj_acc, proj_zo, proj_zi,
    attn_xo, attn_xi, attn_acc, attn_zo, attn_zi,
    core_out, core_in, y_out, y_in, far_in, small_out, small_in,
    up_send, up_recv, down_send, down_recv, x_send, x_recv, z_send, z_recv,
    core_send, core_recv, y_send, y_recv, small_send, small_recv,
):
    z = lax.axis_index("seq")
    t = lax.axis_index("tensor")
    dp = lax.axis_index("dp")
    feats = heads * HEAD_DIM
    share = ghid_ref.shape[0]
    has_up, has_down = z < n - 1, z > 0
    dp_bits = log_bits(dp_count)
    bits = len(dp_bits)
    blocks = dp_count * n
    mesh_ids = pl.DeviceIdType.MESH

    barrier = pltpu.get_barrier_semaphore()
    peers = [{"seq": lax.rem(z + d, n)} for d in range(1, n)]
    peers += [{"tensor": flip(t, bit)} for bit in (1, 2)]
    peers += [{"dp": flip(dp, bit)} for bit in dp_bits]
    for peer in peers:
        pl.semaphore_signal(barrier, inc=1, device_id=peer, device_id_type=mesh_ids)
    pl.semaphore_wait(barrier, len(peers))

    def remote(src, dst, send, recv, to):
        return pltpu.make_async_remote_copy(
            src_ref=src, dst_ref=dst, send_sem=send, recv_sem=recv, device_id=to, device_id_type=mesh_ids
        )

    class Scatter:
        def __init__(self, number, source, xo, xi, acc, zo, zi, out):
            self.number, self.source, self.xo, self.xi = number, source, xo, xi
            self.acc, self.zo, self.zi, self.out = acc, zo, zi, out

        def x_copy(self, s):
            half, start = blocks >> (s + 1), blocks - (blocks >> s)
            sem = self.number * bits + s
            return remote(
                self.xo.at[start : start + half], self.xi.at[start : start + half],
                x_send.at[sem], x_recv.at[sem], {"dp": flip(dp, dp_count >> (s + 1))},
            )

        def mine(self, s):
            return lax.rem(lax.div(dp, dp_count >> (s + 1)), 2)

        def x_begin(self, s):
            half, start = blocks >> (s + 1), blocks - (blocks >> s)
            held = self.source if s == 0 else self.acc
            other = (1 - self.mine(s)) * half

            def body(j, carry):
                self.xo[start + j] = held[other + j].astype(BF16)
                return carry

            lax.fori_loop(0, half, body, 0)
            self.x_copy(s).start()

        def x_end(self):
            for s in range(bits):
                half, start = blocks >> (s + 1), blocks - (blocks >> s)
                held = self.source if s == 0 else self.acc
                own = self.mine(s) * half
                self.x_copy(s).wait_recv()

                def body(j, carry):
                    self.acc[j] = held[own + j] + self.xi[start + j].astype(F32)
                    return carry

                lax.fori_loop(0, half, body, 0)
                if s + 1 < bits:
                    self.x_begin(s + 1)

        def z_copy(self, d):
            sem = self.number * (n - 1) + d - 1
            return remote(
                self.zo.at[d - 1], self.zi.at[d - 1], z_send.at[sem], z_recv.at[sem],
                {"seq": lax.rem(z + d, n)},
            )

        def z_begin(self):
            for d in range(1, n):
                self.zo[d - 1] = self.acc[lax.rem(z + d, n)].astype(BF16)
                self.z_copy(d).start()

        def z_end(self):
            total = self.acc[z]
            for d in range(1, n):
                self.z_copy(d).wait_recv()
                total = total + self.zi[d - 1].astype(F32)
            self.out[...] = total

        def drain(self):
            for s in range(bits):
                self.x_copy(s).wait_send()
            for d in range(1, n):
                self.z_copy(d).wait_send()

    contract = Scatter(0, con_ref, con_xo, con_xi, con_acc, con_zo, con_zi, con_out)
    expand = Scatter(1, exp_ref, exp_xo, exp_xi, exp_acc, exp_zo, exp_zi, exp_out)
    project = Scatter(2, proj_ref, proj_xo, proj_xi, proj_acc, proj_zo, proj_zi, proj_out)
    attn = Scatter(3, attn_sc, attn_xo, attn_xi, attn_acc, attn_zo, attn_zi, attn_out)
    scatters = (contract, expand, project, attn)

    sibling, partner = {"tensor": flip(t, 1)}, {"tensor": flip(t, 2)}
    far_copy = remote(far_ref, far_in, y_send.at[0], y_recv.at[0], partner)
    far_copy.start()
    for one in (contract, expand, project):
        one.x_begin(0)

    def hop(out, inn, d, to, send, recv):
        return remote(out.at[d], inn.at[d], send.at[d], recv.at[d], {"seq": to})

    dq_acc[...] = jnp.zeros_like(dq_acc)
    for h in range(heads):
        rows = slice(h * HEAD_DIM, (h + 1) * HEAD_DIM)
        lse_sc[h] = lse_ref[h:h + 1, :]
        dot_sc[h] = jnp.sum(do_ref[rows, :].astype(F32) * of_ref[rows, :], axis=0, keepdims=True)

    nt = (((1,), (1,)), ((), ()))
    tn = (((0,), (0,)), ((), ()))
    tt = (((0,), (1,)), ((), ()))

    def tile(h, cols, k, v, mask):
        rows = pl.ds(pl.multiple_of(h * HEAD_DIM, HEAD_DIM), HEAD_DIM)
        q, do = q_ref[rows, cols], do_ref[rows, cols]
        s = mask(lax.dot_general(k, q, tn, preferred_element_type=F32))
        p = jnp.exp(s - lse_sc[h, :, cols])
        dp = lax.dot_general(v, do, tn, preferred_element_type=F32)
        ds = (p * (dp - dot_sc[h, :, cols])).astype(BF16)
        p = p.astype(BF16)
        dv = lax.dot_general(do, p, nt, preferred_element_type=F32)
        dk = lax.dot_general(q, ds, nt, preferred_element_type=F32)
        dq_acc[rows, cols] += jnp.dot(k, ds, preferred_element_type=F32)
        return dk, dv

    def head_rows(h):
        return (pl.ds(pl.multiple_of(h * HEAD_DIM, HEAD_DIM), HEAD_DIM),
                pl.ds(pl.multiple_of(feats + h * HEAD_DIM, HEAD_DIM), HEAD_DIM))

    def columns(c):
        return pl.ds(pl.multiple_of(c * PCH, PCH), PCH)

    branch = branch_ref[0, 0]

    def full(source, c, block, total):
        limit = jnp.where(c == 0, n * PCH, branch) - block * PCH
        def mask(s):
            key = lax.broadcasted_iota(jnp.int32, (PCH, 1), 0)
            return s + jnp.where(key < limit, 0.0, big_negative)
        def body(h, carry):
            rows, vrows = head_rows(h)
            dk, dv = tile(h, columns(c), source[rows, :], source[vrows, :], mask)
            total[rows, :] += dk
            total[vrows, :] += dv
            return carry
        lax.fori_loop(0, heads, body, 0)

    def diag(i, carry):
        c, h = i // heads, i % heads
        rows, vrows = head_rows(h)
        cols = columns(c)
        def mask(s):
            key = lax.broadcasted_iota(jnp.int32, s.shape, 0)
            query = lax.broadcasted_iota(jnp.int32, s.shape, 1)
            return jnp.where(key <= query, s, big_negative)
        dk, dv = tile(h, cols, kv_ref[rows, cols], kv_ref[vrows, cols], mask)
        own_acc[rows, cols] = dk
        own_acc[vrows, cols] = dv
        return carry

    own_step = jnp.where(has_up & has_down, 0, n - 1)

    def step_body(step, carry):
        d = n - 1 - step

        @pl.when(step == own_step)
        def _():
            lax.fori_loop(0, 2 * heads, diag, 0)
            full(kv_ref.at[:, 0:PCH], 1, z, own_acc.at[:, 0:PCH])

        @pl.when((d >= 1) & (z + d < n))
        def _():
            far_acc[...] = jnp.zeros_like(far_acc)
            full(all_ref.at[z + d], 1, z + d, far_acc)
            @pl.when(has_down & (d < n - 1))
            def _():
                hop(up_out, up_in, d, z, up_send, up_recv).wait_recv()
                far_acc[...] += up_in[d].astype(F32)
            up_out[d - 1] = far_acc[...].astype(BF16)
            hop(up_out, up_in, d - 1, z + 1, up_send, up_recv).start()

        @pl.when((d >= 1) & (z >= d))
        def _():
            far_acc[...] = jnp.zeros_like(far_acc)
            def both(c, carry):
                full(all_ref.at[z - d], c, z - d, far_acc)
                return carry
            lax.fori_loop(0, 2, both, 0)
            @pl.when(has_up & (d < n - 1))
            def _():
                hop(down_out, down_in, d, z, down_send, down_recv).wait_recv()
                far_acc[...] += down_in[d].astype(F32)
            down_out[d - 1] = far_acc[...].astype(BF16)
            hop(down_out, down_in, d - 1, z - 1, down_send, down_recv).start()

        @pl.when(step == n - 3)
        def _():
            contract.x_end()
            contract.z_begin()

        @pl.when(step == n - 2)
        def _():
            for one in (expand, project):
                one.x_end()
                one.z_begin()
        return carry
    lax.fori_loop(0, n, step_body, 0)

    stacked[0:feats, :] = (dq_acc[...] * (1.0 / math.sqrt(HEAD_DIM))).astype(BF16)
    stacked[feats:, PCH:] = own_acc[:, PCH:].astype(BF16)

    @pl.when(has_down)
    def _():
        hop(up_out, up_in, 0, z, up_send, up_recv).wait_recv()
        own_acc[:, 0:PCH] += up_in[0].astype(F32)
    @pl.when(has_up)
    def _():
        hop(down_out, down_in, 0, z, down_send, down_recv).wait_recv()
        own_acc[:, 0:PCH] += down_in[0].astype(F32)
    stacked[feats:, 0:PCH] = own_acc[:, 0:PCH].astype(BF16)

    def place(k):
        owner = t
        for bit in (1, 2):
            turned = flip(owner, bit)
            if isinstance(k, int):
                owner = turned if k & bit else owner
            else:
                owner = jnp.where(lax.rem(lax.div(k, bit), 2) == 1, turned, owner)
        return pl.ds(pl.multiple_of(owner * share, share), share)

    def grad_normed(k):
        total = None
        for c in range(3):
            term = lax.dot_general(
                stacked[c * feats : (c + 1) * feats, place(k)], wa_ref[c], tt, preferred_element_type=F32
            )
            total = term if total is None else total + term
        mix[k] = total
        return total

    def core_copy(i):
        return remote(core_out.at[i], core_in.at[i], core_send.at[i], core_recv.at[i], sibling)

    core_out[0] = grad_normed(3).astype(BF16)
    core_copy(0).start()

    attn_flat[...] = jnp.dot(stacked[...], normed_ref[...], preferred_element_type=F32).T
    rows = attn_sc.shape[1]
    for b in range(blocks):
        attn_sc[b] = attn_flat[b * rows : (b + 1) * rows, :]
    attn.x_begin(0)

    last = grad_normed(2)
    core_copy(0).wait_recv()
    y_out[...] = (last + core_in[0].astype(F32)).astype(BF16)
    y_copy = remote(y_out, y_in, y_send.at[1], y_recv.at[1], partner)
    y_copy.start()
    core_out[1] = grad_normed(1).astype(BF16)
    core_copy(1).start()
    grad_normed(0)

    small_out[0, 0:2, :] = jnp.zeros((2, small_out.shape[2]), F32)
    small_out[0, 2:6, :] = early_ref[...]
    small_out[0, 6:7, :] = esum_ref[...]
    small_out[0, 7:8, :] = jnp.zeros((1, small_out.shape[2]), F32)
    ones = jnp.ones((8, stacked.shape[1]), BF16)
    small_out[0, 7:8, 0 : 3 * feats] = lax.dot_general(ones, stacked[...], nt, preferred_element_type=F32)[0:1]

    def statistics(i, carry):
        k = 3 - i
        value = tok_ref[place(k), :].astype(F32)
        centred = value - jnp.mean(value, axis=-1, keepdims=True)
        inverse = lax.rsqrt(jnp.mean(centred * centred, axis=-1, keepdims=True) + norm_eps)
        xhat = centred * inverse
        xhat_sc[...] = xhat
        inv_sc[...] = jnp.broadcast_to(inverse, inv_sc.shape)
        small_out[0, 0:1, :] += jnp.sum(mix[k] * xhat, axis=0, keepdims=True)
        small_out[0, 1:2, :] += jnp.sum(mix[k], axis=0, keepdims=True)
        return carry

    lax.fori_loop(0, 4, statistics, 0)

    stages = [{"seq": flip(z, bit)} for bit in log_bits(n)]
    stages += [sibling, partner]
    stages += [{"dp": flip(dp, bit)} for bit in dp_bits]

    def small_copy(i):
        return remote(small_out.at[i], small_in.at[i], small_send.at[i], small_recv.at[i], stages[i])

    def small_end(i):
        small_copy(i).wait_recv()
        value = small_out[i] + small_in[i]
        if "tensor" in stages[i]:
            row = lax.broadcasted_iota(jnp.int32, value.shape, 0)
            value = jnp.where(row < 6, value, small_out[i])
        if i + 1 < len(stages):
            small_out[i + 1] = value
            small_copy(i + 1).start()
        else:
            sums_ref[...] = value

    small_copy(0).start()
    contract.z_end()
    small_end(0)
    far_copy.wait_recv()
    lout_ref[...] = (near_ref[...] + layer_scale * far_in[...].astype(F32)).astype(BF16)
    small_end(1)
    attn.x_end()
    attn.z_begin()
    small_end(2)
    expand.z_end()
    project.z_end()

    core_copy(1).wait_recv()
    y_copy.wait_recv()
    mixed = mix[0] + core_in[1].astype(F32) + y_in[...].astype(F32)
    e = mixed * gain_ref[0:1, :]
    xhat = xhat_sc[...]
    gtok_ref[...] = (
        ghid_ref[...]
        + inv_sc[:, 0:1]
        * (e - jnp.mean(e, axis=-1, keepdims=True) - xhat * jnp.mean(e * xhat, axis=-1, keepdims=True))
    ).astype(BF16)
    for i in range(3, len(stages)):
        small_end(i)
    attn.z_end()

    for d in range(1, n):
        @pl.when(z + d < n)
        def _(): hop(up_out, up_in, d - 1, z + 1, up_send, up_recv).wait_send()
        @pl.when(z >= d)
        def _(): hop(down_out, down_in, d - 1, z - 1, down_send, down_recv).wait_send()
    for one in scatters:
        one.drain()
    far_copy.wait_send()
    y_copy.wait_send()
    for i in range(2):
        core_copy(i).wait_send()
    for i in range(len(stages)):
        small_copy(i).wait_send()


def finish(
    n, dp_count, layer_scale, q, kv, kv_all, branch, do, of, lse, near, far,
    grad_contract, grad_expand, grad_proj, early, expand_terms, w_attn, normed_one, token_rows,
    grad_hidden, norm_gains,
):
    feats, rows = q.shape
    heads = feats // HEAD_DIM
    share, width = grad_hidden.shape
    blocks = dp_count * n
    bits = len(log_bits(dp_count))
    vm = pl.BlockSpec(memory_space=pltpu.VMEM)
    slots = pltpu.VMEM((n - 1, 2 * feats, PCH), BF16)
    shape = jax.ShapeDtypeStruct
    sems = lambda count: pltpu.SemaphoreType.DMA((count,))
    split = lambda weight: weight.reshape(blocks, weight.shape[0] // blocks, weight.shape[1])
    parts = [split(grad_contract), split(grad_expand), split(grad_proj)]
    block_rows = width // blocks
    widths = [part.shape[2] for part in parts] + [3 * feats]
    scatter_scratch = []
    for columns in widths:
        scatter_scratch += [
            pltpu.VMEM((blocks - n, block_rows, columns), BF16),
            pltpu.VMEM((blocks - n, block_rows, columns), BF16),
            pltpu.VMEM((blocks // 2, block_rows, columns), F32),
            pltpu.VMEM((n - 1, block_rows, columns), BF16),
            pltpu.VMEM((n - 1, block_rows, columns), BF16),
        ]
    stages = len(log_bits(n)) + 2 + bits
    return pl.pallas_call(
        functools.partial(finish_kernel, n, dp_count, heads, layer_scale),
        out_shape=(
            shape((share, width), BF16),
            shape((share, width), BF16),
            *(shape((block_rows, columns), F32) for columns in widths),
            shape((8, width), F32),
        ),
        in_specs=[vm, vm, vm, pl.BlockSpec(memory_space=pltpu.SMEM)] + [vm] * 15,
        out_specs=(vm,) * 7,
        scratch_shapes=[
            pltpu.VMEM((feats, rows), F32),
            pltpu.VMEM((2 * feats, rows), F32),
            pltpu.VMEM((2 * feats, PCH), F32),
            pltpu.VMEM((heads, 1, rows), F32),
            pltpu.VMEM((heads, 1, rows), F32),
            slots, slots, slots, slots,
            pltpu.VMEM((3 * feats, rows), BF16),
            pltpu.VMEM((4, share, width), F32),
            pltpu.VMEM((width, 3 * feats), F32),
            pltpu.VMEM((blocks, block_rows, 3 * feats), F32),
            pltpu.VMEM((share, width), F32),
            pltpu.VMEM((share, 128), F32),
            *scatter_scratch,
            pltpu.VMEM((2, share, width), BF16),
            pltpu.VMEM((2, share, width), BF16),
            pltpu.VMEM((share, width), BF16),
            pltpu.VMEM((share, width), BF16),
            pltpu.VMEM((share, width), BF16),
            pltpu.VMEM((stages, 8, width), F32),
            pltpu.VMEM((stages, 8, width), F32),
            sems(n - 1), sems(n - 1), sems(n - 1), sems(n - 1),
            sems(4 * bits), sems(4 * bits), sems(4 * (n - 1)), sems(4 * (n - 1)),
            sems(2), sems(2), sems(2), sems(2), sems(stages), sems(stages),
        ],
        compiler_params=pltpu.CompilerParams(
            collective_id=2, has_side_effects=True, vmem_limit_bytes=60 * 2**20
        ),
        cost_estimate=pl.CostEstimate(flops=4 * 10**10, bytes_accessed=10**7, transcendentals=0),
        name="finish",
    )(
        q, kv, kv_all, branch, do, of, lse, near, far, *parts, early, expand_terms,
        w_attn, normed_one, token_rows, grad_hidden, norm_gains,
    )


def middle_kernel(
    layer_scale, o_ref, tok_ref, cot_ref, wp_ref, we_ref, wc_ref, bb_ref, eb_ref, gain_ref, shift_ref,
    ghid_ref, near_ref, far_ref, gatt_ref, gproj_ref, gexp_ref, gcon_ref, sums_ref, esum_ref,
    ga_sc, mix_sc, n2, gm, act, gp, att, own_sc, xhat_sc, inv_sc, proj_sc,
    core_out, core_in, y_out, y_in, core_send, core_recv, y_send, y_recv, n2_send, n2_recv, att_send, att_recv,
):
    t = lax.axis_index("tensor")
    y, c = t // 2, t % 2
    sibling = y * 2 + (1 - c)
    partner = (1 - y) * 2 + c
    share = own_sc.shape[0]

    def block(k):
        if isinstance(k, int):
            return ((1 - y) if k >= 2 else y) * 2 + ((1 - c) if k % 2 else c)
        return jnp.where(k >= 2, 1 - y, y) * 2 + jnp.where(k % 2 == 1, 1 - c, c)

    def place(k):
        return pl.ds(pl.multiple_of(block(k) * share, share), share)

    barrier = pltpu.get_barrier_semaphore()
    for to in (sibling, partner):
        pl.semaphore_signal(barrier, inc=1, device_id={"tensor": to}, device_id_type=pl.DeviceIdType.MESH)
    pl.semaphore_wait(barrier, 2)

    def copy(src, dst, send, recv, to):
        return pltpu.make_async_remote_copy(
            src_ref=src, dst_ref=dst, send_sem=send, recv_sem=recv,
            device_id={"tensor": to}, device_id_type=pl.DeviceIdType.MESH,
        )

    def core_copy(i):
        return copy(core_out.at[i], core_in.at[i], core_send.at[i], core_recv.at[i], sibling)

    def y_copy(i):
        return copy(y_out.at[i], y_in.at[i], y_send.at[i], y_recv.at[i], partner)

    def gather(ref, send, recv):
        return (
            copy(ref.at[0], ref.at[2], send.at[0], recv.at[0], partner),
            copy(ref.at[0], ref.at[1], send.at[1], recv.at[1], sibling),
            copy(ref.at[2], ref.at[3], send.at[2], recv.at[2], sibling),
        )

    tn = (((0,), (0,)), ((), ()))
    nt = (((1,), (1,)), ((), ()))

    def project(k):
        return lax.dot_general(o_ref[:, place(k)], wp_ref[...], tn, preferred_element_type=F32)

    core_out[0] = project(3).astype(BF16)
    core_copy(0).start()
    own_sc[...] = project(2)
    core_out[1] = project(1).astype(BF16)
    core_copy(1).start()
    core_copy(0).wait_recv()
    y_out[0] = (own_sc[...] + core_in[0].astype(F32)).astype(BF16)
    y_copy(0).start()
    own_sc[...] = project(0)

    def before(k, carry):
        g = (cot_ref[place(k), :].astype(F32) * layer_scale).astype(BF16)
        gm[k] = g
        ga_sc[k] = lax.dot_general(g, wc_ref[...], nt, preferred_element_type=F32)
        return carry

    lax.fori_loop(0, 4, before, 0)
    core_copy(1).wait_recv()
    own_sc[...] += core_in[1].astype(F32)
    y_copy(0).wait_recv()

    hidden = tok_ref[place(0), :].astype(F32) + layer_scale * (
        own_sc[...] + y_in[0].astype(F32) + bb_ref[0:1, :]
    )
    near_ref[...] = hidden + layer_scale * bb_ref[1:2, :]
    centred = hidden - jnp.mean(hidden, axis=-1, keepdims=True)
    inverse = lax.rsqrt(jnp.mean(centred * centred, axis=-1, keepdims=True) + norm_eps)
    xhat = centred * inverse
    n2[0] = (xhat * gain_ref[1:2, :] + shift_ref[1:2, :]).astype(BF16)
    across, near, on = gather(n2, n2_send, n2_recv)
    across.start()
    near.start()
    xhat_sc[...] = xhat
    inv_sc[...] = jnp.broadcast_to(inverse, inv_sc.shape)
    esum_ref[...] = jnp.zeros_like(esum_ref)

    def process(k, carry):
        @pl.when(k == 1)
        def _():
            near.wait_recv()

        @pl.when(k == 2)
        def _():
            across.wait_recv()
            on.start()

        @pl.when(k == 3)
        def _():
            on.wait_recv()

        v = jnp.dot(n2[k], we_ref[...], preferred_element_type=F32) + eb_ref[...]
        square = v * v
        th = jnp.tanh(math.sqrt(2.0 / math.pi) * (v + 0.044715 * (v * square)))
        cdf = 0.5 * (1.0 + th)
        act[k] = (v * cdf).astype(BF16)
        slope = cdf + 0.5 * v * (1.0 - th * th) * (
            math.sqrt(2.0 / math.pi) * (1.0 + 3 * 0.044715 * square)
        )
        g = (slope * ga_sc[k]).astype(BF16)
        gp[k] = g
        esum_ref[...] += jnp.sum(g.astype(F32), axis=0, keepdims=True)
        mix_sc[k] = lax.dot_general(g, we_ref[...], nt, preferred_element_type=F32)
        return carry

    lax.fori_loop(0, 4, process, 0)
    core_out[2] = mix_sc[3].astype(BF16)
    core_copy(2).start()
    core_out[3] = mix_sc[1].astype(BF16)
    core_copy(3).start()
    core_copy(2).wait_recv()
    y_out[1] = (mix_sc[2] + core_in[2].astype(F32)).astype(BF16)
    y_copy(1).start()

    rows = 4 * share
    width = gm.shape[2]
    gcon_ref[...] = lax.dot_general(
        gm[...].reshape(rows, width), act[...].reshape(rows, -1), tn, preferred_element_type=F32
    )
    gexp_ref[...] = lax.dot_general(
        n2[...].reshape(rows, width), gp[...].reshape(rows, -1), tn, preferred_element_type=F32
    )

    def contract(k):
        return jnp.dot(act[k], wc_ref[...], preferred_element_type=F32)

    core_out[4] = contract(3).astype(BF16)
    core_copy(4).start()
    core_out[5] = contract(1).astype(BF16)
    core_copy(5).start()
    near_ref[...] += layer_scale * contract(0)
    last = contract(2)
    core_copy(4).wait_recv()
    far_ref[...] = (last + core_in[4].astype(F32)).astype(BF16)
    core_copy(5).wait_recv()
    near_ref[...] += layer_scale * core_in[5].astype(F32)

    core_copy(3).wait_recv()
    mixed = mix_sc[0] + core_in[3].astype(F32)
    y_copy(1).wait_recv()
    mixed = mixed + y_in[1].astype(F32)
    e = mixed * gain_ref[1:2, :]
    xhat = xhat_sc[...]
    grad_hidden = cot_ref[place(0), :].astype(F32) + inv_sc[:, 0:1] * (
        e - jnp.mean(e, axis=-1, keepdims=True) - xhat * jnp.mean(e * xhat, axis=-1, keepdims=True)
    )
    g = (grad_hidden * layer_scale).astype(BF16)
    att[0] = g
    across_b, near_b, on_b = gather(att, att_send, att_recv)
    across_b.start()
    near_b.start()
    ghid_ref[...] = grad_hidden
    sums_ref[0:1, :] = jnp.sum(g.astype(F32), axis=0, keepdims=True)
    sums_ref[1:2, :] = jnp.sum(gm[0].astype(F32), axis=0, keepdims=True)
    sums_ref[2:3, :] = jnp.sum(mixed * xhat, axis=0, keepdims=True)
    sums_ref[3:4, :] = jnp.sum(mixed, axis=0, keepdims=True)

    proj_sc[...] = jnp.zeros_like(proj_sc)

    def after(k, carry):
        @pl.when(k == 1)
        def _():
            near_b.wait_recv()

        @pl.when(k == 2)
        def _():
            across_b.wait_recv()
            on_b.start()

        @pl.when(k == 3)
        def _():
            on_b.wait_recv()

        gatt_ref[:, place(k)] = lax.dot_general(
            wp_ref[...], att[k], nt, preferred_element_type=F32
        ).astype(BF16)
        proj_sc[...] += jnp.dot(o_ref[:, place(k)], att[k], preferred_element_type=F32)
        return carry

    lax.fori_loop(0, 4, after, 0)
    gproj_ref[...] = proj_sc[...].T
    for i in range(6):
        core_copy(i).wait_send()
    for i in range(2):
        y_copy(i).wait_send()
    for one in (across, near, on, across_b, near_b, on_b):
        one.wait_send()


def middle(
    layer_scale, attended, token_rows, cotangent_rows, w_proj, w_expand, w_contract,
    branch_bias, expand_bias, norm_gains, norm_shifts,
):
    rows, width = token_rows.shape
    feats, hidden_units = w_proj.shape[0], w_expand.shape[1]
    share = rows // 4
    vm = pl.BlockSpec(memory_space=pltpu.VMEM)
    shape = jax.ShapeDtypeStruct
    slots = lambda columns, kind: pltpu.VMEM((4, share, columns), kind)
    sems = lambda count: pltpu.SemaphoreType.DMA((count,))
    return pl.pallas_call(
        functools.partial(middle_kernel, layer_scale),
        out_shape=(
            shape((share, width), F32),
            shape((share, width), F32),
            shape((share, width), BF16),
            shape((feats, rows), BF16),
            shape((width, feats), F32),
            shape((width, hidden_units), F32),
            shape((width, hidden_units), F32),
            shape((4, width), F32),
            shape((1, hidden_units), F32),
        ),
        in_specs=[vm] * 10,
        out_specs=(vm,) * 9,
        scratch_shapes=[
            slots(hidden_units, F32),
            slots(width, F32),
            slots(width, BF16),
            slots(width, BF16),
            slots(hidden_units, BF16),
            slots(hidden_units, BF16),
            slots(width, BF16),
            pltpu.VMEM((share, width), F32),
            pltpu.VMEM((share, width), F32),
            pltpu.VMEM((share, 128), F32),
            pltpu.VMEM((feats, width), F32),
            pltpu.VMEM((6, share, width), BF16),
            pltpu.VMEM((6, share, width), BF16),
            pltpu.VMEM((2, share, width), BF16),
            pltpu.VMEM((2, share, width), BF16),
            sems(6), sems(6), sems(2), sems(2), sems(3), sems(3), sems(3), sems(3),
        ],
        compiler_params=pltpu.CompilerParams(
            collective_id=3, has_side_effects=True, vmem_limit_bytes=56 * 2**20
        ),
        cost_estimate=pl.CostEstimate(flops=5 * 10**10, bytes_accessed=2 * 10**7, transcendentals=0),
        name="middle",
    )(
        attended, token_rows, cotangent_rows, w_proj, w_expand, w_contract,
        branch_bias, expand_bias, norm_gains, norm_shifts,
    )


def shards(
    tokens,
    branch,
    w_attn,
    w_proj,
    w_expand,
    w_contract,
    attn_bias,
    branch_bias,
    expand_bias,
    norm_gains,
    norm_shifts,
    cotangent,
):
    seq_count = lax.axis_size("seq")
    width = tokens.shape[3]
    row_count = tokens.shape[2]
    share = row_count // lax.axis_size("tensor")
    local_width = w_attn.shape[2]
    score_scale = 1.0 / math.sqrt(HEAD_DIM)
    layer_scale = 1.0 / math.sqrt(LAYERS)

    token_rows = tokens.reshape(row_count, width)
    cotangent_rows = cotangent.reshape(row_count, width)
    flat_rows = token_rows.astype(F32)
    normed_one = (
        layer_norm_parts(flat_rows)[0] * norm_gains[0] + norm_shifts[0]
    ).astype(BF16)
    projected = jnp.einsum("cde,rd->cer", w_attn, normed_one, preferred_element_type=F32)
    bias_rows = jnp.stack([attn_bias[0], jnp.zeros_like(attn_bias[0]), attn_bias[1]])
    projected = (projected + bias_rows[:, :, None]).astype(BF16)
    queries = projected[0] * jnp.asarray(score_scale, BF16)
    own_kv = projected[1:].reshape(2 * local_width, row_count)

    attended, attended_wide, logsum, all_kv = attend_forward(seq_count, queries, own_kv, branch)
    (
        grad_hidden, mlp_near, mlp_far, grad_attended,
        grad_proj, grad_expand, grad_contract, early, expand_terms,
    ) = middle(
        layer_scale, attended, token_rows, cotangent_rows, w_proj, w_expand, w_contract,
        branch_bias, expand_bias.reshape(1, -1), norm_gains, norm_shifts,
    )
    layer_out, grad_tokens, grad_contract, grad_expand, grad_proj, grad_attn, sums = finish(
        seq_count, lax.axis_size("dp"), layer_scale, queries, own_kv, all_kv, branch, grad_attended,
        attended_wide, logsum, mlp_near, mlp_far, grad_contract, grad_expand, grad_proj, early,
        expand_terms, w_attn, normed_one, token_rows, grad_hidden, norm_gains,
    )
    out_shape = (1, 1, share, width)
    biases = sums[7, : 3 * local_width].reshape(3, local_width)
    return (
        layer_out.reshape(out_shape),
        grad_tokens.reshape(out_shape),
        jnp.transpose(grad_attn.reshape(-1, 3, local_width), (1, 0, 2)),
        grad_proj.T,
        grad_expand,
        grad_contract.T,
        jnp.stack([biases[0], biases[2]]),
        sums[2:4],
        sums[6],
        jnp.stack([sums[0], sums[4]]),
        jnp.stack([sums[1], sums[5]]),
    )


def solution(mesh):
    placed = (
        P("dp", "seq", None, None),
        P("dp", "seq"),
        P(None, None, "tensor"),
        P("tensor", None),
        P(None, "tensor"),
        P("tensor", None),
        P(None, "tensor"),
        P(),
        P("tensor"),
        P(),
        P(),
        P("dp", "seq", None, None),
    )
    return jax.shard_map(
        shards,
        mesh=mesh,
        in_specs=placed,
        out_specs=(
            P("dp", "seq", "tensor", None),
            P("dp", "seq", "tensor", None),
            P(None, ("dp", "seq"), "tensor"),
            P("tensor", ("dp", "seq")),
            P(("dp", "seq"), "tensor"),
            P("tensor", ("dp", "seq")),
            P(None, "tensor"),
            P(),
            P("tensor"),
            P(),
            P(),
        ),
        check_vma=False,
    )
```

```python
import functools
import math

import jax
import jax.numpy as jnp
from jax import lax
from jax.experimental import pallas as pl
from jax.experimental.pallas import tpu as pltpu
from jax.sharding import PartitionSpec as P

HEAD_DIM = 64
LAYERS = 12
PCH = 512
CLEN = 512
F32 = jnp.float32
BF16 = jnp.bfloat16


norm_eps = 1e-05
big_negative = -1000000000.0


def layer_norm_parts(value):
    centre = jnp.mean(value, axis=-1, keepdims=True)
    centred = value - centre
    spread = jnp.mean(centred * centred, axis=-1, keepdims=True)
    inverse = lax.rsqrt(spread + norm_eps)
    return centred * inverse, inverse


def forward_kernel(n, heads, q_ref, kv_ref, branch_ref, o_ref, of_ref, lse_ref, kv_all, m_sc, l_sc, acc, up_send, up_recv, down_send, down_recv):
    z = lax.axis_index("seq")
    feats = heads * HEAD_DIM
    barrier = pltpu.get_barrier_semaphore()
    has_up, has_down = z < n - 1, z > 0

    def meet(to):
        pl.semaphore_signal(barrier, inc=1, device_id={"seq": to}, device_id_type=pl.DeviceIdType.MESH)

    @pl.when(has_up)
    def _(): meet(z + 1)
    @pl.when(has_down)
    def _(): meet(z - 1)
    pl.semaphore_wait(barrier, has_up.astype(jnp.int32) + has_down.astype(jnp.int32))

    own = kv_ref.at[:, 0:PCH]

    def hop(src, block, step, to, send, recv):
        return pltpu.make_async_remote_copy(src_ref=src, dst_ref=kv_all.at[block], send_sem=send.at[step], recv_sem=recv.at[step], device_id={"seq": to}, device_id_type=pl.DeviceIdType.MESH)

    @pl.when(has_up)
    def _(): hop(own, z, 0, z + 1, up_send, up_recv).start()
    @pl.when(has_down)
    def _(): hop(own, z, 0, z - 1, down_send, down_recv).start()

    def load_q(h, c):
        return q_ref[pl.ds(pl.multiple_of(h * HEAD_DIM, HEAD_DIM), HEAD_DIM), pl.ds(pl.multiple_of(c * PCH, PCH), PCH)]

    def scores(k, q):
        return lax.dot_general(k, q, (((0,), (0,)), ((), ())), preferred_element_type=F32)

    def diag(i, carry):
        c, h = i // heads, i % heads
        rows = pl.ds(pl.multiple_of(h * HEAD_DIM, HEAD_DIM), HEAD_DIM)
        vrows = pl.ds(pl.multiple_of(feats + h * HEAD_DIM, HEAD_DIM), HEAD_DIM)
        cols = pl.ds(pl.multiple_of(c * PCH, PCH), PCH)
        s = scores(kv_ref[rows, cols], load_q(h, c))
        key = lax.broadcasted_iota(jnp.int32, s.shape, 0)
        query = lax.broadcasted_iota(jnp.int32, s.shape, 1)
        s = jnp.where(key <= query, s, big_negative)
        m = jnp.max(s, axis=0, keepdims=True)
        p = jnp.exp(s - m)
        m_sc[h, :, cols] = m
        l_sc[h, :, cols] = jnp.sum(p, axis=0, keepdims=True)
        acc[rows, cols] = jnp.dot(kv_ref[vrows, cols], p.astype(BF16), preferred_element_type=F32)
        return carry
    lax.fori_loop(0, 2 * heads, diag, 0)

    branch = branch_ref[0, 0]

    def full(source, c, block):
        limit = jnp.where(c == 0, n * PCH, branch) - block * PCH
        def body(h, carry):
            rows = pl.ds(pl.multiple_of(h * HEAD_DIM, HEAD_DIM), HEAD_DIM)
            vrows = pl.ds(pl.multiple_of(feats + h * HEAD_DIM, HEAD_DIM), HEAD_DIM)
            cols = pl.ds(pl.multiple_of(c * PCH, PCH), PCH)
            s = scores(source[rows, :], load_q(h, c))
            key = lax.broadcasted_iota(jnp.int32, (PCH, 1), 0)
            s = s + jnp.where(key < limit, 0.0, big_negative)
            m_old = m_sc[h, :, cols]
            m = jnp.maximum(m_old, jnp.max(s, axis=0, keepdims=True))
            p = jnp.exp(s - m)
            alpha = jnp.exp(m_old - m)
            m_sc[h, :, cols] = m
            l_sc[h, :, cols] = l_sc[h, :, cols] * alpha + jnp.sum(p, axis=0, keepdims=True)
            acc[rows, cols] = acc[rows, cols] * alpha + jnp.dot(source[vrows, :], p.astype(BF16), preferred_element_type=F32)
            return carry
        lax.fori_loop(0, heads, body, 0)

    full(own, 1, z)

    def step_body(step, carry):
        @pl.when(z >= step)
        def _():
            hop(own, z - step, step - 1, z, up_send, up_recv).wait_recv()
            @pl.when(has_up & (step < n - 1))
            def _(): hop(kv_all.at[z - step], z - step, step, z + 1, up_send, up_recv).start()
        @pl.when(z + step < n)
        def _():
            hop(own, z + step, step - 1, z, down_send, down_recv).wait_recv()
            @pl.when(has_down & (step < n - 1))
            def _(): hop(kv_all.at[z + step], z + step, step, z - 1, down_send, down_recv).start()
        @pl.when(z >= step)
        def _():
            def both(c, carry):
                full(kv_all.at[z - step], c, z - step)
                return carry
            lax.fori_loop(0, 2, both, 0)
        @pl.when(z + step < n)
        def _(): full(kv_all.at[z + step], 1, z + step)
        return carry
    lax.fori_loop(1, n, step_body, 0)

    for h in range(heads):
        rows = slice(h * HEAD_DIM, (h + 1) * HEAD_DIM)
        total = l_sc[h]
        out = acc[rows, :] / total
        of_ref[rows, :] = out
        o_ref[rows, :] = out.astype(BF16)
        lse_ref[h:h + 1, :] = m_sc[h] + jnp.log(total)

    for step in range(n - 1):
        @pl.when(has_up & (z >= step))
        def _(): hop(own, z, step, z + 1, up_send, up_recv).wait_send()
        @pl.when(has_down & (z + step < n))
        def _(): hop(own, z, step, z - 1, down_send, down_recv).wait_send()

def attend_forward(n, q, kv, branch):
    feats, rows = q.shape
    heads = feats // HEAD_DIM
    vm = pl.BlockSpec(memory_space=pltpu.VMEM)
    return pl.pallas_call(
        functools.partial(forward_kernel, n, heads),
        out_shape=(jax.ShapeDtypeStruct((feats, rows), BF16), jax.ShapeDtypeStruct((feats, rows), F32), jax.ShapeDtypeStruct((heads, rows), F32), jax.ShapeDtypeStruct((n, 2 * feats, PCH), BF16)),
        in_specs=[vm, vm, pl.BlockSpec(memory_space=pltpu.SMEM)],
        out_specs=(vm, vm, vm, vm),
        scratch_shapes=[
            pltpu.VMEM((heads, 1, rows), F32),
            pltpu.VMEM((heads, 1, rows), F32),
            pltpu.VMEM((feats, rows), F32),
            pltpu.SemaphoreType.DMA((n - 1,)), pltpu.SemaphoreType.DMA((n - 1,)),
            pltpu.SemaphoreType.DMA((n - 1,)), pltpu.SemaphoreType.DMA((n - 1,)),
        ],
        compiler_params=pltpu.CompilerParams(collective_id=1, has_side_effects=True, vmem_limit_bytes=40 * 2**20),
        cost_estimate=pl.CostEstimate(flops=4 * 10**10, bytes_accessed=10**7, transcendentals=0),
        name="attend_forward",
    )(q, kv, branch)


def flip(index, bit):
    return index + bit * (1 - 2 * lax.rem(lax.div(index, bit), 2))


def log_bits(size):
    return [1 << k for k in range(size.bit_length() - 1)]


def finish_kernel(
    n, dp_count, heads, layer_scale,
    q_ref, kv_ref, all_ref, branch_ref, do_ref, of_ref, lse_ref, far_ref, con_ref,
    near_any, exp_any, proj_any, early_any, esum_any, wa_any, normed_any, tok_any, ghid_any, gain_any,
    lout_ref, gtok_ref, con_out, exp_out, proj_out, query_out, keyval_out, sums_ref,
    dq_acc, own_acc, far_acc, lse_sc, dot_sc, up_out, up_in, down_out, down_in,
    near_ref, exp_ref, proj_ref, early_ref, esum_ref, wa_ref, normed_ref, tok_ref, ghid_ref, gain_ref,
    stacked, mix, xhat_sc, inv_sc, query_sc, keyval_sc,
    con_xo, con_xi, con_acc, con_zo, con_zi,
    exp_xo, exp_xi, exp_acc, exp_zo, exp_zi,
    proj_xo, proj_xi, proj_acc, proj_zo, proj_zi,
    query_xo, query_xi, query_acc, query_zo, query_zi,
    keyval_xo, keyval_xi, keyval_acc, keyval_zo, keyval_zi,
    core_out, core_in, y_out, y_in, far_in, seq_in, tensor_in, dp_out, dp_in,
    up_send, up_recv, down_send, down_recv, x_send, x_recv, z_send, z_recv,
    core_send, core_recv, y_send, y_recv, seq_send, seq_recv, tensor_send, tensor_recv, dp_send, dp_recv,
    fetch_sem,
):
    z = lax.axis_index("seq")
    t = lax.axis_index("tensor")
    dp = lax.axis_index("dp")
    feats = heads * HEAD_DIM
    share = ghid_ref.shape[0]
    has_up, has_down = z < n - 1, z > 0
    dp_bits = log_bits(dp_count)
    bits = len(dp_bits)
    blocks = dp_count * n
    mesh_ids = pl.DeviceIdType.MESH

    fetches = [
        pltpu.make_async_copy(src, dst, fetch_sem.at[i])
        for i, (src, dst) in enumerate(
            [
                (proj_any, proj_ref), (exp_any, exp_ref), (normed_any, normed_ref), (tok_any, tok_ref),
                (wa_any, wa_ref), (near_any, near_ref), (ghid_any, ghid_ref), (early_any, early_ref),
                (esum_any, esum_ref), (gain_any, gain_ref),
            ]
        )
    ]
    for one in fetches:
        one.start()

    barrier = pltpu.get_barrier_semaphore()
    seq_peers = [{"seq": lax.rem(z + d, n)} for d in range(1, n)]
    tensor_peers = [{"tensor": lax.rem(t + d, 4)} for d in range(1, 4)]
    dp_peers = [{"dp": flip(dp, bit)} for bit in dp_bits]
    for peer in seq_peers + tensor_peers + dp_peers:
        pl.semaphore_signal(barrier, inc=1, device_id=peer, device_id_type=mesh_ids)
    pl.semaphore_wait(barrier, n + 2 + bits)

    def remote(src, dst, send, recv, to):
        return pltpu.make_async_remote_copy(
            src_ref=src, dst_ref=dst, send_sem=send, recv_sem=recv, device_id=to, device_id_type=mesh_ids
        )

    class Scatter:
        def __init__(self, number, first, source, xo, xi, acc, zo, zi, out):
            self.number, self.first, self.source, self.xo, self.xi = number, first, source, xo, xi
            self.acc, self.zo, self.zi, self.out = acc, zo, zi, out

        def mine(self, s):
            return lax.rem(lax.div(dp, dp_count >> (s + 1)), 2)

        def start_of(self, s):
            return (blocks >> self.first) - (blocks >> s)

        def held(self, s):
            return self.source if s == self.first else self.acc

        def x_copy(self, s, j=None):
            half, start = blocks >> (s + 1), self.start_of(s)
            sem = self.number * (bits - 1 + n) + (n + s if j is None else j)
            part = pl.ds(start, half) if j is None else start + j
            return remote(
                self.xo.at[part], self.xi.at[part], x_send.at[sem], x_recv.at[sem],
                {"dp": flip(dp, dp_count >> (s + 1))},
            )

        def x_begin(self, s):
            half, start, held = blocks >> (s + 1), self.start_of(s), self.held(s)
            other = (1 - self.mine(s)) * half
            if s == bits - 1:
                for d in range(n):
                    j = lax.rem(z + 1 + d, n)
                    self.xo[start + j] = held[other + j].astype(BF16)
                    self.x_copy(s, j).start()
                return

            def body(j, carry):
                self.xo[start + j] = held[other + j].astype(BF16)
                return carry

            lax.fori_loop(0, half, body, 0)
            self.x_copy(s).start()

        def relay(self):
            for s in range(self.first, bits - 1):
                half, start, held = blocks >> (s + 1), self.start_of(s), self.held(s)
                own = self.mine(s) * half
                self.x_copy(s).wait_recv()

                def body(j, carry):
                    self.acc[j] = held[own + j] + self.xi[start + j].astype(F32)
                    return carry

                lax.fori_loop(0, half, body, 0)
                self.x_begin(s + 1)
            s = bits - 1
            done = self.first == bits
            for d in range(n):
                j = lax.rem(z + 1 + d, n)
                if done:
                    value = self.source[j]
                else:
                    self.x_copy(s, j).wait_recv()
                    own = self.mine(s) * n
                    value = self.held(s)[own + j] + self.xi[self.start_of(s) + j].astype(F32)
                if d < n - 1:
                    self.zo[j] = value.astype(BF16)
                    self.z_copy(j, z).start()
                else:
                    self.out[...] = value

        def z_copy(self, target, sender):
            base = self.number * n
            return remote(
                self.zo.at[target], self.zi.at[sender], z_send.at[base + target], z_recv.at[base + sender],
                {"seq": target},
            )

        def z_end(self):
            for d in range(1, n):
                i = lax.rem(z + d, n)
                self.z_copy(i, i).wait_recv()
                self.out[...] += self.zi[i].astype(F32)

        def drain(self):
            for s in range(self.first, bits - 1):
                self.x_copy(s).wait_send()
            for j in range(n):
                if self.first < bits:
                    self.x_copy(bits - 1, j).wait_send()
            for d in range(1, n):
                self.z_copy(lax.rem(z + d, n), z).wait_send()

    contract = Scatter(0, 1, con_ref, con_xo, con_xi, con_acc, con_zo, con_zi, con_out)
    expand = Scatter(1, 1, exp_ref, exp_xo, exp_xi, exp_acc, exp_zo, exp_zi, exp_out)
    project = Scatter(2, 0, proj_ref, proj_xo, proj_xi, proj_acc, proj_zo, proj_zi, proj_out)
    query = Scatter(3, 0, query_sc, query_xo, query_xi, query_acc, query_zo, query_zi, query_out)
    keyval = Scatter(4, 0, keyval_sc, keyval_xo, keyval_xi, keyval_acc, keyval_zo, keyval_zi, keyval_out)
    scatters = (contract, expand, project, query, keyval)

    sibling, partner = {"tensor": flip(t, 1)}, {"tensor": flip(t, 2)}
    far_copy = remote(far_ref, far_in, y_send.at[0], y_recv.at[0], partner)
    far_copy.start()
    if contract.first < bits:
        contract.x_begin(contract.first)
    contract.relay()
    fetches[0].wait()
    project.x_begin(0)
    if expand.first < bits:
        fetches[1].wait()
        expand.x_begin(expand.first)

    def hop(out, inn, d, to, send, recv):
        return remote(out.at[d], inn.at[d], send.at[d], recv.at[d], {"seq": to})

    dq_acc[...] = jnp.zeros_like(dq_acc)
    for h in range(heads):
        rows = slice(h * HEAD_DIM, (h + 1) * HEAD_DIM)
        lse_sc[h] = lse_ref[h:h + 1, :]
        dot_sc[h] = jnp.sum(do_ref[rows, :].astype(F32) * of_ref[rows, :], axis=0, keepdims=True)

    nt = (((1,), (1,)), ((), ()))
    tn = (((0,), (0,)), ((), ()))
    tt = (((0,), (1,)), ((), ()))

    def tile(h, cols, k, v, mask):
        rows = pl.ds(pl.multiple_of(h * HEAD_DIM, HEAD_DIM), HEAD_DIM)
        q, do = q_ref[rows, cols], do_ref[rows, cols]
        s = mask(lax.dot_general(k, q, tn, preferred_element_type=F32))
        p = jnp.exp(s - lse_sc[h, :, cols])
        dp = lax.dot_general(v, do, tn, preferred_element_type=F32)
        ds = (p * (dp - dot_sc[h, :, cols])).astype(BF16)
        p = p.astype(BF16)
        dv = lax.dot_general(do, p, nt, preferred_element_type=F32)
        dk = lax.dot_general(q, ds, nt, preferred_element_type=F32)
        dq_acc[rows, cols] += jnp.dot(k, ds, preferred_element_type=F32)
        return dk, dv

    def head_rows(h):
        return (pl.ds(pl.multiple_of(h * HEAD_DIM, HEAD_DIM), HEAD_DIM),
                pl.ds(pl.multiple_of(feats + h * HEAD_DIM, HEAD_DIM), HEAD_DIM))

    def columns(c):
        return pl.ds(pl.multiple_of(c * PCH, PCH), PCH)

    branch = branch_ref[0, 0]

    def full(source, c, block, total):
        limit = jnp.where(c == 0, n * PCH, branch) - block * PCH
        def mask(s):
            key = lax.broadcasted_iota(jnp.int32, (PCH, 1), 0)
            return s + jnp.where(key < limit, 0.0, big_negative)
        def body(h, carry):
            rows, vrows = head_rows(h)
            dk, dv = tile(h, columns(c), source[rows, :], source[vrows, :], mask)
            total[rows, :] += dk
            total[vrows, :] += dv
            return carry
        lax.fori_loop(0, heads, body, 0)

    def diag(i, carry):
        c, h = i // heads, i % heads
        rows, vrows = head_rows(h)
        cols = columns(c)
        def mask(s):
            key = lax.broadcasted_iota(jnp.int32, s.shape, 0)
            query = lax.broadcasted_iota(jnp.int32, s.shape, 1)
            return jnp.where(key <= query, s, big_negative)
        dk, dv = tile(h, cols, kv_ref[rows, cols], kv_ref[vrows, cols], mask)
        own_acc[rows, cols] = dk
        own_acc[vrows, cols] = dv
        return carry

    own_step = jnp.where(has_up & has_down, 0, n - 1)

    def step_body(step, carry):
        d = n - 1 - step

        @pl.when(step == own_step)
        def _():
            lax.fori_loop(0, 2 * heads, diag, 0)
            full(kv_ref.at[:, 0:PCH], 1, z, own_acc.at[:, 0:PCH])

        @pl.when((d >= 1) & (z + d < n))
        def _():
            far_acc[...] = jnp.zeros_like(far_acc)
            full(all_ref.at[z + d], 1, z + d, far_acc)
            @pl.when(has_down & (d < n - 1))
            def _():
                hop(up_out, up_in, d, z, up_send, up_recv).wait_recv()
                far_acc[...] += up_in[d].astype(F32)
            up_out[d - 1] = far_acc[...].astype(BF16)
            hop(up_out, up_in, d - 1, z + 1, up_send, up_recv).start()

        @pl.when((d >= 1) & (z >= d))
        def _():
            far_acc[...] = jnp.zeros_like(far_acc)
            def both(c, carry):
                full(all_ref.at[z - d], c, z - d, far_acc)
                return carry
            lax.fori_loop(0, 2, both, 0)
            @pl.when(has_up & (d < n - 1))
            def _():
                hop(down_out, down_in, d, z, down_send, down_recv).wait_recv()
                far_acc[...] += down_in[d].astype(F32)
            down_out[d - 1] = far_acc[...].astype(BF16)
            hop(down_out, down_in, d - 1, z - 1, down_send, down_recv).start()

        @pl.when(step == n - 2)
        def _():
            if expand.first == bits:
                fetches[1].wait()
            expand.relay()
            project.relay()
        return carry
    lax.fori_loop(0, n, step_body, 0)

    def place(k):
        owner = t
        for bit in (1, 2):
            turned = flip(owner, bit)
            if isinstance(k, int):
                owner = turned if k & bit else owner
            else:
                owner = jnp.where(lax.rem(lax.div(k, bit), 2) == 1, turned, owner)
        return pl.ds(pl.multiple_of(owner * share, share), share)

    rows = query_sc.shape[1]

    def weight_gradient(part, target):
        value = jnp.dot(part, normed_ref[...], preferred_element_type=F32).T
        for b in range(blocks):
            target[b] = value[b * rows : (b + 1) * rows, :]

    stacked[0:feats, :] = (dq_acc[...] * (1.0 / math.sqrt(HEAD_DIM))).astype(BF16)
    for one in fetches[2:]:
        one.wait()
    weight_gradient(stacked[0:feats, :], query_sc)
    query.x_begin(0)
    stacked[feats:, PCH:] = own_acc[:, PCH:].astype(BF16)

    def prepare(k, carry):
        value = tok_ref[place(k), :].astype(F32)
        centred = value - jnp.mean(value, axis=-1, keepdims=True)
        inverse = lax.rsqrt(jnp.mean(centred * centred, axis=-1, keepdims=True) + norm_eps)
        xhat_sc[k] = centred * inverse
        inv_sc[k] = jnp.broadcast_to(inverse, (share, 128))
        return carry

    lax.fori_loop(0, 4, prepare, 0)

    @pl.when(has_down)
    def _():
        hop(up_out, up_in, 0, z, up_send, up_recv).wait_recv()
        own_acc[:, 0:PCH] += up_in[0].astype(F32)
    @pl.when(has_up)
    def _():
        hop(down_out, down_in, 0, z, down_send, down_recv).wait_recv()
        own_acc[:, 0:PCH] += down_in[0].astype(F32)
    stacked[feats:, 0:PCH] = own_acc[:, 0:PCH].astype(BF16)

    weight_gradient(stacked[feats:, :], keyval_sc)
    keyval.x_begin(0)

    def grad_normed(k):
        total = None
        for c in range(3):
            term = lax.dot_general(
                stacked[c * feats : (c + 1) * feats, place(k)], wa_ref[c], tt, preferred_element_type=F32
            )
            total = term if total is None else total + term
        mix[k] = total
        return total

    def core_copy(i):
        return remote(core_out.at[i], core_in.at[i], core_send.at[i], core_recv.at[i], sibling)

    core_out[0] = grad_normed(3).astype(BF16)
    core_copy(0).start()
    last = grad_normed(2)
    core_copy(0).wait_recv()
    y_out[...] = (last + core_in[0].astype(F32)).astype(BF16)
    y_copy = remote(y_out, y_in, y_send.at[1], y_recv.at[1], partner)
    y_copy.start()
    core_out[1] = grad_normed(1).astype(BF16)
    core_copy(1).start()
    query.relay()
    grad_normed(0)

    width = seq_in.shape[2]
    seq_in[z, 0:2, :] = jnp.zeros((2, width), F32)
    seq_in[z, 2:6, :] = early_ref[...]
    seq_in[z, 6:7, :] = esum_ref[...]
    seq_in[z, 7:8, :] = jnp.zeros((1, width), F32)
    ones = jnp.ones((8, stacked.shape[1]), BF16)
    seq_in[z, 7:8, 0 : 3 * feats] = lax.dot_general(ones, stacked[...], nt, preferred_element_type=F32)[0:1]

    def statistics(k, carry):
        seq_in[z, 0:1, :] += jnp.sum(mix[k] * xhat_sc[k], axis=0, keepdims=True)
        seq_in[z, 1:2, :] += jnp.sum(mix[k], axis=0, keepdims=True)
        return carry

    lax.fori_loop(0, 4, statistics, 0)

    def seq_copy(target, sender):
        return remote(seq_in.at[z], seq_in.at[sender], seq_send.at[target], seq_recv.at[sender], {"seq": target})

    def tensor_copy(target, sender):
        return remote(
            tensor_in.at[t], tensor_in.at[sender], tensor_send.at[target], tensor_recv.at[sender],
            {"tensor": target},
        )

    def dp_copy(i):
        return remote(dp_out.at[i], dp_in.at[i], dp_send.at[i], dp_recv.at[i], dp_peers[i])

    for d in range(1, n):
        seq_copy(lax.rem(z + d, n), z).start()
    keyval.relay()
    far_copy.wait_recv()
    lout_ref[...] = (near_ref[...] + layer_scale * far_in[...].astype(F32)).astype(BF16)
    for d in range(1, n):
        other = lax.rem(z + d, n)
        seq_copy(other, other).wait_recv()
    summed = seq_in[0]
    for i in range(1, n):
        summed = summed + seq_in[i]
    tensor_in[t] = summed
    for d in range(1, 4):
        tensor_copy(lax.rem(t + d, 4), t).start()
    contract.z_end()
    for d in range(1, 4):
        other = lax.rem(t + d, 4)
        tensor_copy(other, other).wait_recv()
    total = tensor_in[0]
    for i in range(1, 4):
        total = total + tensor_in[i]
    own = tensor_in[t]
    row = lax.broadcasted_iota(jnp.int32, own.shape, 0)
    dp_out[0] = jnp.where(row < 6, total, own)
    dp_copy(0).start()
    expand.z_end()
    project.z_end()

    core_copy(1).wait_recv()
    y_copy.wait_recv()
    mixed = mix[0] + core_in[1].astype(F32) + y_in[...].astype(F32)
    e = mixed * gain_ref[0:1, :]
    xhat = xhat_sc[0]
    gtok_ref[...] = (
        ghid_ref[...]
        + inv_sc[0][:, 0:1]
        * (e - jnp.mean(e, axis=-1, keepdims=True) - xhat * jnp.mean(e * xhat, axis=-1, keepdims=True))
    ).astype(BF16)
    query.z_end()
    for i in range(bits):
        dp_copy(i).wait_recv()
        value = dp_out[i] + dp_in[i]
        if i + 1 < bits:
            dp_out[i + 1] = value
            dp_copy(i + 1).start()
        else:
            sums_ref[...] = value
    keyval.z_end()

    for d in range(1, n):
        @pl.when(z + d < n)
        def _(): hop(up_out, up_in, d - 1, z + 1, up_send, up_recv).wait_send()
        @pl.when(z >= d)
        def _(): hop(down_out, down_in, d - 1, z - 1, down_send, down_recv).wait_send()
    for one in scatters:
        one.drain()
    far_copy.wait_send()
    y_copy.wait_send()
    for i in range(2):
        core_copy(i).wait_send()
    for d in range(1, n):
        seq_copy(lax.rem(z + d, n), z).wait_send()
    for d in range(1, 4):
        tensor_copy(lax.rem(t + d, 4), t).wait_send()
    for i in range(bits):
        dp_copy(i).wait_send()


def finish(
    n, dp_count, layer_scale, q, kv, kv_all, branch, do, of, lse, near, far,
    grad_contract, grad_expand, grad_proj, early, expand_terms, w_attn, normed_one, token_rows,
    grad_hidden, norm_gains,
):
    feats, rows = q.shape
    heads = feats // HEAD_DIM
    share, width = grad_hidden.shape
    blocks = dp_count * n
    bits = len(log_bits(dp_count))
    vm = pl.BlockSpec(memory_space=pltpu.VMEM)
    anywhere = pl.BlockSpec(memory_space=pl.ANY)
    slots = pltpu.VMEM((n - 1, 2 * feats, PCH), BF16)
    shape = jax.ShapeDtypeStruct
    sems = lambda count: pltpu.SemaphoreType.DMA((count,))
    block_rows = width // blocks
    proj_blocks = grad_proj.reshape(blocks, block_rows, feats)
    units = grad_contract.shape[2]
    fetched = [
        near, grad_expand, proj_blocks, early, expand_terms, w_attn, normed_one, token_rows,
        grad_hidden, norm_gains,
    ]
    widths = [(1, units), (1, units), (0, feats), (0, feats), (0, 2 * feats)]
    scatter_scratch = []
    for first, columns in widths:
        through = max((blocks >> first) - n, 1)
        kept = blocks >> (first + 1) if bits - first > 1 else 1
        scatter_scratch += [
            pltpu.VMEM((through, block_rows, columns), BF16),
            pltpu.VMEM((through, block_rows, columns), BF16),
            pltpu.VMEM((kept, block_rows, columns), F32),
            pltpu.VMEM((n, block_rows, columns), BF16),
            pltpu.VMEM((n, block_rows, columns), BF16),
        ]
    return pl.pallas_call(
        functools.partial(finish_kernel, n, dp_count, heads, layer_scale),
        out_shape=(
            shape((share, width), BF16),
            shape((share, width), BF16),
            *(shape((block_rows, columns), F32) for _, columns in widths),
            shape((8, width), F32),
        ),
        in_specs=[vm, vm, vm, pl.BlockSpec(memory_space=pltpu.SMEM)] + [vm] * 5 + [anywhere] * len(fetched),
        out_specs=(vm,) * 8,
        scratch_shapes=[
            pltpu.VMEM((feats, rows), F32),
            pltpu.VMEM((2 * feats, rows), F32),
            pltpu.VMEM((2 * feats, PCH), F32),
            pltpu.VMEM((heads, 1, rows), F32),
            pltpu.VMEM((heads, 1, rows), F32),
            slots, slots, slots, slots,
            *(pltpu.VMEM(one.shape, one.dtype) for one in fetched),
            pltpu.VMEM((3 * feats, rows), BF16),
            pltpu.VMEM((4, share, width), F32),
            pltpu.VMEM((4, share, width), F32),
            pltpu.VMEM((4, share, 128), F32),
            pltpu.VMEM((blocks, block_rows, feats), F32),
            pltpu.VMEM((blocks, block_rows, 2 * feats), F32),
            *scatter_scratch,
            pltpu.VMEM((2, share, width), BF16),
            pltpu.VMEM((2, share, width), BF16),
            pltpu.VMEM((share, width), BF16),
            pltpu.VMEM((share, width), BF16),
            pltpu.VMEM((share, width), BF16),
            pltpu.VMEM((n, 8, width), F32),
            pltpu.VMEM((4, 8, width), F32),
            pltpu.VMEM((bits, 8, width), F32),
            pltpu.VMEM((bits, 8, width), F32),
            sems(n - 1), sems(n - 1), sems(n - 1), sems(n - 1),
            sems(5 * (bits - 1 + n)), sems(5 * (bits - 1 + n)), sems(5 * n), sems(5 * n),
            sems(2), sems(2), sems(2), sems(2), sems(n), sems(n), sems(4), sems(4), sems(bits), sems(bits),
            sems(len(fetched)),
        ],
        compiler_params=pltpu.CompilerParams(
            collective_id=2, has_side_effects=True, vmem_limit_bytes=60 * 2**20
        ),
        cost_estimate=pl.CostEstimate(flops=4 * 10**10, bytes_accessed=10**7, transcendentals=0),
        name="finish",
    )(q, kv, kv_all, branch, do, of, lse, far, grad_contract, *fetched)


def emit_kernel(
    feats, turned, lout, gtok, con, expand, proj, query, keyval, sums,
    lout_ref, gtok_ref, attn_ref, proj_ref, exp_ref, con_ref, bias_ref, branch_ref, units_ref, gains_ref, shifts_ref,
):
    lout_ref[...] = lout[...]
    gtok_ref[...] = gtok[...]
    attn_ref[0] = query[...]
    attn_ref[1] = keyval[:, 0:feats]
    attn_ref[2] = keyval[:, feats : 2 * feats]
    proj_ref[...] = proj[...].T if turned else proj[...]
    exp_ref[...] = expand[...]
    con_ref[...] = con[...]
    bias_ref[0:1, :] = sums[7:8, 0:feats]
    bias_ref[1:2, :] = sums[7:8, 2 * feats : 3 * feats]
    branch_ref[...] = sums[2:4, :]
    units_ref[...] = sums[6:7, :]
    for row, late, early in ((gains_ref, 0, 4), (shifts_ref, 1, 5)):
        row[0:1, :] = sums[late : late + 1, :]
        row[1:2, :] = sums[early : early + 1, :]


def emit(results):
    lout, gtok, con, expand, proj, query, keyval, sums = results
    rows, feats = query.shape
    share, width = lout.shape
    turned = rows % 8 == 0
    shape = jax.ShapeDtypeStruct
    vm = pl.BlockSpec(memory_space=pltpu.VMEM)
    outputs = pl.pallas_call(
        functools.partial(emit_kernel, feats, turned),
        out_shape=(
            shape((share, width), BF16), shape((share, width), BF16), shape((3, rows, feats), F32),
            shape((feats, rows) if turned else (rows, feats), F32), shape(expand.shape, F32),
            shape(con.shape, F32), shape((2, feats), F32), shape((2, width), F32),
            shape((1, expand.shape[1]), F32), shape((2, width), F32), shape((2, width), F32),
        ),
        in_specs=[vm] * 8,
        out_specs=(vm,) * 11,
        compiler_params=pltpu.CompilerParams(vmem_limit_bytes=16 * 2**20),
        name="emit",
    )(*results)
    lout, gtok, attn, proj, expand, con, bias, branch, units, gains, shifts = outputs
    whole = (1, 1, share, width)
    return (
        lout.reshape(whole), gtok.reshape(whole), attn, proj if turned else proj.T, expand, con.T,
        bias, branch, units.reshape(-1), gains, shifts,
    )


def middle_kernel(
    n, dp_count, layer_scale, o_ref, tok_ref, cot_ref, wp_ref, we_ref, wc_ref, bb_ref, eb_ref, gain_ref, shift_ref,
    ghid_ref, near_ref, far_ref, gatt_ref, gproj_ref, gexp_ref, gcon_ref, sums_ref, esum_ref,
    ga_sc, mix_sc, n2, gm, act, gp, att, own_sc, xhat_sc, inv_sc, proj_sc,
    core_out, core_in, y_out, y_in, con_sc, exp_sc, con_out, con_in, exp_out, exp_in,
    core_send, core_recv, y_send, y_recv, n2_send, n2_recv, att_send, att_recv, x_send, x_recv,
):
    t = lax.axis_index("tensor")
    dp = lax.axis_index("dp")
    y, c = t // 2, t % 2
    sibling = y * 2 + (1 - c)
    partner = (1 - y) * 2 + c
    share = own_sc.shape[0]

    def block(k):
        if isinstance(k, int):
            return ((1 - y) if k >= 2 else y) * 2 + ((1 - c) if k % 2 else c)
        return jnp.where(k >= 2, 1 - y, y) * 2 + jnp.where(k % 2 == 1, 1 - c, c)

    def place(k):
        return pl.ds(pl.multiple_of(block(k) * share, share), share)

    barrier = pltpu.get_barrier_semaphore()
    for to in (sibling, partner):
        pl.semaphore_signal(barrier, inc=1, device_id={"tensor": to}, device_id_type=pl.DeviceIdType.MESH)
    step = dp_count // 2
    across_dp = {"dp": flip(dp, step)}
    pl.semaphore_signal(barrier, inc=1, device_id=across_dp, device_id_type=pl.DeviceIdType.MESH)
    pl.semaphore_wait(barrier, 3)

    blocks = dp_count * n
    half = blocks // 2
    mine = lax.div(dp, step)

    def halves(i):
        out, into = ((con_out, con_in), (exp_out, exp_in))[i]
        return pltpu.make_async_remote_copy(
            src_ref=out, dst_ref=into, send_sem=x_send.at[i], recv_sem=x_recv.at[i],
            device_id=across_dp, device_id_type=pl.DeviceIdType.MESH,
        )

    def send_half(i, value):
        held, out = ((con_sc, con_out), (exp_sc, exp_out))[i]
        size = held.shape[1]
        for b in range(blocks):
            held[b] = value[b * size : (b + 1) * size, :]

        def body(j, carry):
            out[j] = held[(1 - mine) * half + j].astype(BF16)
            return carry

        lax.fori_loop(0, half, body, 0)
        halves(i).start()

    def take_half(i, result):
        held, into = ((con_sc, con_in), (exp_sc, exp_in))[i]
        halves(i).wait_recv()

        def body(j, carry):
            result[j] = held[mine * half + j] + into[j].astype(F32)
            return carry

        lax.fori_loop(0, half, body, 0)

    def copy(src, dst, send, recv, to):
        return pltpu.make_async_remote_copy(
            src_ref=src, dst_ref=dst, send_sem=send, recv_sem=recv,
            device_id={"tensor": to}, device_id_type=pl.DeviceIdType.MESH,
        )

    def core_copy(i):
        return copy(core_out.at[i], core_in.at[i], core_send.at[i], core_recv.at[i], sibling)

    def y_copy(i):
        return copy(y_out.at[i], y_in.at[i], y_send.at[i], y_recv.at[i], partner)

    def gather(ref, send, recv):
        return (
            copy(ref.at[0], ref.at[2], send.at[0], recv.at[0], partner),
            copy(ref.at[0], ref.at[1], send.at[1], recv.at[1], sibling),
            copy(ref.at[2], ref.at[3], send.at[2], recv.at[2], sibling),
        )

    tn = (((0,), (0,)), ((), ()))
    nt = (((1,), (1,)), ((), ()))

    def project(k):
        return lax.dot_general(o_ref[:, place(k)], wp_ref[...], tn, preferred_element_type=F32)

    core_out[0] = project(3).astype(BF16)
    core_copy(0).start()
    own_sc[...] = project(2)
    core_out[1] = project(1).astype(BF16)
    core_copy(1).start()
    core_copy(0).wait_recv()
    y_out[0] = (own_sc[...] + core_in[0].astype(F32)).astype(BF16)
    y_copy(0).start()
    own_sc[...] = project(0)

    def before(k, carry):
        g = (cot_ref[place(k), :].astype(F32) * layer_scale).astype(BF16)
        gm[k] = g
        ga_sc[k] = lax.dot_general(g, wc_ref[...], nt, preferred_element_type=F32)
        return carry

    lax.fori_loop(0, 4, before, 0)
    core_copy(1).wait_recv()
    own_sc[...] += core_in[1].astype(F32)
    y_copy(0).wait_recv()

    hidden = tok_ref[place(0), :].astype(F32) + layer_scale * (
        own_sc[...] + y_in[0].astype(F32) + bb_ref[0:1, :]
    )
    near_ref[...] = hidden + layer_scale * bb_ref[1:2, :]
    centred = hidden - jnp.mean(hidden, axis=-1, keepdims=True)
    inverse = lax.rsqrt(jnp.mean(centred * centred, axis=-1, keepdims=True) + norm_eps)
    xhat = centred * inverse
    n2[0] = (xhat * gain_ref[1:2, :] + shift_ref[1:2, :]).astype(BF16)
    across, near, on = gather(n2, n2_send, n2_recv)
    across.start()
    near.start()
    xhat_sc[...] = xhat
    inv_sc[...] = jnp.broadcast_to(inverse, inv_sc.shape)
    esum_ref[...] = jnp.zeros_like(esum_ref)

    def process(k, carry):
        @pl.when(k == 1)
        def _():
            near.wait_recv()

        @pl.when(k == 2)
        def _():
            across.wait_recv()
            on.start()

        @pl.when(k == 3)
        def _():
            on.wait_recv()

        v = jnp.dot(n2[k], we_ref[...], preferred_element_type=F32) + eb_ref[...]
        square = v * v
        th = jnp.tanh(math.sqrt(2.0 / math.pi) * (v + 0.044715 * (v * square)))
        cdf = 0.5 * (1.0 + th)
        act[k] = (v * cdf).astype(BF16)
        slope = cdf + 0.5 * v * (1.0 - th * th) * (
            math.sqrt(2.0 / math.pi) * (1.0 + 3 * 0.044715 * square)
        )
        g = (slope * ga_sc[k]).astype(BF16)
        gp[k] = g
        esum_ref[...] += jnp.sum(g.astype(F32), axis=0, keepdims=True)
        mix_sc[k] = lax.dot_general(g, we_ref[...], nt, preferred_element_type=F32)
        return carry

    lax.fori_loop(0, 4, process, 0)
    core_out[2] = mix_sc[3].astype(BF16)
    core_copy(2).start()
    core_out[3] = mix_sc[1].astype(BF16)
    core_copy(3).start()
    core_copy(2).wait_recv()
    y_out[1] = (mix_sc[2] + core_in[2].astype(F32)).astype(BF16)
    y_copy(1).start()

    rows = 4 * share
    width = gm.shape[2]
    send_half(0, lax.dot_general(
        gm[...].reshape(rows, width), act[...].reshape(rows, -1), tn, preferred_element_type=F32
    ))
    send_half(1, lax.dot_general(
        n2[...].reshape(rows, width), gp[...].reshape(rows, -1), tn, preferred_element_type=F32
    ))

    def contract(k):
        return jnp.dot(act[k], wc_ref[...], preferred_element_type=F32)

    core_out[4] = contract(3).astype(BF16)
    core_copy(4).start()
    core_out[5] = contract(1).astype(BF16)
    core_copy(5).start()
    near_ref[...] += layer_scale * contract(0)
    last = contract(2)
    core_copy(4).wait_recv()
    far_ref[...] = (last + core_in[4].astype(F32)).astype(BF16)
    core_copy(5).wait_recv()
    near_ref[...] += layer_scale * core_in[5].astype(F32)

    core_copy(3).wait_recv()
    mixed = mix_sc[0] + core_in[3].astype(F32)
    y_copy(1).wait_recv()
    mixed = mixed + y_in[1].astype(F32)
    e = mixed * gain_ref[1:2, :]
    xhat = xhat_sc[...]
    grad_hidden = cot_ref[place(0), :].astype(F32) + inv_sc[:, 0:1] * (
        e - jnp.mean(e, axis=-1, keepdims=True) - xhat * jnp.mean(e * xhat, axis=-1, keepdims=True)
    )
    g = (grad_hidden * layer_scale).astype(BF16)
    att[0] = g
    across_b, near_b, on_b = gather(att, att_send, att_recv)
    across_b.start()
    near_b.start()
    ghid_ref[...] = grad_hidden
    sums_ref[0:1, :] = jnp.sum(g.astype(F32), axis=0, keepdims=True)
    sums_ref[1:2, :] = jnp.sum(gm[0].astype(F32), axis=0, keepdims=True)
    sums_ref[2:3, :] = jnp.sum(mixed * xhat, axis=0, keepdims=True)
    sums_ref[3:4, :] = jnp.sum(mixed, axis=0, keepdims=True)

    proj_sc[...] = jnp.zeros_like(proj_sc)

    def after(k, carry):
        @pl.when(k == 1)
        def _():
            near_b.wait_recv()

        @pl.when(k == 2)
        def _():
            across_b.wait_recv()
            on_b.start()

        @pl.when(k == 3)
        def _():
            on_b.wait_recv()

        gatt_ref[:, place(k)] = lax.dot_general(
            wp_ref[...], att[k], nt, preferred_element_type=F32
        ).astype(BF16)
        proj_sc[...] += jnp.dot(o_ref[:, place(k)], att[k], preferred_element_type=F32)
        return carry

    lax.fori_loop(0, 4, after, 0)
    gproj_ref[...] = proj_sc[...].T
    take_half(0, gcon_ref)
    take_half(1, gexp_ref)
    for i in range(2):
        halves(i).wait_send()
    for i in range(6):
        core_copy(i).wait_send()
    for i in range(2):
        y_copy(i).wait_send()
    for one in (across, near, on, across_b, near_b, on_b):
        one.wait_send()


def middle(
    n, dp_count, layer_scale, attended, token_rows, cotangent_rows, w_proj, w_expand, w_contract,
    branch_bias, expand_bias, norm_gains, norm_shifts,
):
    rows, width = token_rows.shape
    feats, hidden_units = w_proj.shape[0], w_expand.shape[1]
    share = rows // 4
    half, size = dp_count * n // 2, width // (dp_count * n)
    vm = pl.BlockSpec(memory_space=pltpu.VMEM)
    shape = jax.ShapeDtypeStruct
    slots = lambda columns, kind: pltpu.VMEM((4, share, columns), kind)
    sems = lambda count: pltpu.SemaphoreType.DMA((count,))
    return pl.pallas_call(
        functools.partial(middle_kernel, n, dp_count, layer_scale),
        out_shape=(
            shape((share, width), F32),
            shape((share, width), F32),
            shape((share, width), BF16),
            shape((feats, rows), BF16),
            shape((width, feats), F32),
            shape((half, size, hidden_units), F32),
            shape((half, size, hidden_units), F32),
            shape((4, width), F32),
            shape((1, hidden_units), F32),
        ),
        in_specs=[vm] * 10,
        out_specs=(vm,) * 9,
        scratch_shapes=[
            slots(hidden_units, F32),
            slots(width, F32),
            slots(width, BF16),
            slots(width, BF16),
            slots(hidden_units, BF16),
            slots(hidden_units, BF16),
            slots(width, BF16),
            pltpu.VMEM((share, width), F32),
            pltpu.VMEM((share, width), F32),
            pltpu.VMEM((share, 128), F32),
            pltpu.VMEM((feats, width), F32),
            pltpu.VMEM((6, share, width), BF16),
            pltpu.VMEM((6, share, width), BF16),
            pltpu.VMEM((2, share, width), BF16),
            pltpu.VMEM((2, share, width), BF16),
            pltpu.VMEM((2 * half, size, hidden_units), F32),
            pltpu.VMEM((2 * half, size, hidden_units), F32),
            pltpu.VMEM((half, size, hidden_units), BF16),
            pltpu.VMEM((half, size, hidden_units), BF16),
            pltpu.VMEM((half, size, hidden_units), BF16),
            pltpu.VMEM((half, size, hidden_units), BF16),
            sems(6), sems(6), sems(2), sems(2), sems(3), sems(3), sems(3), sems(3), sems(2), sems(2),
        ],
        compiler_params=pltpu.CompilerParams(
            collective_id=3, has_side_effects=True, vmem_limit_bytes=56 * 2**20
        ),
        cost_estimate=pl.CostEstimate(flops=5 * 10**10, bytes_accessed=2 * 10**7, transcendentals=0),
        name="middle",
    )(
        attended, token_rows, cotangent_rows, w_proj, w_expand, w_contract,
        branch_bias, expand_bias, norm_gains, norm_shifts,
    )


def shards(
    tokens,
    branch,
    w_attn,
    w_proj,
    w_expand,
    w_contract,
    attn_bias,
    branch_bias,
    expand_bias,
    norm_gains,
    norm_shifts,
    cotangent,
):
    seq_count = lax.axis_size("seq")
    width = tokens.shape[3]
    row_count = tokens.shape[2]
    share = row_count // lax.axis_size("tensor")
    local_width = w_attn.shape[2]
    score_scale = 1.0 / math.sqrt(HEAD_DIM)
    layer_scale = 1.0 / math.sqrt(LAYERS)

    token_rows = tokens.reshape(row_count, width)
    cotangent_rows = cotangent.reshape(row_count, width)
    flat_rows = token_rows.astype(F32)
    normed_one = (
        layer_norm_parts(flat_rows)[0] * norm_gains[0] + norm_shifts[0]
    ).astype(BF16)
    projected = jnp.einsum("cde,rd->cer", w_attn, normed_one, preferred_element_type=F32)
    bias_rows = jnp.stack([attn_bias[0], jnp.zeros_like(attn_bias[0]), attn_bias[1]])
    projected = (projected + bias_rows[:, :, None]).astype(BF16)
    queries = projected[0] * jnp.asarray(score_scale, BF16)
    own_kv = projected[1:].reshape(2 * local_width, row_count)

    attended, attended_wide, logsum, all_kv = attend_forward(seq_count, queries, own_kv, branch)
    (
        grad_hidden, mlp_near, mlp_far, grad_attended,
        grad_proj, grad_expand, grad_contract, early, expand_terms,
    ) = middle(
        seq_count, lax.axis_size("dp"), layer_scale, attended, token_rows, cotangent_rows, w_proj, w_expand, w_contract,
        branch_bias, expand_bias.reshape(1, -1), norm_gains, norm_shifts,
    )
    return emit(finish(
        seq_count, lax.axis_size("dp"), layer_scale, queries, own_kv, all_kv, branch, grad_attended,
        attended_wide, logsum, mlp_near, mlp_far, grad_contract, grad_expand, grad_proj, early,
        expand_terms, w_attn, normed_one, token_rows, grad_hidden, norm_gains,
    ))


def solution(mesh):
    placed = (
        P("dp", "seq", None, None),
        P("dp", "seq"),
        P(None, None, "tensor"),
        P("tensor", None),
        P(None, "tensor"),
        P("tensor", None),
        P(None, "tensor"),
        P(),
        P("tensor"),
        P(),
        P(),
        P("dp", "seq", None, None),
    )
    return jax.shard_map(
        shards,
        mesh=mesh,
        in_specs=placed,
        out_specs=(
            P("dp", "seq", "tensor", None),
            P("dp", "seq", "tensor", None),
            P(None, ("dp", "seq"), "tensor"),
            P("tensor", ("dp", "seq")),
            P(("dp", "seq"), "tensor"),
            P("tensor", ("dp", "seq")),
            P(None, "tensor"),
            P(),
            P("tensor"),
            P(),
            P(),
        ),
        check_vma=False,
    )
```

```python
import functools
import math

import jax
import jax.numpy as jnp
from jax import lax
from jax.experimental import pallas as pl
from jax.experimental.pallas import tpu as pltpu
from jax.sharding import PartitionSpec as P

HEAD_DIM = 64
LAYERS = 12
PCH = 512
CLEN = 512
F32 = jnp.float32
BF16 = jnp.bfloat16


norm_eps = 1e-05
big_negative = -1000000000.0


def layer_norm_parts(value):
    centre = jnp.mean(value, axis=-1, keepdims=True)
    centred = value - centre
    spread = jnp.mean(centred * centred, axis=-1, keepdims=True)
    inverse = lax.rsqrt(spread + norm_eps)
    return centred * inverse, inverse


def forward_kernel(n, heads, tok_ref, wa_ref, bias_ref, gain_ref, shift_ref, branch_ref, o_ref, of_ref, lse_ref, kv_all, q_ref, kv_ref, normed_ref, m_sc, l_sc, acc, up_send, up_recv, down_send, down_recv):
    z = lax.axis_index("seq")
    feats = heads * HEAD_DIM
    barrier = pltpu.get_barrier_semaphore()
    has_up, has_down = z < n - 1, z > 0

    def meet(to):
        pl.semaphore_signal(barrier, inc=1, device_id={"seq": to}, device_id_type=pl.DeviceIdType.MESH)

    @pl.when(has_up)
    def _(): meet(z + 1)
    @pl.when(has_down)
    def _(): meet(z - 1)

    bias = [jnp.broadcast_to(bias_ref[i : i + 1, :], (8, feats)).T[:, 0:1] for i in range(2)]

    def project(first, cols):
        normed = normed_ref[cols, :]
        value = lax.dot_general(
            wa_ref[first * feats :, :] if first else wa_ref[0:feats, :], normed,
            (((1,), (1,)), ((), ())), preferred_element_type=F32,
        )
        return value

    def norm_rows(cols):
        value = layer_norm_parts(tok_ref[cols, :].astype(F32))[0]
        normed_ref[cols, :] = (value * gain_ref[0:1, :] + shift_ref[0:1, :]).astype(BF16)

    def keys_values(cols):
        value = project(1, cols)
        kv_ref[0:feats, cols] = value[0:feats].astype(BF16)
        kv_ref[feats:, cols] = (value[feats:] + bias[1]).astype(BF16)

    prompt_cols, other_cols = slice(0, PCH), slice(PCH, q_ref.shape[1])
    norm_rows(prompt_cols)
    keys_values(prompt_cols)
    pl.semaphore_wait(barrier, has_up.astype(jnp.int32) + has_down.astype(jnp.int32))

    own = kv_ref.at[:, 0:PCH]

    def hop(src, block, step, to, send, recv):
        return pltpu.make_async_remote_copy(src_ref=src, dst_ref=kv_all.at[block], send_sem=send.at[step], recv_sem=recv.at[step], device_id={"seq": to}, device_id_type=pl.DeviceIdType.MESH)

    @pl.when(has_up)
    def _(): hop(own, z, 0, z + 1, up_send, up_recv).start()
    @pl.when(has_down)
    def _(): hop(own, z, 0, z - 1, down_send, down_recv).start()

    norm_rows(other_cols)
    keys_values(other_cols)
    for cols in (prompt_cols, other_cols):
        value = (project(0, cols) + bias[0]).astype(BF16)
        q_ref[:, cols] = value * jnp.asarray(1.0 / math.sqrt(HEAD_DIM), BF16)

    def load_q(h, c):
        return q_ref[pl.ds(pl.multiple_of(h * HEAD_DIM, HEAD_DIM), HEAD_DIM), pl.ds(pl.multiple_of(c * PCH, PCH), PCH)]

    def scores(k, q):
        return lax.dot_general(k, q, (((0,), (0,)), ((), ())), preferred_element_type=F32)

    def diag(i, carry):
        c, h = i // heads, i % heads
        rows = pl.ds(pl.multiple_of(h * HEAD_DIM, HEAD_DIM), HEAD_DIM)
        vrows = pl.ds(pl.multiple_of(feats + h * HEAD_DIM, HEAD_DIM), HEAD_DIM)
        cols = pl.ds(pl.multiple_of(c * PCH, PCH), PCH)
        s = scores(kv_ref[rows, cols], load_q(h, c))
        key = lax.broadcasted_iota(jnp.int32, s.shape, 0)
        query = lax.broadcasted_iota(jnp.int32, s.shape, 1)
        s = jnp.where(key <= query, s, big_negative)
        m = jnp.max(s, axis=0, keepdims=True)
        p = jnp.exp(s - m)
        m_sc[h, :, cols] = m
        l_sc[h, :, cols] = jnp.sum(p, axis=0, keepdims=True)
        acc[rows, cols] = jnp.dot(kv_ref[vrows, cols], p.astype(BF16), preferred_element_type=F32)
        return carry
    lax.fori_loop(0, 2 * heads, diag, 0)

    branch = branch_ref[0, 0]

    def full(source, c, block):
        limit = jnp.where(c == 0, n * PCH, branch) - block * PCH
        def body(h, carry):
            rows = pl.ds(pl.multiple_of(h * HEAD_DIM, HEAD_DIM), HEAD_DIM)
            vrows = pl.ds(pl.multiple_of(feats + h * HEAD_DIM, HEAD_DIM), HEAD_DIM)
            cols = pl.ds(pl.multiple_of(c * PCH, PCH), PCH)
            s = scores(source[rows, :], load_q(h, c))
            key = lax.broadcasted_iota(jnp.int32, (PCH, 1), 0)
            s = s + jnp.where(key < limit, 0.0, big_negative)
            m_old = m_sc[h, :, cols]
            m = jnp.maximum(m_old, jnp.max(s, axis=0, keepdims=True))
            p = jnp.exp(s - m)
            alpha = jnp.exp(m_old - m)
            m_sc[h, :, cols] = m
            l_sc[h, :, cols] = l_sc[h, :, cols] * alpha + jnp.sum(p, axis=0, keepdims=True)
            acc[rows, cols] = acc[rows, cols] * alpha + jnp.dot(source[vrows, :], p.astype(BF16), preferred_element_type=F32)
            return carry
        lax.fori_loop(0, heads, body, 0)

    full(own, 1, z)

    def step_body(step, carry):
        @pl.when(z >= step)
        def _():
            hop(own, z - step, step - 1, z, up_send, up_recv).wait_recv()
            @pl.when(has_up & (step < n - 1))
            def _(): hop(kv_all.at[z - step], z - step, step, z + 1, up_send, up_recv).start()
        @pl.when(z + step < n)
        def _():
            hop(own, z + step, step - 1, z, down_send, down_recv).wait_recv()
            @pl.when(has_down & (step < n - 1))
            def _(): hop(kv_all.at[z + step], z + step, step, z - 1, down_send, down_recv).start()
        @pl.when(z >= step)
        def _():
            def both(c, carry):
                full(kv_all.at[z - step], c, z - step)
                return carry
            lax.fori_loop(0, 2, both, 0)
        @pl.when(z + step < n)
        def _(): full(kv_all.at[z + step], 1, z + step)
        return carry
    lax.fori_loop(1, n, step_body, 0)

    for h in range(heads):
        rows = slice(h * HEAD_DIM, (h + 1) * HEAD_DIM)
        total = l_sc[h]
        out = acc[rows, :] / total
        of_ref[rows, :] = out
        o_ref[rows, :] = out.astype(BF16)
        lse_ref[h:h + 1, :] = m_sc[h] + jnp.log(total)

    for step in range(n - 1):
        @pl.when(has_up & (z >= step))
        def _(): hop(own, z, step, z + 1, up_send, up_recv).wait_send()
        @pl.when(has_down & (z + step < n))
        def _(): hop(own, z, step, z - 1, down_send, down_recv).wait_send()

def attend_forward(n, tokens, w_attn, attn_bias, norm_gains, norm_shifts, branch):
    rows, width = tokens.shape
    feats = attn_bias.shape[1]
    heads = feats // HEAD_DIM
    vm = pl.BlockSpec(memory_space=pltpu.VMEM)
    shape = jax.ShapeDtypeStruct
    sems = pltpu.SemaphoreType.DMA((n - 1,))
    return pl.pallas_call(
        functools.partial(forward_kernel, n, heads),
        out_shape=(
            shape((feats, rows), BF16), shape((feats, rows), F32), shape((heads, rows), F32),
            shape((n, 2 * feats, PCH), BF16), shape((feats, rows), BF16), shape((2 * feats, rows), BF16),
            shape((rows, width), BF16),
        ),
        in_specs=[vm] * 5 + [pl.BlockSpec(memory_space=pltpu.SMEM)],
        out_specs=(vm,) * 7,
        scratch_shapes=[
            pltpu.VMEM((heads, 1, rows), F32),
            pltpu.VMEM((heads, 1, rows), F32),
            pltpu.VMEM((feats, rows), F32),
            sems, sems, sems, sems,
        ],
        compiler_params=pltpu.CompilerParams(collective_id=1, has_side_effects=True, vmem_limit_bytes=60 * 2**20),
        cost_estimate=pl.CostEstimate(flops=4 * 10**10, bytes_accessed=10**7, transcendentals=0),
        name="attend_forward",
    )(tokens, w_attn, attn_bias, norm_gains, norm_shifts, branch)


def flip(index, bit):
    return index + bit * (1 - 2 * lax.rem(lax.div(index, bit), 2))


def log_bits(size):
    return [1 << k for k in range(size.bit_length() - 1)]


def finish_kernel(
    n, dp_count, heads, layer_scale,
    q_ref, kv_ref, all_ref, branch_ref, do_ref, of_ref, lse_ref, far_ref, con_ref,
    near_any, exp_any, proj_any, early_any, esum_any, wa_any, normed_any, tok_any, ghid_any, gain_any,
    lout_ref, gtok_ref, con_out, exp_out, proj_out, query_out, keyval_out, sums_ref,
    dq_acc, own_acc, far_up, far_down, lse_sc, dot_sc, up_out, up_in, down_out, down_in,
    near_ref, exp_ref, proj_ref, early_ref, esum_ref, wa_ref, normed_ref, tok_ref, ghid_ref, gain_ref,
    stacked, mix, xhat_sc, inv_sc, query_sc, keyval_sc,
    con_xo, con_xi, con_acc, con_zo, con_zi,
    exp_xo, exp_xi, exp_acc, exp_zo, exp_zi,
    proj_xo, proj_xi, proj_acc, proj_zo, proj_zi,
    query_xo, query_xi, query_acc, query_zo, query_zi,
    keyval_xo, keyval_xi, keyval_acc, keyval_zo, keyval_zi,
    core_out, core_in, y_out, y_in, far_in, seq_in, tensor_in, dp_out, dp_in,
    up_send, up_recv, down_send, down_recv, x_send, x_recv, z_send, z_recv,
    core_send, core_recv, y_send, y_recv, seq_send, seq_recv, tensor_send, tensor_recv, dp_send, dp_recv,
    fetch_sem,
):
    z = lax.axis_index("seq")
    t = lax.axis_index("tensor")
    dp = lax.axis_index("dp")
    feats = heads * HEAD_DIM
    share = ghid_ref.shape[0]
    has_up, has_down = z < n - 1, z > 0
    dp_bits = log_bits(dp_count)
    bits = len(dp_bits)
    blocks = dp_count * n
    mesh_ids = pl.DeviceIdType.MESH

    fetches = [
        pltpu.make_async_copy(src, dst, fetch_sem.at[i])
        for i, (src, dst) in enumerate(
            [
                (proj_any, proj_ref), (exp_any, exp_ref), (normed_any, normed_ref), (tok_any, tok_ref),
                (wa_any, wa_ref), (near_any, near_ref), (ghid_any, ghid_ref), (early_any, early_ref),
                (esum_any, esum_ref), (gain_any, gain_ref),
            ]
        )
    ]
    for one in fetches:
        one.start()

    barrier = pltpu.get_barrier_semaphore()
    seq_peers = [{"seq": lax.rem(z + d, n)} for d in range(1, n)]
    tensor_peers = [{"tensor": lax.rem(t + d, 4)} for d in range(1, 4)]
    dp_peers = [{"dp": flip(dp, bit)} for bit in dp_bits]
    for peer in seq_peers + tensor_peers + dp_peers:
        pl.semaphore_signal(barrier, inc=1, device_id=peer, device_id_type=mesh_ids)
    pl.semaphore_wait(barrier, n + 2 + bits)

    def remote(src, dst, send, recv, to):
        return pltpu.make_async_remote_copy(
            src_ref=src, dst_ref=dst, send_sem=send, recv_sem=recv, device_id=to, device_id_type=mesh_ids
        )

    class Scatter:
        def __init__(self, number, first, source, xo, xi, acc, zo, zi, out):
            self.number, self.first, self.source, self.xo, self.xi = number, first, source, xo, xi
            self.acc, self.zo, self.zi, self.out = acc, zo, zi, out

        def mine(self, s):
            return lax.rem(lax.div(dp, dp_count >> (s + 1)), 2)

        def start_of(self, s):
            return (blocks >> self.first) - (blocks >> s)

        def held(self, s):
            return self.source if s == self.first else self.acc

        def x_copy(self, s, j=None):
            half, start = blocks >> (s + 1), self.start_of(s)
            sem = self.number * (bits - 1 + n) + (n + s if j is None else j)
            part = pl.ds(start, half) if j is None else start + j
            return remote(
                self.xo.at[part], self.xi.at[part], x_send.at[sem], x_recv.at[sem],
                {"dp": flip(dp, dp_count >> (s + 1))},
            )

        def x_begin(self, s):
            half, start, held = blocks >> (s + 1), self.start_of(s), self.held(s)
            other = (1 - self.mine(s)) * half
            if s == bits - 1:
                for d in range(n):
                    j = lax.rem(z + 1 + d, n)
                    self.xo[start + j] = held[other + j].astype(BF16)
                    self.x_copy(s, j).start()
                return

            def body(j, carry):
                self.xo[start + j] = held[other + j].astype(BF16)
                return carry

            lax.fori_loop(0, half, body, 0)
            self.x_copy(s).start()

        def relay(self):
            for s in range(self.first, bits - 1):
                half, start, held = blocks >> (s + 1), self.start_of(s), self.held(s)
                own = self.mine(s) * half
                self.x_copy(s).wait_recv()

                def body(j, carry):
                    self.acc[j] = held[own + j] + self.xi[start + j].astype(F32)
                    return carry

                lax.fori_loop(0, half, body, 0)
                self.x_begin(s + 1)
            s = bits - 1
            done = self.first == bits
            for d in range(n):
                j = lax.rem(z + 1 + d, n)
                if done:
                    value = self.source[j]
                else:
                    self.x_copy(s, j).wait_recv()
                    own = self.mine(s) * n
                    value = self.held(s)[own + j] + self.xi[self.start_of(s) + j].astype(F32)
                if d < n - 1:
                    self.zo[j] = value.astype(BF16)
                    self.z_copy(j, z).start()
                else:
                    self.out[...] = value

        def z_copy(self, target, sender):
            base = self.number * n
            return remote(
                self.zo.at[target], self.zi.at[sender], z_send.at[base + target], z_recv.at[base + sender],
                {"seq": target},
            )

        def z_end(self):
            for d in range(1, n):
                i = lax.rem(z + d, n)
                self.z_copy(i, i).wait_recv()
                self.out[...] += self.zi[i].astype(F32)

        def drain(self):
            for s in range(self.first, bits - 1):
                self.x_copy(s).wait_send()
            for j in range(n):
                if self.first < bits:
                    self.x_copy(bits - 1, j).wait_send()
            for d in range(1, n):
                self.z_copy(lax.rem(z + d, n), z).wait_send()

    contract = Scatter(0, 1, con_ref, con_xo, con_xi, con_acc, con_zo, con_zi, con_out)
    expand = Scatter(1, 0, exp_ref, exp_xo, exp_xi, exp_acc, exp_zo, exp_zi, exp_out)
    project = Scatter(2, 0, proj_ref, proj_xo, proj_xi, proj_acc, proj_zo, proj_zi, proj_out)
    query = Scatter(3, 0, query_sc, query_xo, query_xi, query_acc, query_zo, query_zi, query_out)
    keyval = Scatter(4, 0, keyval_sc, keyval_xo, keyval_xi, keyval_acc, keyval_zo, keyval_zi, keyval_out)
    scatters = (contract, expand, project, query, keyval)

    sibling, partner = {"tensor": flip(t, 1)}, {"tensor": flip(t, 2)}
    far_copy = remote(far_ref, far_in, y_send.at[0], y_recv.at[0], partner)
    far_copy.start()
    if contract.first < bits:
        contract.x_begin(contract.first)
    contract.relay()
    fetches[0].wait()
    project.x_begin(0)
    fetches[1].wait()
    expand.x_begin(0)

    def hop(out, inn, d, to, send, recv):
        return remote(out.at[d], inn.at[d], send.at[d], recv.at[d], {"seq": to})

    dq_acc[...] = jnp.zeros_like(dq_acc)
    for h in range(heads):
        rows = slice(h * HEAD_DIM, (h + 1) * HEAD_DIM)
        lse_sc[h] = lse_ref[h:h + 1, :]
        dot_sc[h] = jnp.sum(do_ref[rows, :].astype(F32) * of_ref[rows, :], axis=0, keepdims=True)

    nt = (((1,), (1,)), ((), ()))
    tn = (((0,), (0,)), ((), ()))

    def tile(h, cols, k, v, mask):
        rows = pl.ds(pl.multiple_of(h * HEAD_DIM, HEAD_DIM), HEAD_DIM)
        q, do = q_ref[rows, cols], do_ref[rows, cols]
        s = mask(lax.dot_general(k, q, tn, preferred_element_type=F32))
        p = jnp.exp(s - lse_sc[h, :, cols])
        dp = lax.dot_general(v, do, tn, preferred_element_type=F32)
        ds = (p * (dp - dot_sc[h, :, cols])).astype(BF16)
        p = p.astype(BF16)
        dv = lax.dot_general(do, p, nt, preferred_element_type=F32)
        dk = lax.dot_general(q, ds, nt, preferred_element_type=F32)
        dq_acc[rows, cols] += jnp.dot(k, ds, preferred_element_type=F32)
        return dk, dv

    def head_rows(h):
        return (pl.ds(pl.multiple_of(h * HEAD_DIM, HEAD_DIM), HEAD_DIM),
                pl.ds(pl.multiple_of(feats + h * HEAD_DIM, HEAD_DIM), HEAD_DIM))

    def columns(c):
        return pl.ds(pl.multiple_of(c * PCH, PCH), PCH)

    branch = branch_ref[0, 0]

    def full(source, c, block, total):
        limit = jnp.where(c == 0, n * PCH, branch) - block * PCH
        def mask(s):
            key = lax.broadcasted_iota(jnp.int32, (PCH, 1), 0)
            return s + jnp.where(key < limit, 0.0, big_negative)
        def body(h, carry):
            rows, vrows = head_rows(h)
            dk, dv = tile(h, columns(c), source[rows, :], source[vrows, :], mask)
            total[rows, :] += dk
            total[vrows, :] += dv
            return carry
        lax.fori_loop(0, heads, body, 0)

    def diag(i, carry):
        c, h = i // heads, i % heads
        rows, vrows = head_rows(h)
        cols = columns(c)
        def mask(s):
            key = lax.broadcasted_iota(jnp.int32, s.shape, 0)
            query = lax.broadcasted_iota(jnp.int32, s.shape, 1)
            return jnp.where(key <= query, s, big_negative)
        dk, dv = tile(h, cols, kv_ref[rows, cols], kv_ref[vrows, cols], mask)
        own_acc[rows, cols] = dk
        own_acc[vrows, cols] = dv
        return carry

    def far_blocks(i, carry):
        d = n - 1 - i

        @pl.when(z + d < n)
        def _():
            far_up[d - 1] = jnp.zeros(far_up.shape[1:], F32)
            full(all_ref.at[z + d], 1, z + d, far_up.at[d - 1])
            @pl.when(~has_down | (d == n - 1))
            def _():
                up_out[d - 1] = far_up[d - 1].astype(BF16)
                hop(up_out, up_in, d - 1, z + 1, up_send, up_recv).start()

        @pl.when(z >= d)
        def _():
            far_down[d - 1] = jnp.zeros(far_down.shape[1:], F32)
            def both(c, carry):
                full(all_ref.at[z - d], c, z - d, far_down.at[d - 1])
                return carry
            lax.fori_loop(0, 2, both, 0)
            @pl.when(~has_up | (d == n - 1))
            def _():
                down_out[d - 1] = far_down[d - 1].astype(BF16)
                hop(down_out, down_in, d - 1, z - 1, down_send, down_recv).start()
        return carry

    lax.fori_loop(0, n - 1, far_blocks, 0)

    def relays(i, carry):
        d = n - 2 - i

        @pl.when(d == 1)
        def _():
            lax.fori_loop(0, 2 * heads, diag, 0)
            full(kv_ref.at[:, 0:PCH], 1, z, own_acc.at[:, 0:PCH])

        @pl.when((z + d < n) & has_down)
        def _():
            hop(up_out, up_in, d, z, up_send, up_recv).wait_recv()
            up_out[d - 1] = (far_up[d - 1] + up_in[d].astype(F32)).astype(BF16)
            hop(up_out, up_in, d - 1, z + 1, up_send, up_recv).start()

        @pl.when((z >= d) & has_up)
        def _():
            hop(down_out, down_in, d, z, down_send, down_recv).wait_recv()
            down_out[d - 1] = (far_down[d - 1] + down_in[d].astype(F32)).astype(BF16)
            hop(down_out, down_in, d - 1, z - 1, down_send, down_recv).start()
        return carry

    lax.fori_loop(0, n - 2, relays, 0)
    expand.relay()
    project.relay()

    def place(k):
        owner = t
        for bit in (1, 2):
            turned = flip(owner, bit)
            if isinstance(k, int):
                owner = turned if k & bit else owner
            else:
                owner = jnp.where(lax.rem(lax.div(k, bit), 2) == 1, turned, owner)
        return pl.ds(pl.multiple_of(owner * share, share), share)

    rows = query_sc.shape[1]

    def weight_gradient(part, target):
        value = jnp.dot(part, normed_ref[...], preferred_element_type=F32).T
        for b in range(blocks):
            target[b] = value[b * rows : (b + 1) * rows, :]

    stacked[0:feats, :] = (dq_acc[...] * (1.0 / math.sqrt(HEAD_DIM))).astype(BF16)
    for one in fetches[2:]:
        one.wait()
    weight_gradient(stacked[0:feats, :], query_sc)
    query.x_begin(0)
    stacked[feats:, PCH:] = own_acc[:, PCH:].astype(BF16)

    def prepare(k, carry):
        value = tok_ref[place(k), :].astype(F32)
        centred = value - jnp.mean(value, axis=-1, keepdims=True)
        inverse = lax.rsqrt(jnp.mean(centred * centred, axis=-1, keepdims=True) + norm_eps)
        xhat_sc[k] = centred * inverse
        inv_sc[k] = jnp.broadcast_to(inverse, (share, 128))
        return carry

    lax.fori_loop(0, 4, prepare, 0)

    @pl.when(has_down)
    def _():
        hop(up_out, up_in, 0, z, up_send, up_recv).wait_recv()
        own_acc[:, 0:PCH] += up_in[0].astype(F32)
    @pl.when(has_up)
    def _():
        hop(down_out, down_in, 0, z, down_send, down_recv).wait_recv()
        own_acc[:, 0:PCH] += down_in[0].astype(F32)
    stacked[feats:, 0:PCH] = own_acc[:, 0:PCH].astype(BF16)

    weight_gradient(stacked[feats:, :], keyval_sc)
    keyval.x_begin(0)

    def grad_normed(k):
        mix[k] = lax.dot_general(stacked[:, place(k)], wa_ref[...], tn, preferred_element_type=F32)
        return mix[k]

    def core_copy(i):
        return remote(core_out.at[i], core_in.at[i], core_send.at[i], core_recv.at[i], sibling)

    core_out[0] = grad_normed(3).astype(BF16)
    core_copy(0).start()
    last = grad_normed(2)
    core_copy(0).wait_recv()
    y_out[...] = (last + core_in[0].astype(F32)).astype(BF16)
    y_copy = remote(y_out, y_in, y_send.at[1], y_recv.at[1], partner)
    y_copy.start()
    core_out[1] = grad_normed(1).astype(BF16)
    core_copy(1).start()
    query.relay()
    grad_normed(0)

    width = seq_in.shape[2]
    seq_in[z, 0:2, :] = jnp.zeros((2, width), F32)
    seq_in[z, 2:6, :] = early_ref[...]
    seq_in[z, 6:7, :] = esum_ref[...]
    seq_in[z, 7:8, :] = jnp.zeros((1, width), F32)
    ones = jnp.ones((8, stacked.shape[1]), BF16)
    seq_in[z, 7:8, 0 : 3 * feats] = lax.dot_general(ones, stacked[...], nt, preferred_element_type=F32)[0:1]

    def statistics(k, carry):
        seq_in[z, 0:1, :] += jnp.sum(mix[k] * xhat_sc[k], axis=0, keepdims=True)
        seq_in[z, 1:2, :] += jnp.sum(mix[k], axis=0, keepdims=True)
        return carry

    lax.fori_loop(0, 4, statistics, 0)

    def seq_copy(target, sender):
        return remote(seq_in.at[z], seq_in.at[sender], seq_send.at[target], seq_recv.at[sender], {"seq": target})

    def tensor_copy(target, sender):
        return remote(
            tensor_in.at[t], tensor_in.at[sender], tensor_send.at[target], tensor_recv.at[sender],
            {"tensor": target},
        )

    def dp_copy(i):
        return remote(dp_out.at[i], dp_in.at[i], dp_send.at[i], dp_recv.at[i], dp_peers[i])

    for d in range(1, n):
        seq_copy(lax.rem(z + d, n), z).start()
    keyval.relay()
    far_copy.wait_recv()
    lout_ref[...] = (near_ref[...] + layer_scale * far_in[...].astype(F32)).astype(BF16)
    for d in range(1, n):
        other = lax.rem(z + d, n)
        seq_copy(other, other).wait_recv()
    summed = seq_in[0]
    for i in range(1, n):
        summed = summed + seq_in[i]
    tensor_in[t] = summed
    for d in range(1, 4):
        tensor_copy(lax.rem(t + d, 4), t).start()
    contract.z_end()
    for d in range(1, 4):
        other = lax.rem(t + d, 4)
        tensor_copy(other, other).wait_recv()
    total = tensor_in[0]
    for i in range(1, 4):
        total = total + tensor_in[i]
    own = tensor_in[t]
    row = lax.broadcasted_iota(jnp.int32, own.shape, 0)
    dp_out[0] = jnp.where(row < 6, total, own)
    dp_copy(0).start()
    expand.z_end()
    project.z_end()

    core_copy(1).wait_recv()
    y_copy.wait_recv()
    mixed = mix[0] + core_in[1].astype(F32) + y_in[...].astype(F32)
    e = mixed * gain_ref[0:1, :]
    xhat = xhat_sc[0]
    gtok_ref[...] = (
        ghid_ref[...]
        + inv_sc[0][:, 0:1]
        * (e - jnp.mean(e, axis=-1, keepdims=True) - xhat * jnp.mean(e * xhat, axis=-1, keepdims=True))
    ).astype(BF16)
    query.z_end()
    for i in range(bits):
        dp_copy(i).wait_recv()
        value = dp_out[i] + dp_in[i]
        if i + 1 < bits:
            dp_out[i + 1] = value
            dp_copy(i + 1).start()
        else:
            sums_ref[...] = value
    keyval.z_end()

    for d in range(1, n):
        @pl.when(z + d < n)
        def _(): hop(up_out, up_in, d - 1, z + 1, up_send, up_recv).wait_send()
        @pl.when(z >= d)
        def _(): hop(down_out, down_in, d - 1, z - 1, down_send, down_recv).wait_send()
    for one in scatters:
        one.drain()
    far_copy.wait_send()
    y_copy.wait_send()
    for i in range(2):
        core_copy(i).wait_send()
    for d in range(1, n):
        seq_copy(lax.rem(z + d, n), z).wait_send()
    for d in range(1, 4):
        tensor_copy(lax.rem(t + d, 4), t).wait_send()
    for i in range(bits):
        dp_copy(i).wait_send()


def finish(
    n, dp_count, layer_scale, q, kv, kv_all, branch, do, of, lse, near, far,
    grad_contract, grad_expand, grad_proj, early, expand_terms, w_attn, normed_one, token_rows,
    grad_hidden, norm_gains,
):
    feats, rows = q.shape
    heads = feats // HEAD_DIM
    share, width = grad_hidden.shape
    blocks = dp_count * n
    bits = len(log_bits(dp_count))
    vm = pl.BlockSpec(memory_space=pltpu.VMEM)
    anywhere = pl.BlockSpec(memory_space=pl.ANY)
    slots = pltpu.VMEM((n - 1, 2 * feats, PCH), BF16)
    shape = jax.ShapeDtypeStruct
    sems = lambda count: pltpu.SemaphoreType.DMA((count,))
    block_rows = width // blocks
    proj_blocks = grad_proj.reshape(blocks, block_rows, feats)
    units = grad_contract.shape[2]
    fetched = [
        near, grad_expand.reshape(blocks, block_rows, units), proj_blocks, early, expand_terms, w_attn, normed_one, token_rows,
        grad_hidden, norm_gains,
    ]
    widths = [(1, units), (0, units), (0, feats), (0, feats), (0, 2 * feats)]
    scatter_scratch = []
    for first, columns in widths:
        through = max((blocks >> first) - n, 1)
        kept = blocks >> (first + 1) if bits - first > 1 else 1
        scatter_scratch += [
            pltpu.VMEM((through, block_rows, columns), BF16),
            pltpu.VMEM((through, block_rows, columns), BF16),
            pltpu.VMEM((kept, block_rows, columns), F32),
            pltpu.VMEM((n, block_rows, columns), BF16),
            pltpu.VMEM((n, block_rows, columns), BF16),
        ]
    return pl.pallas_call(
        functools.partial(finish_kernel, n, dp_count, heads, layer_scale),
        out_shape=(
            shape((share, width), BF16),
            shape((share, width), BF16),
            *(shape((block_rows, columns), F32) for _, columns in widths),
            shape((8, width), F32),
        ),
        in_specs=[vm, vm, vm, pl.BlockSpec(memory_space=pltpu.SMEM)] + [vm] * 5 + [anywhere] * len(fetched),
        out_specs=(vm,) * 8,
        scratch_shapes=[
            pltpu.VMEM((feats, rows), F32),
            pltpu.VMEM((2 * feats, rows), F32),
            pltpu.VMEM((n - 1, 2 * feats, PCH), F32),
            pltpu.VMEM((n - 1, 2 * feats, PCH), F32),
            pltpu.VMEM((heads, 1, rows), F32),
            pltpu.VMEM((heads, 1, rows), F32),
            slots, slots, slots, slots,
            *(pltpu.VMEM(one.shape, one.dtype) for one in fetched),
            pltpu.VMEM((3 * feats, rows), BF16),
            pltpu.VMEM((4, share, width), F32),
            pltpu.VMEM((4, share, width), F32),
            pltpu.VMEM((4, share, 128), F32),
            pltpu.VMEM((blocks, block_rows, feats), F32),
            pltpu.VMEM((blocks, block_rows, 2 * feats), F32),
            *scatter_scratch,
            pltpu.VMEM((2, share, width), BF16),
            pltpu.VMEM((2, share, width), BF16),
            pltpu.VMEM((share, width), BF16),
            pltpu.VMEM((share, width), BF16),
            pltpu.VMEM((share, width), BF16),
            pltpu.VMEM((n, 8, width), F32),
            pltpu.VMEM((4, 8, width), F32),
            pltpu.VMEM((bits, 8, width), F32),
            pltpu.VMEM((bits, 8, width), F32),
            sems(n - 1), sems(n - 1), sems(n - 1), sems(n - 1),
            sems(5 * (bits - 1 + n)), sems(5 * (bits - 1 + n)), sems(5 * n), sems(5 * n),
            sems(2), sems(2), sems(2), sems(2), sems(n), sems(n), sems(4), sems(4), sems(bits), sems(bits),
            sems(len(fetched)),
        ],
        compiler_params=pltpu.CompilerParams(
            collective_id=2, has_side_effects=True, vmem_limit_bytes=60 * 2**20
        ),
        cost_estimate=pl.CostEstimate(flops=4 * 10**10, bytes_accessed=10**7, transcendentals=0),
        name="finish",
    )(q, kv, kv_all, branch, do, of, lse, far, grad_contract, *fetched)


def emit_kernel(
    feats, turned, lout, gtok, con, expand, proj, query, keyval, sums,
    lout_ref, gtok_ref, attn_ref, proj_ref, exp_ref, con_ref, bias_ref, branch_ref, units_ref, gains_ref, shifts_ref,
):
    lout_ref[...] = lout[...]
    gtok_ref[...] = gtok[...]
    attn_ref[0] = query[...]
    attn_ref[1] = keyval[:, 0:feats]
    attn_ref[2] = keyval[:, feats : 2 * feats]
    proj_ref[...] = proj[...].T if turned else proj[...]
    exp_ref[...] = expand[...]
    con_ref[...] = con[...]
    bias_ref[0:1, :] = sums[7:8, 0:feats]
    bias_ref[1:2, :] = sums[7:8, 2 * feats : 3 * feats]
    branch_ref[...] = sums[2:4, :]
    units_ref[...] = sums[6:7, :]
    for row, late, early in ((gains_ref, 0, 4), (shifts_ref, 1, 5)):
        row[0:1, :] = sums[late : late + 1, :]
        row[1:2, :] = sums[early : early + 1, :]


def emit(results):
    lout, gtok, con, expand, proj, query, keyval, sums = results
    rows, feats = query.shape
    share, width = lout.shape
    turned = rows % 8 == 0
    shape = jax.ShapeDtypeStruct
    vm = pl.BlockSpec(memory_space=pltpu.VMEM)
    outputs = pl.pallas_call(
        functools.partial(emit_kernel, feats, turned),
        out_shape=(
            shape((share, width), BF16), shape((share, width), BF16), shape((3, rows, feats), F32),
            shape((feats, rows) if turned else (rows, feats), F32), shape(expand.shape, F32),
            shape(con.shape, F32), shape((2, feats), F32), shape((2, width), F32),
            shape((1, expand.shape[1]), F32), shape((2, width), F32), shape((2, width), F32),
        ),
        in_specs=[vm] * 8,
        out_specs=(vm,) * 11,
        compiler_params=pltpu.CompilerParams(vmem_limit_bytes=60 * 2**20),
        name="emit",
    )(*results)
    lout, gtok, attn, proj, expand, con, bias, branch, units, gains, shifts = outputs
    whole = (1, 1, share, width)
    return (
        lout.reshape(whole), gtok.reshape(whole), attn, proj if turned else proj.T, expand, con.T,
        bias, branch, units.reshape(-1), gains, shifts,
    )


def middle_kernel(
    n, dp_count, layer_scale, o_ref, tok_ref, cot_ref, wp_ref, we_ref, wc_ref, bb_ref, eb_ref, gain_ref, shift_ref,
    ghid_ref, near_ref, far_ref, gatt_ref, gproj_ref, gexp_ref, gcon_ref, sums_ref, esum_ref,
    ga_sc, mix_sc, n2, gm, act, gp, att, own_sc, xhat_sc, inv_sc, proj_sc,
    core_out, core_in, y_out, y_in, con_sc, con_out, con_in,
    core_send, core_recv, y_send, y_recv, n2_send, n2_recv, att_send, att_recv, x_send, x_recv,
):
    t = lax.axis_index("tensor")
    dp = lax.axis_index("dp")
    y, c = t // 2, t % 2
    sibling = y * 2 + (1 - c)
    partner = (1 - y) * 2 + c
    share = own_sc.shape[0]

    def block(k):
        if isinstance(k, int):
            return ((1 - y) if k >= 2 else y) * 2 + ((1 - c) if k % 2 else c)
        return jnp.where(k >= 2, 1 - y, y) * 2 + jnp.where(k % 2 == 1, 1 - c, c)

    def place(k):
        return pl.ds(pl.multiple_of(block(k) * share, share), share)

    barrier = pltpu.get_barrier_semaphore()
    for to in (sibling, partner):
        pl.semaphore_signal(barrier, inc=1, device_id={"tensor": to}, device_id_type=pl.DeviceIdType.MESH)
    step = dp_count // 2
    across_dp = {"dp": flip(dp, step)}
    pl.semaphore_signal(barrier, inc=1, device_id=across_dp, device_id_type=pl.DeviceIdType.MESH)
    pl.semaphore_wait(barrier, 3)

    blocks = dp_count * n
    half = blocks // 2
    mine = lax.div(dp, step)

    halves = pltpu.make_async_remote_copy(
        src_ref=con_out, dst_ref=con_in, send_sem=x_send.at[0], recv_sem=x_recv.at[0],
        device_id=across_dp, device_id_type=pl.DeviceIdType.MESH,
    )

    def send_half(value):
        size = con_sc.shape[1]
        for b in range(blocks):
            con_sc[b] = value[b * size : (b + 1) * size, :]

        def body(j, carry):
            con_out[j] = con_sc[(1 - mine) * half + j].astype(BF16)
            return carry

        lax.fori_loop(0, half, body, 0)
        halves.start()

    def take_half(result):
        halves.wait_recv()

        def body(j, carry):
            result[j] = con_sc[mine * half + j] + con_in[j].astype(F32)
            return carry

        lax.fori_loop(0, half, body, 0)

    def copy(src, dst, send, recv, to):
        return pltpu.make_async_remote_copy(
            src_ref=src, dst_ref=dst, send_sem=send, recv_sem=recv,
            device_id={"tensor": to}, device_id_type=pl.DeviceIdType.MESH,
        )

    def core_copy(i):
        return copy(core_out.at[i], core_in.at[i], core_send.at[i], core_recv.at[i], sibling)

    def y_copy(i):
        return copy(y_out.at[i], y_in.at[i], y_send.at[i], y_recv.at[i], partner)

    def gather(ref, send, recv):
        return (
            copy(ref.at[0], ref.at[2], send.at[0], recv.at[0], partner),
            copy(ref.at[0], ref.at[1], send.at[1], recv.at[1], sibling),
            copy(ref.at[2], ref.at[3], send.at[2], recv.at[2], sibling),
        )

    tn = (((0,), (0,)), ((), ()))
    nt = (((1,), (1,)), ((), ()))

    def project(k):
        return lax.dot_general(o_ref[:, place(k)], wp_ref[...], tn, preferred_element_type=F32)

    core_out[0] = project(3).astype(BF16)
    core_copy(0).start()
    own_sc[...] = project(2)
    core_out[1] = project(1).astype(BF16)
    core_copy(1).start()
    core_copy(0).wait_recv()
    y_out[0] = (own_sc[...] + core_in[0].astype(F32)).astype(BF16)
    y_copy(0).start()
    own_sc[...] = project(0)

    def before(k, carry):
        g = (cot_ref[place(k), :].astype(F32) * layer_scale).astype(BF16)
        gm[k] = g
        ga_sc[k] = lax.dot_general(g, wc_ref[...], nt, preferred_element_type=F32)
        return carry

    lax.fori_loop(0, 4, before, 0)
    core_copy(1).wait_recv()
    own_sc[...] += core_in[1].astype(F32)
    y_copy(0).wait_recv()

    hidden = tok_ref[place(0), :].astype(F32) + layer_scale * (
        own_sc[...] + y_in[0].astype(F32) + bb_ref[0:1, :]
    )
    near_ref[...] = hidden + layer_scale * bb_ref[1:2, :]
    centred = hidden - jnp.mean(hidden, axis=-1, keepdims=True)
    inverse = lax.rsqrt(jnp.mean(centred * centred, axis=-1, keepdims=True) + norm_eps)
    xhat = centred * inverse
    n2[0] = (xhat * gain_ref[1:2, :] + shift_ref[1:2, :]).astype(BF16)
    across, near, on = gather(n2, n2_send, n2_recv)
    across.start()
    near.start()
    xhat_sc[...] = xhat
    inv_sc[...] = jnp.broadcast_to(inverse, inv_sc.shape)
    esum_ref[...] = jnp.zeros_like(esum_ref)

    def process(k, carry):
        @pl.when(k == 1)
        def _():
            near.wait_recv()

        @pl.when(k == 2)
        def _():
            across.wait_recv()
            on.start()

        @pl.when(k == 3)
        def _():
            on.wait_recv()

        v = jnp.dot(n2[k], we_ref[...], preferred_element_type=F32) + eb_ref[...]
        square = v * v
        th = jnp.tanh(math.sqrt(2.0 / math.pi) * (v + 0.044715 * (v * square)))
        cdf = 0.5 * (1.0 + th)
        act[k] = (v * cdf).astype(BF16)
        slope = cdf + 0.5 * v * (1.0 - th * th) * (
            math.sqrt(2.0 / math.pi) * (1.0 + 3 * 0.044715 * square)
        )
        g = (slope * ga_sc[k]).astype(BF16)
        gp[k] = g
        esum_ref[...] += jnp.sum(g.astype(F32), axis=0, keepdims=True)
        mix_sc[k] = lax.dot_general(g, we_ref[...], nt, preferred_element_type=F32)
        return carry

    lax.fori_loop(0, 4, process, 0)
    core_out[2] = mix_sc[3].astype(BF16)
    core_copy(2).start()
    core_out[3] = mix_sc[1].astype(BF16)
    core_copy(3).start()
    core_copy(2).wait_recv()
    y_out[1] = (mix_sc[2] + core_in[2].astype(F32)).astype(BF16)
    y_copy(1).start()

    rows = 4 * share
    width = gm.shape[2]
    send_half(lax.dot_general(
        gm[...].reshape(rows, width), act[...].reshape(rows, -1), tn, preferred_element_type=F32
    ))
    gexp_ref[...] = lax.dot_general(
        n2[...].reshape(rows, width), gp[...].reshape(rows, -1), tn, preferred_element_type=F32
    )

    def contract(k):
        return jnp.dot(act[k], wc_ref[...], preferred_element_type=F32)

    core_out[4] = contract(3).astype(BF16)
    core_copy(4).start()
    core_out[5] = contract(1).astype(BF16)
    core_copy(5).start()
    near_ref[...] += layer_scale * contract(0)
    last = contract(2)
    core_copy(4).wait_recv()
    far_ref[...] = (last + core_in[4].astype(F32)).astype(BF16)
    core_copy(5).wait_recv()
    near_ref[...] += layer_scale * core_in[5].astype(F32)

    core_copy(3).wait_recv()
    mixed = mix_sc[0] + core_in[3].astype(F32)
    y_copy(1).wait_recv()
    mixed = mixed + y_in[1].astype(F32)
    e = mixed * gain_ref[1:2, :]
    xhat = xhat_sc[...]
    grad_hidden = cot_ref[place(0), :].astype(F32) + inv_sc[:, 0:1] * (
        e - jnp.mean(e, axis=-1, keepdims=True) - xhat * jnp.mean(e * xhat, axis=-1, keepdims=True)
    )
    g = (grad_hidden * layer_scale).astype(BF16)
    att[0] = g
    across_b, near_b, on_b = gather(att, att_send, att_recv)
    across_b.start()
    near_b.start()
    ghid_ref[...] = grad_hidden
    sums_ref[0:1, :] = jnp.sum(g.astype(F32), axis=0, keepdims=True)
    sums_ref[1:2, :] = jnp.sum(gm[0].astype(F32), axis=0, keepdims=True)
    sums_ref[2:3, :] = jnp.sum(mixed * xhat, axis=0, keepdims=True)
    sums_ref[3:4, :] = jnp.sum(mixed, axis=0, keepdims=True)

    proj_sc[...] = jnp.zeros_like(proj_sc)

    def after(k, carry):
        @pl.when(k == 1)
        def _():
            near_b.wait_recv()

        @pl.when(k == 2)
        def _():
            across_b.wait_recv()
            on_b.start()

        @pl.when(k == 3)
        def _():
            on_b.wait_recv()

        gatt_ref[:, place(k)] = lax.dot_general(
            wp_ref[...], att[k], nt, preferred_element_type=F32
        ).astype(BF16)
        proj_sc[...] += jnp.dot(o_ref[:, place(k)], att[k], preferred_element_type=F32)
        return carry

    lax.fori_loop(0, 4, after, 0)
    gproj_ref[...] = proj_sc[...].T
    take_half(gcon_ref)
    halves.wait_send()
    for i in range(6):
        core_copy(i).wait_send()
    for i in range(2):
        y_copy(i).wait_send()
    for one in (across, near, on, across_b, near_b, on_b):
        one.wait_send()


def middle(
    n, dp_count, layer_scale, attended, token_rows, cotangent_rows, w_proj, w_expand, w_contract,
    branch_bias, expand_bias, norm_gains, norm_shifts,
):
    rows, width = token_rows.shape
    feats, hidden_units = w_proj.shape[0], w_expand.shape[1]
    share = rows // 4
    half, size = dp_count * n // 2, width // (dp_count * n)
    vm = pl.BlockSpec(memory_space=pltpu.VMEM)
    shape = jax.ShapeDtypeStruct
    slots = lambda columns, kind: pltpu.VMEM((4, share, columns), kind)
    sems = lambda count: pltpu.SemaphoreType.DMA((count,))
    return pl.pallas_call(
        functools.partial(middle_kernel, n, dp_count, layer_scale),
        out_shape=(
            shape((share, width), F32),
            shape((share, width), F32),
            shape((share, width), BF16),
            shape((feats, rows), BF16),
            shape((width, feats), F32),
            shape((width, hidden_units), F32),
            shape((half, size, hidden_units), F32),
            shape((4, width), F32),
            shape((1, hidden_units), F32),
        ),
        in_specs=[vm] * 10,
        out_specs=(vm,) * 9,
        scratch_shapes=[
            slots(hidden_units, F32),
            slots(width, F32),
            slots(width, BF16),
            slots(width, BF16),
            slots(hidden_units, BF16),
            slots(hidden_units, BF16),
            slots(width, BF16),
            pltpu.VMEM((share, width), F32),
            pltpu.VMEM((share, width), F32),
            pltpu.VMEM((share, 128), F32),
            pltpu.VMEM((feats, width), F32),
            pltpu.VMEM((6, share, width), BF16),
            pltpu.VMEM((6, share, width), BF16),
            pltpu.VMEM((2, share, width), BF16),
            pltpu.VMEM((2, share, width), BF16),
            pltpu.VMEM((2 * half, size, hidden_units), F32),
            pltpu.VMEM((half, size, hidden_units), BF16),
            pltpu.VMEM((half, size, hidden_units), BF16),
            sems(6), sems(6), sems(2), sems(2), sems(3), sems(3), sems(3), sems(3), sems(1), sems(1),
        ],
        compiler_params=pltpu.CompilerParams(
            collective_id=3, has_side_effects=True, vmem_limit_bytes=56 * 2**20
        ),
        cost_estimate=pl.CostEstimate(flops=5 * 10**10, bytes_accessed=2 * 10**7, transcendentals=0),
        name="middle",
    )(
        attended, token_rows, cotangent_rows, w_proj, w_expand, w_contract,
        branch_bias, expand_bias, norm_gains, norm_shifts,
    )


def shards(
    tokens,
    branch,
    w_attn,
    w_proj,
    w_expand,
    w_contract,
    attn_bias,
    branch_bias,
    expand_bias,
    norm_gains,
    norm_shifts,
    cotangent,
):
    seq_count = lax.axis_size("seq")
    width = tokens.shape[3]
    row_count = tokens.shape[2]
    share = row_count // lax.axis_size("tensor")
    local_width = w_attn.shape[2]
    layer_scale = 1.0 / math.sqrt(LAYERS)

    token_rows = tokens.reshape(row_count, width)
    cotangent_rows = cotangent.reshape(row_count, width)
    w_attn = jnp.transpose(w_attn, (0, 2, 1)).reshape(3 * local_width, width)
    attended, attended_wide, logsum, all_kv, queries, own_kv, normed_one = attend_forward(
        seq_count, token_rows, w_attn, attn_bias, norm_gains, norm_shifts, branch
    )
    (
        grad_hidden, mlp_near, mlp_far, grad_attended,
        grad_proj, grad_expand, grad_contract, early, expand_terms,
    ) = middle(
        seq_count, lax.axis_size("dp"), layer_scale, attended, token_rows, cotangent_rows, w_proj, w_expand, w_contract,
        branch_bias, expand_bias.reshape(1, -1), norm_gains, norm_shifts,
    )
    return emit(finish(
        seq_count, lax.axis_size("dp"), layer_scale, queries, own_kv, all_kv, branch, grad_attended,
        attended_wide, logsum, mlp_near, mlp_far, grad_contract, grad_expand, grad_proj, early,
        expand_terms, w_attn, normed_one, token_rows, grad_hidden, norm_gains,
    ))


def solution(mesh):
    placed = (
        P("dp", "seq", None, None),
        P("dp", "seq"),
        P(None, None, "tensor"),
        P("tensor", None),
        P(None, "tensor"),
        P("tensor", None),
        P(None, "tensor"),
        P(),
        P("tensor"),
        P(),
        P(),
        P("dp", "seq", None, None),
    )
    return jax.shard_map(
        shards,
        mesh=mesh,
        in_specs=placed,
        out_specs=(
            P("dp", "seq", "tensor", None),
            P("dp", "seq", "tensor", None),
            P(None, ("dp", "seq"), "tensor"),
            P("tensor", ("dp", "seq")),
            P(("dp", "seq"), "tensor"),
            P("tensor", ("dp", "seq")),
            P(None, "tensor"),
            P(),
            P("tensor"),
            P(),
            P(),
        ),
        check_vma=False,
    )
```

```python
import functools
import math

import jax
import jax.numpy as jnp
from jax import lax
from jax.experimental import pallas as pl
from jax.experimental.pallas import tpu as pltpu
from jax.sharding import PartitionSpec as P

HEAD_DIM = 64
LAYERS = 12
PCH = 512
CLEN = 512
F32 = jnp.float32
BF16 = jnp.bfloat16


norm_eps = 1e-05
big_negative = -1000000000.0


def layer_norm_parts(value):
    centre = jnp.mean(value, axis=-1, keepdims=True)
    centred = value - centre
    spread = jnp.mean(centred * centred, axis=-1, keepdims=True)
    inverse = lax.rsqrt(spread + norm_eps)
    return centred * inverse, inverse


def forward_kernel(n, heads, tok_ref, wa_ref, bias_ref, gain_ref, shift_ref, branch_ref, o_ref, of_ref, lse_ref, kv_all, q_ref, kv_ref, normed_ref, m_sc, l_sc, acc, up_send, up_recv, down_send, down_recv):
    z = lax.axis_index("seq")
    feats = heads * HEAD_DIM
    barrier = pltpu.get_barrier_semaphore()
    has_up, has_down = z < n - 1, z > 0

    def meet(to):
        pl.semaphore_signal(barrier, inc=1, device_id={"seq": to}, device_id_type=pl.DeviceIdType.MESH)

    @pl.when(has_up)
    def _(): meet(z + 1)
    @pl.when(has_down)
    def _(): meet(z - 1)

    bias = [jnp.broadcast_to(bias_ref[i : i + 1, :], (8, feats)).T[:, 0:1] for i in range(2)]

    def project(first, cols):
        normed = normed_ref[cols, :]
        value = lax.dot_general(
            wa_ref[first * feats :, :] if first else wa_ref[0:feats, :], normed,
            (((1,), (1,)), ((), ())), preferred_element_type=F32,
        )
        return value

    def norm_rows(cols):
        value = layer_norm_parts(tok_ref[cols, :].astype(F32))[0]
        normed_ref[cols, :] = (value * gain_ref[0:1, :] + shift_ref[0:1, :]).astype(BF16)

    def keys_values(cols):
        value = project(1, cols)
        kv_ref[0:feats, cols] = value[0:feats].astype(BF16)
        kv_ref[feats:, cols] = (value[feats:] + bias[1]).astype(BF16)

    prompt_cols, other_cols = slice(0, PCH), slice(PCH, q_ref.shape[1])
    norm_rows(prompt_cols)
    keys_values(prompt_cols)
    pl.semaphore_wait(barrier, has_up.astype(jnp.int32) + has_down.astype(jnp.int32))

    own = kv_ref.at[:, 0:PCH]

    def hop(src, block, step, to, send, recv):
        return pltpu.make_async_remote_copy(src_ref=src, dst_ref=kv_all.at[block], send_sem=send.at[step], recv_sem=recv.at[step], device_id={"seq": to}, device_id_type=pl.DeviceIdType.MESH)

    @pl.when(has_up)
    def _(): hop(own, z, 0, z + 1, up_send, up_recv).start()
    @pl.when(has_down)
    def _(): hop(own, z, 0, z - 1, down_send, down_recv).start()

    norm_rows(other_cols)
    keys_values(other_cols)
    for cols in (prompt_cols, other_cols):
        value = (project(0, cols) + bias[0]).astype(BF16)
        q_ref[:, cols] = value * jnp.asarray(1.0 / math.sqrt(HEAD_DIM), BF16)

    def load_q(h, c):
        return q_ref[pl.ds(pl.multiple_of(h * HEAD_DIM, HEAD_DIM), HEAD_DIM), pl.ds(pl.multiple_of(c * PCH, PCH), PCH)]

    def scores(k, q):
        return lax.dot_general(k, q, (((0,), (0,)), ((), ())), preferred_element_type=F32)

    def diag(i, carry):
        c, h = i // heads, i % heads
        rows = pl.ds(pl.multiple_of(h * HEAD_DIM, HEAD_DIM), HEAD_DIM)
        vrows = pl.ds(pl.multiple_of(feats + h * HEAD_DIM, HEAD_DIM), HEAD_DIM)
        cols = pl.ds(pl.multiple_of(c * PCH, PCH), PCH)
        s = scores(kv_ref[rows, cols], load_q(h, c))
        key = lax.broadcasted_iota(jnp.int32, s.shape, 0)
        query = lax.broadcasted_iota(jnp.int32, s.shape, 1)
        s = jnp.where(key <= query, s, big_negative)
        m = jnp.max(s, axis=0, keepdims=True)
        p = jnp.exp(s - m)
        m_sc[h, :, cols] = m
        l_sc[h, :, cols] = jnp.sum(p, axis=0, keepdims=True)
        acc[rows, cols] = jnp.dot(kv_ref[vrows, cols], p.astype(BF16), preferred_element_type=F32)
        return carry
    lax.fori_loop(0, 2 * heads, diag, 0)

    branch = branch_ref[0, 0]

    def full(source, c, block):
        limit = jnp.where(c == 0, n * PCH, branch) - block * PCH
        def body(h, carry):
            rows = pl.ds(pl.multiple_of(h * HEAD_DIM, HEAD_DIM), HEAD_DIM)
            vrows = pl.ds(pl.multiple_of(feats + h * HEAD_DIM, HEAD_DIM), HEAD_DIM)
            cols = pl.ds(pl.multiple_of(c * PCH, PCH), PCH)
            s = scores(source[rows, :], load_q(h, c))
            key = lax.broadcasted_iota(jnp.int32, (PCH, 1), 0)
            s = s + jnp.where(key < limit, 0.0, big_negative)
            m_old = m_sc[h, :, cols]
            m = jnp.maximum(m_old, jnp.max(s, axis=0, keepdims=True))
            p = jnp.exp(s - m)
            alpha = jnp.exp(m_old - m)
            m_sc[h, :, cols] = m
            l_sc[h, :, cols] = l_sc[h, :, cols] * alpha + jnp.sum(p, axis=0, keepdims=True)
            acc[rows, cols] = acc[rows, cols] * alpha + jnp.dot(source[vrows, :], p.astype(BF16), preferred_element_type=F32)
            return carry
        lax.fori_loop(0, heads, body, 0)

    full(own, 1, z)

    def step_body(step, carry):
        @pl.when(z >= step)
        def _():
            hop(own, z - step, step - 1, z, up_send, up_recv).wait_recv()
            @pl.when(has_up & (step < n - 1))
            def _(): hop(kv_all.at[z - step], z - step, step, z + 1, up_send, up_recv).start()
        @pl.when(z + step < n)
        def _():
            hop(own, z + step, step - 1, z, down_send, down_recv).wait_recv()
            @pl.when(has_down & (step < n - 1))
            def _(): hop(kv_all.at[z + step], z + step, step, z - 1, down_send, down_recv).start()
        @pl.when(z >= step)
        def _():
            def both(c, carry):
                full(kv_all.at[z - step], c, z - step)
                return carry
            lax.fori_loop(0, 2, both, 0)
        @pl.when(z + step < n)
        def _(): full(kv_all.at[z + step], 1, z + step)
        return carry
    lax.fori_loop(1, n, step_body, 0)

    for h in range(heads):
        rows = slice(h * HEAD_DIM, (h + 1) * HEAD_DIM)
        total = l_sc[h]
        out = acc[rows, :] / total
        of_ref[rows, :] = out
        o_ref[rows, :] = out.astype(BF16)
        lse_ref[h:h + 1, :] = m_sc[h] + jnp.log(total)

    for step in range(n - 1):
        @pl.when(has_up & (z >= step))
        def _(): hop(own, z, step, z + 1, up_send, up_recv).wait_send()
        @pl.when(has_down & (z + step < n))
        def _(): hop(own, z, step, z - 1, down_send, down_recv).wait_send()

def attend_forward(n, tokens, w_attn, attn_bias, norm_gains, norm_shifts, branch):
    rows, width = tokens.shape
    feats = attn_bias.shape[1]
    heads = feats // HEAD_DIM
    vm = pl.BlockSpec(memory_space=pltpu.VMEM)
    shape = jax.ShapeDtypeStruct
    sems = pltpu.SemaphoreType.DMA((n - 1,))
    return pl.pallas_call(
        functools.partial(forward_kernel, n, heads),
        out_shape=(
            shape((feats, rows), BF16), shape((feats, rows), F32), shape((heads, rows), F32),
            shape((n, 2 * feats, PCH), BF16), shape((feats, rows), BF16), shape((2 * feats, rows), BF16),
            shape((rows, width), BF16),
        ),
        in_specs=[vm] * 5 + [pl.BlockSpec(memory_space=pltpu.SMEM)],
        out_specs=(vm,) * 7,
        scratch_shapes=[
            pltpu.VMEM((heads, 1, rows), F32),
            pltpu.VMEM((heads, 1, rows), F32),
            pltpu.VMEM((feats, rows), F32),
            sems, sems, sems, sems,
        ],
        compiler_params=pltpu.CompilerParams(collective_id=1, has_side_effects=True, vmem_limit_bytes=60 * 2**20),
        cost_estimate=pl.CostEstimate(flops=4 * 10**10, bytes_accessed=10**7, transcendentals=0),
        name="attend_forward",
    )(tokens, w_attn, attn_bias, norm_gains, norm_shifts, branch)


def flip(index, bit):
    return index + bit * (1 - 2 * lax.rem(lax.div(index, bit), 2))


def log_bits(size):
    return [1 << k for k in range(size.bit_length() - 1)]


class Links:
    def __init__(self, n, dp_count, x_send, x_recv, z_send, z_recv):
        self.z, self.dp = lax.axis_index("seq"), lax.axis_index("dp")
        self.n, self.dp_count, self.bits = n, dp_count, len(log_bits(dp_count))
        self.x_send, self.x_recv, self.z_send, self.z_recv = x_send, x_recv, z_send, z_recv


class Scatter:
    def __init__(self, links, number, source, xo, xi, acc, zo, zi, out):
        self.links, self.number, self.source, self.xo, self.xi = links, number, source, xo, xi
        self.acc, self.zo, self.zi, self.out = acc, zo, zi, out
        self.n, self.bits, self.z = links.n, links.bits, links.z
        self.blocks = links.dp_count * links.n

    def mine(self, s):
        return lax.rem(lax.div(self.links.dp, self.links.dp_count >> (s + 1)), 2)

    def start_of(self, s):
        return self.blocks - (self.blocks >> s)

    def held(self, s):
        return self.source if s == 0 else self.acc

    def x_copy(self, s, j=None):
        half, start, links = self.blocks >> (s + 1), self.start_of(s), self.links
        sem = self.number * (self.bits - 1 + self.n) + (self.n + s if j is None else j)
        part = pl.ds(start, half) if j is None else start + j
        return remote(
            self.xo.at[part], self.xi.at[part], links.x_send.at[sem], links.x_recv.at[sem],
            {"dp": flip(links.dp, links.dp_count >> (s + 1))},
        )

    def x_begin(self, s=0):
        half, start, held = self.blocks >> (s + 1), self.start_of(s), self.held(s)
        other = (1 - self.mine(s)) * half
        if s == self.bits - 1:
            for d in range(self.n):
                j = lax.rem(self.z + 1 + d, self.n)
                self.xo[start + j] = held[other + j].astype(BF16)
                self.x_copy(s, j).start()
            return

        def body(j, carry):
            self.xo[start + j] = held[other + j].astype(BF16)
            return carry

        lax.fori_loop(0, half, body, 0)
        self.x_copy(s).start()

    def relay(self, part=None):
        part = range(self.n) if part is None else part
        if 0 in part:
            for s in range(self.bits - 1):
                half, start, held = self.blocks >> (s + 1), self.start_of(s), self.held(s)
                own = self.mine(s) * half
                self.x_copy(s).wait_recv()

                def body(j, carry):
                    self.acc[j] = held[own + j] + self.xi[start + j].astype(F32)
                    return carry

                lax.fori_loop(0, half, body, 0)
                self.x_begin(s + 1)
        s = self.bits - 1
        own = self.mine(s) * self.n
        for d in part:
            j = lax.rem(self.z + 1 + d, self.n)
            self.x_copy(s, j).wait_recv()
            value = self.held(s)[own + j] + self.xi[self.start_of(s) + j].astype(F32)
            if d < self.n - 1:
                self.zo[j] = value.astype(BF16)
                self.z_copy(j, self.z).start()
            else:
                self.out[...] = value

    def z_copy(self, target, sender):
        base, links = self.number * self.n, self.links
        return remote(
            self.zo.at[target], self.zi.at[sender], links.z_send.at[base + target], links.z_recv.at[base + sender],
            {"seq": target},
        )

    def z_end(self):
        for d in range(1, self.n):
            i = lax.rem(self.z + d, self.n)
            self.z_copy(i, i).wait_recv()
            self.out[...] += self.zi[i].astype(F32)

    def drain(self):
        for s in range(self.bits - 1):
            self.x_copy(s).wait_send()
        for j in range(self.n):
            self.x_copy(self.bits - 1, j).wait_send()
        for d in range(1, self.n):
            self.z_copy(lax.rem(self.z + d, self.n), self.z).wait_send()


def scatter_buffers(n, dp_count, rows, columns):
    blocks = dp_count * n
    return [
        pltpu.VMEM((max(blocks - n, 1), rows, columns), BF16),
        pltpu.VMEM((max(blocks - n, 1), rows, columns), BF16),
        pltpu.VMEM((blocks // 2 if dp_count > 2 else 1, rows, columns), F32),
        pltpu.VMEM((n, rows, columns), BF16),
        pltpu.VMEM((n, rows, columns), BF16),
    ]


def scatter_sems(n, dp_count, count):
    over_dp = pltpu.SemaphoreType.DMA((count * (len(log_bits(dp_count)) - 1 + n),))
    over_seq = pltpu.SemaphoreType.DMA((count * n,))
    return [over_dp, over_dp, over_seq, over_seq]


def remote(src, dst, send, recv, to):
    return pltpu.make_async_remote_copy(
        src_ref=src, dst_ref=dst, send_sem=send, recv_sem=recv, device_id=to,
        device_id_type=pl.DeviceIdType.MESH,
    )


def finish_kernel(
    n, dp_count, heads, layer_scale,
    q_ref, kv_ref, all_ref, branch_ref, do_ref, of_ref, lse_ref, far_ref,
    near_any, exp_any, proj_any, early_any, esum_any, wa_any, normed_any, tok_any, ghid_any, gain_any,
    lout_ref, gtok_ref, exp_out, proj_out, query_out, keyval_out, sums_ref,
    dq_acc, own_acc, far_up, far_down, lse_sc, dot_sc, up_out, up_in, down_out, down_in,
    near_ref, exp_ref, proj_ref, early_ref, esum_ref, wa_ref, normed_ref, tok_ref, ghid_ref, gain_ref,
    stacked, mix, xhat_sc, inv_sc, query_sc, keyval_sc,
    exp_xo, exp_xi, exp_acc, exp_zo, exp_zi,
    proj_xo, proj_xi, proj_acc, proj_zo, proj_zi,
    query_xo, query_xi, query_acc, query_zo, query_zi,
    keyval_xo, keyval_xi, keyval_acc, keyval_zo, keyval_zi,
    core_out, core_in, y_out, y_in, far_in, seq_in, tensor_in, dp_out, dp_in,
    up_send, up_recv, down_send, down_recv, x_send, x_recv, z_send, z_recv,
    core_send, core_recv, y_send, y_recv, seq_send, seq_recv, tensor_send, tensor_recv, dp_send, dp_recv,
    fetch_sem,
):
    z = lax.axis_index("seq")
    t = lax.axis_index("tensor")
    dp = lax.axis_index("dp")
    feats = heads * HEAD_DIM
    share = ghid_ref.shape[0]
    has_up, has_down = z < n - 1, z > 0
    dp_bits = log_bits(dp_count)
    bits = len(dp_bits)
    blocks = dp_count * n
    mesh_ids = pl.DeviceIdType.MESH

    fetches = [
        pltpu.make_async_copy(src, dst, fetch_sem.at[i])
        for i, (src, dst) in enumerate(
            [
                (proj_any, proj_ref), (exp_any, exp_ref), (normed_any, normed_ref), (tok_any, tok_ref),
                (wa_any, wa_ref), (near_any, near_ref), (ghid_any, ghid_ref), (early_any, early_ref),
                (esum_any, esum_ref), (gain_any, gain_ref),
            ]
        )
    ]
    for one in fetches:
        one.start()

    barrier = pltpu.get_barrier_semaphore()
    seq_peers = [{"seq": lax.rem(z + d, n)} for d in range(1, n)]
    tensor_peers = [{"tensor": lax.rem(t + d, 4)} for d in range(1, 4)]
    dp_peers = [{"dp": flip(dp, bit)} for bit in dp_bits]
    for peer in seq_peers + tensor_peers + dp_peers:
        pl.semaphore_signal(barrier, inc=1, device_id=peer, device_id_type=mesh_ids)
    pl.semaphore_wait(barrier, n + 2 + bits)

    links = Links(n, dp_count, x_send, x_recv, z_send, z_recv)
    expand = Scatter(links, 0, exp_ref, exp_xo, exp_xi, exp_acc, exp_zo, exp_zi, exp_out)
    project = Scatter(links, 1, proj_ref, proj_xo, proj_xi, proj_acc, proj_zo, proj_zi, proj_out)
    query = Scatter(links, 2, query_sc, query_xo, query_xi, query_acc, query_zo, query_zi, query_out)
    keyval = Scatter(links, 3, keyval_sc, keyval_xo, keyval_xi, keyval_acc, keyval_zo, keyval_zi, keyval_out)
    scatters = (expand, project, query, keyval)

    sibling, partner = {"tensor": flip(t, 1)}, {"tensor": flip(t, 2)}
    far_copy = remote(far_ref, far_in, y_send.at[0], y_recv.at[0], partner)
    far_copy.start()
    fetches[1].wait()
    expand.x_begin()
    fetches[0].wait()
    project.x_begin()

    def hop(out, inn, d, to, send, recv):
        return remote(out.at[d], inn.at[d], send.at[d], recv.at[d], {"seq": to})

    dq_acc[...] = jnp.zeros_like(dq_acc)
    for h in range(heads):
        rows = slice(h * HEAD_DIM, (h + 1) * HEAD_DIM)
        lse_sc[h] = lse_ref[h:h + 1, :]
        dot_sc[h] = jnp.sum(do_ref[rows, :].astype(F32) * of_ref[rows, :], axis=0, keepdims=True)

    nt = (((1,), (1,)), ((), ()))
    tn = (((0,), (0,)), ((), ()))

    def tile(h, cols, k, v, mask):
        rows = pl.ds(pl.multiple_of(h * HEAD_DIM, HEAD_DIM), HEAD_DIM)
        q, do = q_ref[rows, cols], do_ref[rows, cols]
        s = mask(lax.dot_general(k, q, tn, preferred_element_type=F32))
        p = jnp.exp(s - lse_sc[h, :, cols])
        dp = lax.dot_general(v, do, tn, preferred_element_type=F32)
        ds = (p * (dp - dot_sc[h, :, cols])).astype(BF16)
        p = p.astype(BF16)
        dv = lax.dot_general(do, p, nt, preferred_element_type=F32)
        dk = lax.dot_general(q, ds, nt, preferred_element_type=F32)
        dq_acc[rows, cols] += jnp.dot(k, ds, preferred_element_type=F32)
        return dk, dv

    def head_rows(h):
        return (pl.ds(pl.multiple_of(h * HEAD_DIM, HEAD_DIM), HEAD_DIM),
                pl.ds(pl.multiple_of(feats + h * HEAD_DIM, HEAD_DIM), HEAD_DIM))

    def columns(c):
        return pl.ds(pl.multiple_of(c * PCH, PCH), PCH)

    branch = branch_ref[0, 0]

    def full(source, c, block, total):
        limit = jnp.where(c == 0, n * PCH, branch) - block * PCH
        def mask(s):
            key = lax.broadcasted_iota(jnp.int32, (PCH, 1), 0)
            return s + jnp.where(key < limit, 0.0, big_negative)
        def body(h, carry):
            rows, vrows = head_rows(h)
            dk, dv = tile(h, columns(c), source[rows, :], source[vrows, :], mask)
            total[rows, :] += dk
            total[vrows, :] += dv
            return carry
        lax.fori_loop(0, heads, body, 0)

    def diag(i, carry):
        c, h = i // heads, i % heads
        rows, vrows = head_rows(h)
        cols = columns(c)
        def mask(s):
            key = lax.broadcasted_iota(jnp.int32, s.shape, 0)
            query = lax.broadcasted_iota(jnp.int32, s.shape, 1)
            return jnp.where(key <= query, s, big_negative)
        dk, dv = tile(h, cols, kv_ref[rows, cols], kv_ref[vrows, cols], mask)
        own_acc[rows, cols] = dk
        own_acc[vrows, cols] = dv
        return carry

    def far_blocks(i, carry):
        d = n - 1 - i

        @pl.when(z + d < n)
        def _():
            far_up[d - 1] = jnp.zeros(far_up.shape[1:], F32)
            full(all_ref.at[z + d], 1, z + d, far_up.at[d - 1])
            @pl.when(~has_down | (d == n - 1))
            def _():
                up_out[d - 1] = far_up[d - 1].astype(BF16)
                hop(up_out, up_in, d - 1, z + 1, up_send, up_recv).start()

        @pl.when(z >= d)
        def _():
            far_down[d - 1] = jnp.zeros(far_down.shape[1:], F32)
            def both(c, carry):
                full(all_ref.at[z - d], c, z - d, far_down.at[d - 1])
                return carry
            lax.fori_loop(0, 2, both, 0)
            @pl.when(~has_up | (d == n - 1))
            def _():
                down_out[d - 1] = far_down[d - 1].astype(BF16)
                hop(down_out, down_in, d - 1, z - 1, down_send, down_recv).start()
        return carry

    lax.fori_loop(0, n - 1, far_blocks, 0)

    def relays(i, carry):
        d = n - 2 - i

        @pl.when(d == 1)
        def _():
            expand.relay()
            lax.fori_loop(0, 2 * heads, diag, 0)
            full(kv_ref.at[:, 0:PCH], 1, z, own_acc.at[:, 0:PCH])

        @pl.when((z + d < n) & has_down)
        def _():
            hop(up_out, up_in, d, z, up_send, up_recv).wait_recv()
            up_out[d - 1] = (far_up[d - 1] + up_in[d].astype(F32)).astype(BF16)
            hop(up_out, up_in, d - 1, z + 1, up_send, up_recv).start()

        @pl.when((z >= d) & has_up)
        def _():
            hop(down_out, down_in, d, z, down_send, down_recv).wait_recv()
            down_out[d - 1] = (far_down[d - 1] + down_in[d].astype(F32)).astype(BF16)
            hop(down_out, down_in, d - 1, z - 1, down_send, down_recv).start()
        return carry

    lax.fori_loop(0, n - 2, relays, 0)
    project.relay()

    def place(k):
        owner = t
        for bit in (1, 2):
            turned = flip(owner, bit)
            if isinstance(k, int):
                owner = turned if k & bit else owner
            else:
                owner = jnp.where(lax.rem(lax.div(k, bit), 2) == 1, turned, owner)
        return pl.ds(pl.multiple_of(owner * share, share), share)

    rows = query_sc.shape[1]

    def weight_gradient(part, target):
        value = jnp.dot(part, normed_ref[...], preferred_element_type=F32).T
        for b in range(blocks):
            target[b] = value[b * rows : (b + 1) * rows, :]

    stacked[0:feats, :] = (dq_acc[...] * (1.0 / math.sqrt(HEAD_DIM))).astype(BF16)
    for one in fetches[2:]:
        one.wait()
    weight_gradient(stacked[0:feats, :], query_sc)
    query.x_begin()
    stacked[feats:, PCH:] = own_acc[:, PCH:].astype(BF16)

    def prepare(k, carry):
        value = tok_ref[place(k), :].astype(F32)
        centred = value - jnp.mean(value, axis=-1, keepdims=True)
        inverse = lax.rsqrt(jnp.mean(centred * centred, axis=-1, keepdims=True) + norm_eps)
        xhat_sc[k] = centred * inverse
        inv_sc[k] = jnp.broadcast_to(inverse, (share, 128))
        return carry

    lax.fori_loop(0, 4, prepare, 0)

    @pl.when(has_down)
    def _():
        hop(up_out, up_in, 0, z, up_send, up_recv).wait_recv()
        own_acc[:, 0:PCH] += up_in[0].astype(F32)
    @pl.when(has_up)
    def _():
        hop(down_out, down_in, 0, z, down_send, down_recv).wait_recv()
        own_acc[:, 0:PCH] += down_in[0].astype(F32)
    stacked[feats:, 0:PCH] = own_acc[:, 0:PCH].astype(BF16)

    weight_gradient(stacked[feats:, :], keyval_sc)
    keyval.x_begin()

    def grad_normed(k):
        mix[k] = lax.dot_general(stacked[:, place(k)], wa_ref[...], tn, preferred_element_type=F32)
        return mix[k]

    def core_copy(i):
        return remote(core_out.at[i], core_in.at[i], core_send.at[i], core_recv.at[i], sibling)

    core_out[0] = grad_normed(3).astype(BF16)
    core_copy(0).start()
    last = grad_normed(2)
    core_copy(0).wait_recv()
    y_out[...] = (last + core_in[0].astype(F32)).astype(BF16)
    y_copy = remote(y_out, y_in, y_send.at[1], y_recv.at[1], partner)
    y_copy.start()
    core_out[1] = grad_normed(1).astype(BF16)
    core_copy(1).start()
    query.relay()
    grad_normed(0)

    width = seq_in.shape[2]
    seq_in[z, 0:2, :] = jnp.zeros((2, width), F32)
    seq_in[z, 2:6, :] = early_ref[...]
    seq_in[z, 6:7, :] = esum_ref[...]
    seq_in[z, 7:8, :] = jnp.zeros((1, width), F32)
    ones = jnp.ones((8, stacked.shape[1]), BF16)
    seq_in[z, 7:8, 0 : 3 * feats] = lax.dot_general(ones, stacked[...], nt, preferred_element_type=F32)[0:1]

    def statistics(k, carry):
        seq_in[z, 0:1, :] += jnp.sum(mix[k] * xhat_sc[k], axis=0, keepdims=True)
        seq_in[z, 1:2, :] += jnp.sum(mix[k], axis=0, keepdims=True)
        return carry

    lax.fori_loop(0, 4, statistics, 0)

    def seq_copy(target, sender):
        return remote(seq_in.at[z], seq_in.at[sender], seq_send.at[target], seq_recv.at[sender], {"seq": target})

    def tensor_copy(target, sender):
        return remote(
            tensor_in.at[t], tensor_in.at[sender], tensor_send.at[target], tensor_recv.at[sender],
            {"tensor": target},
        )

    def dp_copy(i):
        return remote(dp_out.at[i], dp_in.at[i], dp_send.at[i], dp_recv.at[i], dp_peers[i])

    for d in range(1, n):
        seq_copy(lax.rem(z + d, n), z).start()
    keyval.relay()
    far_copy.wait_recv()
    lout_ref[...] = (near_ref[...] + layer_scale * far_in[...].astype(F32)).astype(BF16)
    for d in range(1, n):
        other = lax.rem(z + d, n)
        seq_copy(other, other).wait_recv()
    summed = seq_in[0]
    for i in range(1, n):
        summed = summed + seq_in[i]
    tensor_in[t] = summed
    for d in range(1, 4):
        tensor_copy(lax.rem(t + d, 4), t).start()
    for d in range(1, 4):
        other = lax.rem(t + d, 4)
        tensor_copy(other, other).wait_recv()
    total = tensor_in[0]
    for i in range(1, 4):
        total = total + tensor_in[i]
    own = tensor_in[t]
    row = lax.broadcasted_iota(jnp.int32, own.shape, 0)
    dp_out[0] = jnp.where(row < 6, total, own)
    dp_copy(0).start()
    expand.z_end()
    project.z_end()

    core_copy(1).wait_recv()
    y_copy.wait_recv()
    mixed = mix[0] + core_in[1].astype(F32) + y_in[...].astype(F32)
    e = mixed * gain_ref[0:1, :]
    xhat = xhat_sc[0]
    gtok_ref[...] = (
        ghid_ref[...]
        + inv_sc[0][:, 0:1]
        * (e - jnp.mean(e, axis=-1, keepdims=True) - xhat * jnp.mean(e * xhat, axis=-1, keepdims=True))
    ).astype(BF16)
    query.z_end()
    for i in range(bits):
        dp_copy(i).wait_recv()
        value = dp_out[i] + dp_in[i]
        if i + 1 < bits:
            dp_out[i + 1] = value
            dp_copy(i + 1).start()
        else:
            sums_ref[...] = value
    keyval.z_end()

    for d in range(1, n):
        @pl.when(z + d < n)
        def _(): hop(up_out, up_in, d - 1, z + 1, up_send, up_recv).wait_send()
        @pl.when(z >= d)
        def _(): hop(down_out, down_in, d - 1, z - 1, down_send, down_recv).wait_send()
    for one in scatters:
        one.drain()
    far_copy.wait_send()
    y_copy.wait_send()
    for i in range(2):
        core_copy(i).wait_send()
    for d in range(1, n):
        seq_copy(lax.rem(z + d, n), z).wait_send()
    for d in range(1, 4):
        tensor_copy(lax.rem(t + d, 4), t).wait_send()
    for i in range(bits):
        dp_copy(i).wait_send()


def finish(
    n, dp_count, layer_scale, q, kv, kv_all, branch, do, of, lse, near, far,
    grad_expand, grad_proj, early, expand_terms, w_attn, normed_one, token_rows,
    grad_hidden, norm_gains,
):
    feats, rows = q.shape
    heads = feats // HEAD_DIM
    share, width = grad_hidden.shape
    blocks = dp_count * n
    bits = len(log_bits(dp_count))
    vm = pl.BlockSpec(memory_space=pltpu.VMEM)
    anywhere = pl.BlockSpec(memory_space=pl.ANY)
    slots = pltpu.VMEM((n - 1, 2 * feats, PCH), BF16)
    shape = jax.ShapeDtypeStruct
    sems = lambda count: pltpu.SemaphoreType.DMA((count,))
    block_rows = width // blocks
    proj_blocks = grad_proj.reshape(blocks, block_rows, feats)
    units = grad_expand.shape[1]
    fetched = [
        near, grad_expand.reshape(blocks, block_rows, units), proj_blocks, early, expand_terms, w_attn, normed_one, token_rows,
        grad_hidden, norm_gains,
    ]
    widths = [units, feats, feats, 2 * feats]
    scatter_scratch = []
    for columns in widths:
        scatter_scratch += scatter_buffers(n, dp_count, block_rows, columns)
    return pl.pallas_call(
        functools.partial(finish_kernel, n, dp_count, heads, layer_scale),
        out_shape=(
            shape((share, width), BF16),
            shape((share, width), BF16),
            *(shape((block_rows, columns), F32) for columns in widths),
            shape((8, width), F32),
        ),
        in_specs=[vm, vm, vm, pl.BlockSpec(memory_space=pltpu.SMEM)] + [vm] * 4 + [anywhere] * len(fetched),
        out_specs=(vm,) * 7,
        scratch_shapes=[
            pltpu.VMEM((feats, rows), F32),
            pltpu.VMEM((2 * feats, rows), F32),
            pltpu.VMEM((n - 1, 2 * feats, PCH), F32),
            pltpu.VMEM((n - 1, 2 * feats, PCH), F32),
            pltpu.VMEM((heads, 1, rows), F32),
            pltpu.VMEM((heads, 1, rows), F32),
            slots, slots, slots, slots,
            *(pltpu.VMEM(one.shape, one.dtype) for one in fetched),
            pltpu.VMEM((3 * feats, rows), BF16),
            pltpu.VMEM((4, share, width), F32),
            pltpu.VMEM((4, share, width), F32),
            pltpu.VMEM((4, share, 128), F32),
            pltpu.VMEM((blocks, block_rows, feats), F32),
            pltpu.VMEM((blocks, block_rows, 2 * feats), F32),
            *scatter_scratch,
            pltpu.VMEM((2, share, width), BF16),
            pltpu.VMEM((2, share, width), BF16),
            pltpu.VMEM((share, width), BF16),
            pltpu.VMEM((share, width), BF16),
            pltpu.VMEM((share, width), BF16),
            pltpu.VMEM((n, 8, width), F32),
            pltpu.VMEM((4, 8, width), F32),
            pltpu.VMEM((bits, 8, width), F32),
            pltpu.VMEM((bits, 8, width), F32),
            sems(n - 1), sems(n - 1), sems(n - 1), sems(n - 1),
            *scatter_sems(n, dp_count, 4),
            sems(2), sems(2), sems(2), sems(2), sems(n), sems(n), sems(4), sems(4), sems(bits), sems(bits),
            sems(len(fetched)),
        ],
        compiler_params=pltpu.CompilerParams(
            collective_id=2, has_side_effects=True, vmem_limit_bytes=60 * 2**20
        ),
        cost_estimate=pl.CostEstimate(flops=4 * 10**10, bytes_accessed=10**7, transcendentals=0),
        name="finish",
    )(q, kv, kv_all, branch, do, of, lse, far, *fetched)


def emit_kernel(
    feats, turned, con, lout, gtok, expand, proj, query, keyval, sums,
    lout_ref, gtok_ref, attn_ref, proj_ref, exp_ref, con_ref, bias_ref, branch_ref, units_ref, gains_ref, shifts_ref,
):
    lout_ref[...] = lout[...]
    gtok_ref[...] = gtok[...]
    attn_ref[0] = query[...]
    attn_ref[1] = keyval[:, 0:feats]
    attn_ref[2] = keyval[:, feats : 2 * feats]
    proj_ref[...] = proj[...].T if turned else proj[...]
    exp_ref[...] = expand[...]
    con_ref[...] = con[...]
    bias_ref[0:1, :] = sums[7:8, 0:feats]
    bias_ref[1:2, :] = sums[7:8, 2 * feats : 3 * feats]
    branch_ref[...] = sums[2:4, :]
    units_ref[...] = sums[6:7, :]
    for row, late, early in ((gains_ref, 0, 4), (shifts_ref, 1, 5)):
        row[0:1, :] = sums[late : late + 1, :]
        row[1:2, :] = sums[early : early + 1, :]


def emit(con, results):
    lout, gtok, expand, proj, query, keyval, sums = results
    rows, feats = query.shape
    share, width = lout.shape
    turned = rows % 8 == 0
    shape = jax.ShapeDtypeStruct
    vm = pl.BlockSpec(memory_space=pltpu.VMEM)
    outputs = pl.pallas_call(
        functools.partial(emit_kernel, feats, turned),
        out_shape=(
            shape((share, width), BF16), shape((share, width), BF16), shape((3, rows, feats), F32),
            shape((feats, rows) if turned else (rows, feats), F32), shape(expand.shape, F32),
            shape(con.shape, F32), shape((2, feats), F32), shape((2, width), F32),
            shape((1, expand.shape[1]), F32), shape((2, width), F32), shape((2, width), F32),
        ),
        in_specs=[vm] * 8,
        out_specs=(vm,) * 11,
        compiler_params=pltpu.CompilerParams(vmem_limit_bytes=60 * 2**20),
        name="emit",
    )(con, *results)
    lout, gtok, attn, proj, expand, con, bias, branch, units, gains, shifts = outputs
    whole = (1, 1, share, width)
    return (
        lout.reshape(whole), gtok.reshape(whole), attn, proj if turned else proj.T, expand, con.T,
        bias, branch, units.reshape(-1), gains, shifts,
    )


def middle_kernel(
    n, dp_count, layer_scale, o_ref, tok_ref, cot_ref, wp_ref, we_ref, wc_ref, bb_ref, eb_ref, gain_ref, shift_ref,
    ghid_ref, near_ref, far_ref, gatt_ref, gproj_ref, gexp_ref, gcon_ref, sums_ref, esum_ref,
    ga_sc, mix_sc, n2, gm, act, gp, att, own_sc, xhat_sc, inv_sc, proj_sc,
    core_out, core_in, y_out, y_in, con_sc, con_xo, con_xi, con_acc, con_zo, con_zi,
    core_send, core_recv, y_send, y_recv, n2_send, n2_recv, att_send, att_recv, x_send, x_recv, z_send, z_recv,
):
    t = lax.axis_index("tensor")
    y, c = t // 2, t % 2
    sibling = y * 2 + (1 - c)
    partner = (1 - y) * 2 + c
    share = own_sc.shape[0]

    def block(k):
        if isinstance(k, int):
            return ((1 - y) if k >= 2 else y) * 2 + ((1 - c) if k % 2 else c)
        return jnp.where(k >= 2, 1 - y, y) * 2 + jnp.where(k % 2 == 1, 1 - c, c)

    def place(k):
        return pl.ds(pl.multiple_of(block(k) * share, share), share)

    barrier = pltpu.get_barrier_semaphore()
    for to in (sibling, partner):
        pl.semaphore_signal(barrier, inc=1, device_id={"tensor": to}, device_id_type=pl.DeviceIdType.MESH)
    links = Links(n, dp_count, x_send, x_recv, z_send, z_recv)
    peers = [{"seq": lax.rem(links.z + d, n)} for d in range(1, n)]
    peers += [{"dp": flip(links.dp, bit)} for bit in log_bits(dp_count)]
    for peer in peers:
        pl.semaphore_signal(barrier, inc=1, device_id=peer, device_id_type=pl.DeviceIdType.MESH)
    pl.semaphore_wait(barrier, 2 + len(peers))
    weights = Scatter(links, 0, con_sc, con_xo, con_xi, con_acc, con_zo, con_zi, gcon_ref)

    def copy(src, dst, send, recv, to):
        return pltpu.make_async_remote_copy(
            src_ref=src, dst_ref=dst, send_sem=send, recv_sem=recv,
            device_id={"tensor": to}, device_id_type=pl.DeviceIdType.MESH,
        )

    def core_copy(i):
        return copy(core_out.at[i], core_in.at[i], core_send.at[i], core_recv.at[i], sibling)

    def y_copy(i):
        return copy(y_out.at[i], y_in.at[i], y_send.at[i], y_recv.at[i], partner)

    def gather(ref, send, recv):
        return (
            copy(ref.at[0], ref.at[2], send.at[0], recv.at[0], partner),
            copy(ref.at[0], ref.at[1], send.at[1], recv.at[1], sibling),
            copy(ref.at[2], ref.at[3], send.at[2], recv.at[2], sibling),
        )

    tn = (((0,), (0,)), ((), ()))
    nt = (((1,), (1,)), ((), ()))

    def project(k):
        return lax.dot_general(o_ref[:, place(k)], wp_ref[...], tn, preferred_element_type=F32)

    core_out[0] = project(3).astype(BF16)
    core_copy(0).start()
    own_sc[...] = project(2)
    core_out[1] = project(1).astype(BF16)
    core_copy(1).start()
    core_copy(0).wait_recv()
    y_out[0] = (own_sc[...] + core_in[0].astype(F32)).astype(BF16)
    y_copy(0).start()
    own_sc[...] = project(0)

    def before(k, carry):
        g = (cot_ref[place(k), :].astype(F32) * layer_scale).astype(BF16)
        gm[k] = g
        ga_sc[k] = lax.dot_general(g, wc_ref[...], nt, preferred_element_type=F32)
        return carry

    lax.fori_loop(0, 4, before, 0)
    core_copy(1).wait_recv()
    own_sc[...] += core_in[1].astype(F32)
    y_copy(0).wait_recv()

    hidden = tok_ref[place(0), :].astype(F32) + layer_scale * (
        own_sc[...] + y_in[0].astype(F32) + bb_ref[0:1, :]
    )
    near_ref[...] = hidden + layer_scale * bb_ref[1:2, :]
    centred = hidden - jnp.mean(hidden, axis=-1, keepdims=True)
    inverse = lax.rsqrt(jnp.mean(centred * centred, axis=-1, keepdims=True) + norm_eps)
    xhat = centred * inverse
    n2[0] = (xhat * gain_ref[1:2, :] + shift_ref[1:2, :]).astype(BF16)
    across, near, on = gather(n2, n2_send, n2_recv)
    across.start()
    near.start()
    xhat_sc[...] = xhat
    inv_sc[...] = jnp.broadcast_to(inverse, inv_sc.shape)
    esum_ref[...] = jnp.zeros_like(esum_ref)

    def process(k, carry):
        @pl.when(k == 1)
        def _():
            near.wait_recv()

        @pl.when(k == 2)
        def _():
            across.wait_recv()
            on.start()

        @pl.when(k == 3)
        def _():
            on.wait_recv()

        v = jnp.dot(n2[k], we_ref[...], preferred_element_type=F32) + eb_ref[...]
        square = v * v
        th = jnp.tanh(math.sqrt(2.0 / math.pi) * (v + 0.044715 * (v * square)))
        cdf = 0.5 * (1.0 + th)
        act[k] = (v * cdf).astype(BF16)
        slope = cdf + 0.5 * v * (1.0 - th * th) * (
            math.sqrt(2.0 / math.pi) * (1.0 + 3 * 0.044715 * square)
        )
        g = (slope * ga_sc[k]).astype(BF16)
        gp[k] = g
        esum_ref[...] += jnp.sum(g.astype(F32), axis=0, keepdims=True)
        mix_sc[k] = lax.dot_general(g, we_ref[...], nt, preferred_element_type=F32)
        return carry

    lax.fori_loop(0, 4, process, 0)
    core_out[2] = mix_sc[3].astype(BF16)
    core_copy(2).start()
    core_out[3] = mix_sc[1].astype(BF16)
    core_copy(3).start()
    core_copy(2).wait_recv()
    y_out[1] = (mix_sc[2] + core_in[2].astype(F32)).astype(BF16)
    y_copy(1).start()

    rows = 4 * share
    width = gm.shape[2]
    value = lax.dot_general(
        gm[...].reshape(rows, width), act[...].reshape(rows, -1), tn, preferred_element_type=F32
    )
    size = con_sc.shape[1]
    for b in range(con_sc.shape[0]):
        con_sc[b] = value[b * size : (b + 1) * size, :]
    weights.x_begin()
    gexp_ref[...] = lax.dot_general(
        n2[...].reshape(rows, width), gp[...].reshape(rows, -1), tn, preferred_element_type=F32
    )

    def contract(k):
        return jnp.dot(act[k], wc_ref[...], preferred_element_type=F32)

    core_out[4] = contract(3).astype(BF16)
    core_copy(4).start()
    core_out[5] = contract(1).astype(BF16)
    core_copy(5).start()
    near_ref[...] += layer_scale * contract(0)
    last = contract(2)
    core_copy(4).wait_recv()
    far_ref[...] = (last + core_in[4].astype(F32)).astype(BF16)
    core_copy(5).wait_recv()
    near_ref[...] += layer_scale * core_in[5].astype(F32)
    weights.relay(range(0, 1))

    core_copy(3).wait_recv()
    mixed = mix_sc[0] + core_in[3].astype(F32)
    y_copy(1).wait_recv()
    mixed = mixed + y_in[1].astype(F32)
    e = mixed * gain_ref[1:2, :]
    xhat = xhat_sc[...]
    grad_hidden = cot_ref[place(0), :].astype(F32) + inv_sc[:, 0:1] * (
        e - jnp.mean(e, axis=-1, keepdims=True) - xhat * jnp.mean(e * xhat, axis=-1, keepdims=True)
    )
    g = (grad_hidden * layer_scale).astype(BF16)
    att[0] = g
    across_b, near_b, on_b = gather(att, att_send, att_recv)
    across_b.start()
    near_b.start()
    ghid_ref[...] = grad_hidden
    sums_ref[0:1, :] = jnp.sum(g.astype(F32), axis=0, keepdims=True)
    sums_ref[1:2, :] = jnp.sum(gm[0].astype(F32), axis=0, keepdims=True)
    sums_ref[2:3, :] = jnp.sum(mixed * xhat, axis=0, keepdims=True)
    sums_ref[3:4, :] = jnp.sum(mixed, axis=0, keepdims=True)

    proj_sc[...] = jnp.zeros_like(proj_sc)
    weights.relay(range(1, n))

    def after(k, carry):
        @pl.when(k == 1)
        def _():
            near_b.wait_recv()

        @pl.when(k == 2)
        def _():
            across_b.wait_recv()
            on_b.start()

        @pl.when(k == 3)
        def _():
            on_b.wait_recv()

        gatt_ref[:, place(k)] = lax.dot_general(
            wp_ref[...], att[k], nt, preferred_element_type=F32
        ).astype(BF16)
        proj_sc[...] += jnp.dot(o_ref[:, place(k)], att[k], preferred_element_type=F32)
        return carry

    lax.fori_loop(0, 4, after, 0)
    gproj_ref[...] = proj_sc[...].T
    weights.z_end()
    weights.drain()
    for i in range(6):
        core_copy(i).wait_send()
    for i in range(2):
        y_copy(i).wait_send()
    for one in (across, near, on, across_b, near_b, on_b):
        one.wait_send()


def middle(
    n, dp_count, layer_scale, attended, token_rows, cotangent_rows, w_proj, w_expand, w_contract,
    branch_bias, expand_bias, norm_gains, norm_shifts,
):
    rows, width = token_rows.shape
    feats, hidden_units = w_proj.shape[0], w_expand.shape[1]
    share = rows // 4
    size = width // (dp_count * n)
    vm = pl.BlockSpec(memory_space=pltpu.VMEM)
    shape = jax.ShapeDtypeStruct
    slots = lambda columns, kind: pltpu.VMEM((4, share, columns), kind)
    sems = lambda count: pltpu.SemaphoreType.DMA((count,))
    return pl.pallas_call(
        functools.partial(middle_kernel, n, dp_count, layer_scale),
        out_shape=(
            shape((share, width), F32),
            shape((share, width), F32),
            shape((share, width), BF16),
            shape((feats, rows), BF16),
            shape((width, feats), F32),
            shape((width, hidden_units), F32),
            shape((size, hidden_units), F32),
            shape((4, width), F32),
            shape((1, hidden_units), F32),
        ),
        in_specs=[vm] * 10,
        out_specs=(vm,) * 9,
        scratch_shapes=[
            slots(hidden_units, F32),
            slots(width, F32),
            slots(width, BF16),
            slots(width, BF16),
            slots(hidden_units, BF16),
            slots(hidden_units, BF16),
            slots(width, BF16),
            pltpu.VMEM((share, width), F32),
            pltpu.VMEM((share, width), F32),
            pltpu.VMEM((share, 128), F32),
            pltpu.VMEM((feats, width), F32),
            pltpu.VMEM((6, share, width), BF16),
            pltpu.VMEM((6, share, width), BF16),
            pltpu.VMEM((2, share, width), BF16),
            pltpu.VMEM((2, share, width), BF16),
            pltpu.VMEM((dp_count * n, size, hidden_units), F32),
            *scatter_buffers(n, dp_count, size, hidden_units),
            sems(6), sems(6), sems(2), sems(2), sems(3), sems(3), sems(3), sems(3),
            *scatter_sems(n, dp_count, 1),
        ],
        compiler_params=pltpu.CompilerParams(
            collective_id=3, has_side_effects=True, vmem_limit_bytes=56 * 2**20
        ),
        cost_estimate=pl.CostEstimate(flops=5 * 10**10, bytes_accessed=2 * 10**7, transcendentals=0),
        name="middle",
    )(
        attended, token_rows, cotangent_rows, w_proj, w_expand, w_contract,
        branch_bias, expand_bias, norm_gains, norm_shifts,
    )


def shards(
    tokens,
    branch,
    w_attn,
    w_proj,
    w_expand,
    w_contract,
    attn_bias,
    branch_bias,
    expand_bias,
    norm_gains,
    norm_shifts,
    cotangent,
):
    seq_count = lax.axis_size("seq")
    width = tokens.shape[3]
    row_count = tokens.shape[2]
    share = row_count // lax.axis_size("tensor")
    local_width = w_attn.shape[2]
    layer_scale = 1.0 / math.sqrt(LAYERS)

    token_rows = tokens.reshape(row_count, width)
    cotangent_rows = cotangent.reshape(row_count, width)
    w_attn = jnp.transpose(w_attn, (0, 2, 1)).reshape(3 * local_width, width)
    attended, attended_wide, logsum, all_kv, queries, own_kv, normed_one = attend_forward(
        seq_count, token_rows, w_attn, attn_bias, norm_gains, norm_shifts, branch
    )
    (
        grad_hidden, mlp_near, mlp_far, grad_attended,
        grad_proj, grad_expand, grad_contract, early, expand_terms,
    ) = middle(
        seq_count, lax.axis_size("dp"), layer_scale, attended, token_rows, cotangent_rows, w_proj, w_expand, w_contract,
        branch_bias, expand_bias.reshape(1, -1), norm_gains, norm_shifts,
    )
    return emit(grad_contract, finish(
        seq_count, lax.axis_size("dp"), layer_scale, queries, own_kv, all_kv, branch, grad_attended,
        attended_wide, logsum, mlp_near, mlp_far, grad_expand, grad_proj, early,
        expand_terms, w_attn, normed_one, token_rows, grad_hidden, norm_gains,
    ))


def solution(mesh):
    placed = (
        P("dp", "seq", None, None),
        P("dp", "seq"),
        P(None, None, "tensor"),
        P("tensor", None),
        P(None, "tensor"),
        P("tensor", None),
        P(None, "tensor"),
        P(),
        P("tensor"),
        P(),
        P(),
        P("dp", "seq", None, None),
    )
    return jax.shard_map(
        shards,
        mesh=mesh,
        in_specs=placed,
        out_specs=(
            P("dp", "seq", "tensor", None),
            P("dp", "seq", "tensor", None),
            P(None, ("dp", "seq"), "tensor"),
            P("tensor", ("dp", "seq")),
            P(("dp", "seq"), "tensor"),
            P("tensor", ("dp", "seq")),
            P(None, "tensor"),
            P(),
            P("tensor"),
            P(),
            P(),
        ),
        check_vma=False,
    )
```

```python
import functools
import math

import jax
import jax.numpy as jnp
from jax import lax
from jax.experimental import pallas as pl
from jax.experimental.pallas import tpu as pltpu
from jax.sharding import PartitionSpec as P

HEAD_DIM = 64
LAYERS = 12
PCH = 512
CLEN = 512
F32 = jnp.float32
BF16 = jnp.bfloat16


norm_eps = 1e-05
big_negative = -1000000000.0


def layer_norm_parts(value):
    centre = jnp.mean(value, axis=-1, keepdims=True)
    centred = value - centre
    spread = jnp.mean(centred * centred, axis=-1, keepdims=True)
    inverse = lax.rsqrt(spread + norm_eps)
    return centred * inverse, inverse


def forward_kernel(n, heads, tok_ref, wa_ref, bias_ref, gain_ref, shift_ref, branch_ref, o_ref, of_ref, lse_ref, kv_all, q_ref, kv_ref, normed_ref, m_sc, l_sc, acc, up_send, up_recv, down_send, down_recv):
    z = lax.axis_index("seq")
    feats = heads * HEAD_DIM
    barrier = pltpu.get_barrier_semaphore()
    has_up, has_down = z < n - 1, z > 0

    def meet(to):
        pl.semaphore_signal(barrier, inc=1, device_id={"seq": to}, device_id_type=pl.DeviceIdType.MESH)

    @pl.when(has_up)
    def _(): meet(z + 1)
    @pl.when(has_down)
    def _(): meet(z - 1)

    bias = [jnp.broadcast_to(bias_ref[i : i + 1, :], (8, feats)).T[:, 0:1] for i in range(2)]

    def project(first, cols):
        normed = normed_ref[cols, :]
        value = lax.dot_general(
            wa_ref[first * feats :, :] if first else wa_ref[0:feats, :], normed,
            (((1,), (1,)), ((), ())), preferred_element_type=F32,
        )
        return value

    def norm_rows(cols):
        value = layer_norm_parts(tok_ref[cols, :].astype(F32))[0]
        normed_ref[cols, :] = (value * gain_ref[0:1, :] + shift_ref[0:1, :]).astype(BF16)

    def keys_values(cols):
        value = project(1, cols)
        kv_ref[0:feats, cols] = value[0:feats].astype(BF16)
        kv_ref[feats:, cols] = (value[feats:] + bias[1]).astype(BF16)

    prompt_cols, other_cols = slice(0, PCH), slice(PCH, q_ref.shape[1])
    norm_rows(prompt_cols)
    keys_values(prompt_cols)
    pl.semaphore_wait(barrier, has_up.astype(jnp.int32) + has_down.astype(jnp.int32))

    own = kv_ref.at[:, 0:PCH]

    def hop(src, block, step, to, send, recv):
        return pltpu.make_async_remote_copy(src_ref=src, dst_ref=kv_all.at[block], send_sem=send.at[step], recv_sem=recv.at[step], device_id={"seq": to}, device_id_type=pl.DeviceIdType.MESH)

    @pl.when(has_up)
    def _(): hop(own, z, 0, z + 1, up_send, up_recv).start()
    @pl.when(has_down)
    def _(): hop(own, z, 0, z - 1, down_send, down_recv).start()

    norm_rows(other_cols)
    keys_values(other_cols)
    for cols in (prompt_cols, other_cols):
        value = (project(0, cols) + bias[0]).astype(BF16)
        q_ref[:, cols] = value * jnp.asarray(1.0 / math.sqrt(HEAD_DIM), BF16)

    def load_q(h, c):
        return q_ref[pl.ds(pl.multiple_of(h * HEAD_DIM, HEAD_DIM), HEAD_DIM), pl.ds(pl.multiple_of(c * PCH, PCH), PCH)]

    def scores(k, q):
        return lax.dot_general(k, q, (((0,), (0,)), ((), ())), preferred_element_type=F32)

    def diag(i, carry):
        c, h = i // heads, i % heads
        rows = pl.ds(pl.multiple_of(h * HEAD_DIM, HEAD_DIM), HEAD_DIM)
        vrows = pl.ds(pl.multiple_of(feats + h * HEAD_DIM, HEAD_DIM), HEAD_DIM)
        cols = pl.ds(pl.multiple_of(c * PCH, PCH), PCH)
        s = scores(kv_ref[rows, cols], load_q(h, c))
        key = lax.broadcasted_iota(jnp.int32, s.shape, 0)
        query = lax.broadcasted_iota(jnp.int32, s.shape, 1)
        s = jnp.where(key <= query, s, big_negative)
        m = jnp.max(s, axis=0, keepdims=True)
        p = jnp.exp(s - m)
        m_sc[h, :, cols] = m
        l_sc[h, :, cols] = jnp.sum(p, axis=0, keepdims=True)
        acc[rows, cols] = jnp.dot(kv_ref[vrows, cols], p.astype(BF16), preferred_element_type=F32)
        return carry
    lax.fori_loop(0, 2 * heads, diag, 0)

    branch = branch_ref[0, 0]

    def full(source, c, block):
        limit = jnp.where(c == 0, n * PCH, branch) - block * PCH
        def body(h, carry):
            rows = pl.ds(pl.multiple_of(h * HEAD_DIM, HEAD_DIM), HEAD_DIM)
            vrows = pl.ds(pl.multiple_of(feats + h * HEAD_DIM, HEAD_DIM), HEAD_DIM)
            cols = pl.ds(pl.multiple_of(c * PCH, PCH), PCH)
            s = scores(source[rows, :], load_q(h, c))
            key = lax.broadcasted_iota(jnp.int32, (PCH, 1), 0)
            s = s + jnp.where(key < limit, 0.0, big_negative)
            m_old = m_sc[h, :, cols]
            m = jnp.maximum(m_old, jnp.max(s, axis=0, keepdims=True))
            p = jnp.exp(s - m)
            alpha = jnp.exp(m_old - m)
            m_sc[h, :, cols] = m
            l_sc[h, :, cols] = l_sc[h, :, cols] * alpha + jnp.sum(p, axis=0, keepdims=True)
            acc[rows, cols] = acc[rows, cols] * alpha + jnp.dot(source[vrows, :], p.astype(BF16), preferred_element_type=F32)
            return carry
        lax.fori_loop(0, heads, body, 0)

    full(own, 1, z)

    def step_body(step, carry):
        @pl.when(z >= step)
        def _():
            hop(own, z - step, step - 1, z, up_send, up_recv).wait_recv()
            @pl.when(has_up & (step < n - 1))
            def _(): hop(kv_all.at[z - step], z - step, step, z + 1, up_send, up_recv).start()
        @pl.when(z + step < n)
        def _():
            hop(own, z + step, step - 1, z, down_send, down_recv).wait_recv()
            @pl.when(has_down & (step < n - 1))
            def _(): hop(kv_all.at[z + step], z + step, step, z - 1, down_send, down_recv).start()
        @pl.when(z >= step)
        def _():
            def both(c, carry):
                full(kv_all.at[z - step], c, z - step)
                return carry
            lax.fori_loop(0, 2, both, 0)
        @pl.when(z + step < n)
        def _(): full(kv_all.at[z + step], 1, z + step)
        return carry
    lax.fori_loop(1, n, step_body, 0)

    for h in range(heads):
        rows = slice(h * HEAD_DIM, (h + 1) * HEAD_DIM)
        total = l_sc[h]
        out = acc[rows, :] / total
        of_ref[rows, :] = out
        o_ref[rows, :] = out.astype(BF16)
        lse_ref[h:h + 1, :] = m_sc[h] + jnp.log(total)

    for step in range(n - 1):
        @pl.when(has_up & (z >= step))
        def _(): hop(own, z, step, z + 1, up_send, up_recv).wait_send()
        @pl.when(has_down & (z + step < n))
        def _(): hop(own, z, step, z - 1, down_send, down_recv).wait_send()

def attend_forward(n, tokens, w_attn, attn_bias, norm_gains, norm_shifts, branch):
    rows, width = tokens.shape
    feats = attn_bias.shape[1]
    heads = feats // HEAD_DIM
    vm = pl.BlockSpec(memory_space=pltpu.VMEM)
    shape = jax.ShapeDtypeStruct
    sems = pltpu.SemaphoreType.DMA((n - 1,))
    return pl.pallas_call(
        functools.partial(forward_kernel, n, heads),
        out_shape=(
            shape((feats, rows), BF16), shape((feats, rows), F32), shape((heads, rows), F32),
            shape((n, 2 * feats, PCH), BF16), shape((feats, rows), BF16), shape((2 * feats, rows), BF16),
            shape((rows, width), BF16),
        ),
        in_specs=[vm] * 5 + [pl.BlockSpec(memory_space=pltpu.SMEM)],
        out_specs=(vm,) * 7,
        scratch_shapes=[
            pltpu.VMEM((heads, 1, rows), F32),
            pltpu.VMEM((heads, 1, rows), F32),
            pltpu.VMEM((feats, rows), F32),
            sems, sems, sems, sems,
        ],
        compiler_params=pltpu.CompilerParams(collective_id=1, has_side_effects=True, vmem_limit_bytes=60 * 2**20),
        cost_estimate=pl.CostEstimate(flops=4 * 10**10, bytes_accessed=10**7, transcendentals=0),
        name="attend_forward",
    )(tokens, w_attn, attn_bias, norm_gains, norm_shifts, branch)


def flip(index, bit):
    return index + bit * (1 - 2 * lax.rem(lax.div(index, bit), 2))


def log_bits(size):
    return [1 << k for k in range(size.bit_length() - 1)]


class Links:
    def __init__(self, n, dp_count, x_send, x_recv, z_send, z_recv):
        self.z, self.dp = lax.axis_index("seq"), lax.axis_index("dp")
        self.n, self.dp_count, self.bits = n, dp_count, len(log_bits(dp_count))
        self.x_send, self.x_recv, self.z_send, self.z_recv = x_send, x_recv, z_send, z_recv


class Scatter:
    def __init__(self, links, number, source, xo, xi, acc, zo, zi, out):
        self.links, self.number, self.source, self.xo, self.xi = links, number, source, xo, xi
        self.acc, self.zo, self.zi, self.out = acc, zo, zi, out
        self.n, self.bits, self.z = links.n, links.bits, links.z
        self.blocks = links.dp_count * links.n

    def mine(self, s):
        return lax.rem(lax.div(self.links.dp, self.links.dp_count >> (s + 1)), 2)

    def start_of(self, s):
        return self.blocks - (self.blocks >> s)

    def held(self, s):
        return self.source if s == 0 else self.acc

    def x_copy(self, s, j=None):
        half, start, links = self.blocks >> (s + 1), self.start_of(s), self.links
        sem = self.number * (self.bits - 1 + self.n) + (self.n + s if j is None else j)
        part = pl.ds(start, half) if j is None else start + j
        return remote(
            self.xo.at[part], self.xi.at[part], links.x_send.at[sem], links.x_recv.at[sem],
            {"dp": flip(links.dp, links.dp_count >> (s + 1))},
        )

    def x_begin(self, s=0):
        half, start, held = self.blocks >> (s + 1), self.start_of(s), self.held(s)
        other = (1 - self.mine(s)) * half
        if s == self.bits - 1:
            for d in range(self.n):
                j = lax.rem(self.z + 1 + d, self.n)
                self.xo[start + j] = held[other + j].astype(BF16)
                self.x_copy(s, j).start()
            return

        def body(j, carry):
            self.xo[start + j] = held[other + j].astype(BF16)
            return carry

        lax.fori_loop(0, half, body, 0)
        self.x_copy(s).start()

    def relay(self, part=None):
        part = range(self.n) if part is None else part
        if 0 in part:
            for s in range(self.bits - 1):
                half, start, held = self.blocks >> (s + 1), self.start_of(s), self.held(s)
                own = self.mine(s) * half
                self.x_copy(s).wait_recv()

                def body(j, carry):
                    self.acc[j] = held[own + j] + self.xi[start + j].astype(F32)
                    return carry

                lax.fori_loop(0, half, body, 0)
                self.x_begin(s + 1)
        s = self.bits - 1
        own = self.mine(s) * self.n
        for d in part:
            j = lax.rem(self.z + 1 + d, self.n)
            self.x_copy(s, j).wait_recv()
            value = self.held(s)[own + j] + self.xi[self.start_of(s) + j].astype(F32)
            if d < self.n - 1:
                self.zo[j] = value.astype(BF16)
                self.z_copy(j, self.z).start()
            else:
                self.out[...] = value

    def z_copy(self, target, sender):
        base, links = self.number * self.n, self.links
        return remote(
            self.zo.at[target], self.zi.at[sender], links.z_send.at[base + target], links.z_recv.at[base + sender],
            {"seq": target},
        )

    def z_end(self):
        for d in range(1, self.n):
            i = lax.rem(self.z + d, self.n)
            self.z_copy(i, i).wait_recv()
            self.out[...] += self.zi[i].astype(F32)

    def drain(self):
        for s in range(self.bits - 1):
            self.x_copy(s).wait_send()
        for j in range(self.n):
            self.x_copy(self.bits - 1, j).wait_send()
        for d in range(1, self.n):
            self.z_copy(lax.rem(self.z + d, self.n), self.z).wait_send()


def scatter_buffers(n, dp_count, rows, columns):
    blocks = dp_count * n
    return [
        pltpu.VMEM((max(blocks - n, 1), rows, columns), BF16),
        pltpu.VMEM((max(blocks - n, 1), rows, columns), BF16),
        pltpu.VMEM((blocks // 2 if dp_count > 2 else 1, rows, columns), F32),
        pltpu.VMEM((n, rows, columns), BF16),
        pltpu.VMEM((n, rows, columns), BF16),
    ]


def scatter_sems(n, dp_count, count):
    over_dp = pltpu.SemaphoreType.DMA((count * (len(log_bits(dp_count)) - 1 + n),))
    over_seq = pltpu.SemaphoreType.DMA((count * n,))
    return [over_dp, over_dp, over_seq, over_seq]


def remote(src, dst, send, recv, to):
    return pltpu.make_async_remote_copy(
        src_ref=src, dst_ref=dst, send_sem=send, recv_sem=recv, device_id=to,
        device_id_type=pl.DeviceIdType.MESH,
    )


def finish_kernel(
    n, dp_count, heads, layer_scale,
    q_ref, kv_ref, all_ref, branch_ref, do_ref, of_ref, lse_ref, far_ref,
    near_any, exp_any, proj_any, early_any, esum_any, wa_any, normed_any, tok_any, ghid_any, gain_any,
    lout_ref, gtok_ref, exp_out, proj_out, query_out, keyval_out, sums_ref,
    dq_acc, own_acc, far_up, far_down, lse_sc, dot_sc, up_out, up_in, down_out, down_in,
    near_ref, exp_ref, proj_ref, early_ref, esum_ref, wa_ref, normed_ref, tok_ref, ghid_ref, gain_ref,
    stacked, mix, xhat_sc, inv_sc, query_sc, keyval_sc,
    exp_xo, exp_xi, exp_acc, exp_zo, exp_zi,
    proj_xo, proj_xi, proj_acc, proj_zo, proj_zi,
    query_xo, query_xi, query_acc, query_zo, query_zi,
    keyval_xo, keyval_xi, keyval_acc, keyval_zo, keyval_zi,
    core_out, core_in, y_out, y_in, far_in, seq_in, tensor_in, dp_out, dp_in,
    up_send, up_recv, down_send, down_recv, x_send, x_recv, z_send, z_recv,
    core_send, core_recv, y_send, y_recv, seq_send, seq_recv, tensor_send, tensor_recv, dp_send, dp_recv,
    fetch_sem,
):
    z = lax.axis_index("seq")
    t = lax.axis_index("tensor")
    dp = lax.axis_index("dp")
    feats = heads * HEAD_DIM
    share = ghid_ref.shape[0]
    has_up, has_down = z < n - 1, z > 0
    dp_bits = log_bits(dp_count)
    bits = len(dp_bits)
    blocks = dp_count * n
    mesh_ids = pl.DeviceIdType.MESH

    fetches = [
        pltpu.make_async_copy(src, dst, fetch_sem.at[i])
        for i, (src, dst) in enumerate(
            [
                (proj_any, proj_ref), (exp_any, exp_ref), (normed_any, normed_ref), (tok_any, tok_ref),
                (wa_any, wa_ref), (near_any, near_ref), (ghid_any, ghid_ref), (early_any, early_ref),
                (esum_any, esum_ref), (gain_any, gain_ref),
            ]
        )
    ]
    for one in fetches:
        one.start()

    barrier = pltpu.get_barrier_semaphore()
    seq_peers = [{"seq": lax.rem(z + d, n)} for d in range(1, n)]
    tensor_peers = [{"tensor": lax.rem(t + d, 4)} for d in range(1, 4)]
    dp_peers = [{"dp": flip(dp, bit)} for bit in dp_bits]
    for peer in seq_peers + tensor_peers + dp_peers:
        pl.semaphore_signal(barrier, inc=1, device_id=peer, device_id_type=mesh_ids)
    pl.semaphore_wait(barrier, n + 2 + bits)

    links = Links(n, dp_count, x_send, x_recv, z_send, z_recv)
    expand = Scatter(links, 0, exp_ref, exp_xo, exp_xi, exp_acc, exp_zo, exp_zi, exp_out)
    project = Scatter(links, 1, proj_ref, proj_xo, proj_xi, proj_acc, proj_zo, proj_zi, proj_out)
    query = Scatter(links, 2, query_sc, query_xo, query_xi, query_acc, query_zo, query_zi, query_out)
    keyval = Scatter(links, 3, keyval_sc, keyval_xo, keyval_xi, keyval_acc, keyval_zo, keyval_zi, keyval_out)
    scatters = (expand, project, query, keyval)

    sibling, partner = {"tensor": flip(t, 1)}, {"tensor": flip(t, 2)}
    far_copy = remote(far_ref, far_in, y_send.at[0], y_recv.at[0], partner)
    far_copy.start()
    fetches[1].wait()
    expand.x_begin()
    fetches[0].wait()
    project.x_begin()

    def hop(out, inn, d, to, send, recv):
        return remote(out.at[d], inn.at[d], send.at[d], recv.at[d], {"seq": to})

    dq_acc[...] = jnp.zeros_like(dq_acc)
    for h in range(heads):
        rows = slice(h * HEAD_DIM, (h + 1) * HEAD_DIM)
        lse_sc[h] = lse_ref[h:h + 1, :]
        dot_sc[h] = jnp.sum(do_ref[rows, :].astype(F32) * of_ref[rows, :], axis=0, keepdims=True)

    nt = (((1,), (1,)), ((), ()))
    tn = (((0,), (0,)), ((), ()))

    def tile(h, cols, k, v, mask):
        rows = pl.ds(pl.multiple_of(h * HEAD_DIM, HEAD_DIM), HEAD_DIM)
        q, do = q_ref[rows, cols], do_ref[rows, cols]
        s = mask(lax.dot_general(k, q, tn, preferred_element_type=F32))
        p = jnp.exp(s - lse_sc[h, :, cols])
        dp = lax.dot_general(v, do, tn, preferred_element_type=F32)
        ds = (p * (dp - dot_sc[h, :, cols])).astype(BF16)
        p = p.astype(BF16)
        dv = lax.dot_general(do, p, nt, preferred_element_type=F32)
        dk = lax.dot_general(q, ds, nt, preferred_element_type=F32)
        dq_acc[rows, cols] += jnp.dot(k, ds, preferred_element_type=F32)
        return dk, dv

    def head_rows(h):
        return (pl.ds(pl.multiple_of(h * HEAD_DIM, HEAD_DIM), HEAD_DIM),
                pl.ds(pl.multiple_of(feats + h * HEAD_DIM, HEAD_DIM), HEAD_DIM))

    def columns(c):
        return pl.ds(pl.multiple_of(c * PCH, PCH), PCH)

    branch = branch_ref[0, 0]

    def full(source, c, block, total):
        limit = jnp.where(c == 0, n * PCH, branch) - block * PCH
        def mask(s):
            key = lax.broadcasted_iota(jnp.int32, (PCH, 1), 0)
            return s + jnp.where(key < limit, 0.0, big_negative)
        def body(h, carry):
            rows, vrows = head_rows(h)
            dk, dv = tile(h, columns(c), source[rows, :], source[vrows, :], mask)
            total[rows, :] += dk
            total[vrows, :] += dv
            return carry
        lax.fori_loop(0, heads, body, 0)

    def diag(i, carry):
        c, h = i // heads, i % heads
        rows, vrows = head_rows(h)
        cols = columns(c)
        def mask(s):
            key = lax.broadcasted_iota(jnp.int32, s.shape, 0)
            query = lax.broadcasted_iota(jnp.int32, s.shape, 1)
            return jnp.where(key <= query, s, big_negative)
        dk, dv = tile(h, cols, kv_ref[rows, cols], kv_ref[vrows, cols], mask)
        own_acc[rows, cols] = dk
        own_acc[vrows, cols] = dv
        return carry

    def far_blocks(i, carry):
        d = n - 1 - i

        @pl.when(z + d < n)
        def _():
            far_up[d - 1] = jnp.zeros(far_up.shape[1:], F32)
            full(all_ref.at[z + d], 1, z + d, far_up.at[d - 1])
            @pl.when(~has_down | (d == n - 1))
            def _():
                up_out[d - 1] = far_up[d - 1].astype(BF16)
                hop(up_out, up_in, d - 1, z + 1, up_send, up_recv).start()

        @pl.when(z >= d)
        def _():
            far_down[d - 1] = jnp.zeros(far_down.shape[1:], F32)
            def both(c, carry):
                full(all_ref.at[z - d], c, z - d, far_down.at[d - 1])
                return carry
            lax.fori_loop(0, 2, both, 0)
            @pl.when(~has_up | (d == n - 1))
            def _():
                down_out[d - 1] = far_down[d - 1].astype(BF16)
                hop(down_out, down_in, d - 1, z - 1, down_send, down_recv).start()
        return carry

    lax.fori_loop(0, n - 1, far_blocks, 0)

    def relays(i, carry):
        d = n - 2 - i

        @pl.when(d == 1)
        def _():
            lax.fori_loop(0, 2 * heads, diag, 0)
            full(kv_ref.at[:, 0:PCH], 1, z, own_acc.at[:, 0:PCH])

        @pl.when((z + d < n) & has_down)
        def _():
            hop(up_out, up_in, d, z, up_send, up_recv).wait_recv()
            up_out[d - 1] = (far_up[d - 1] + up_in[d].astype(F32)).astype(BF16)
            hop(up_out, up_in, d - 1, z + 1, up_send, up_recv).start()

        @pl.when((z >= d) & has_up)
        def _():
            hop(down_out, down_in, d, z, down_send, down_recv).wait_recv()
            down_out[d - 1] = (far_down[d - 1] + down_in[d].astype(F32)).astype(BF16)
            hop(down_out, down_in, d - 1, z - 1, down_send, down_recv).start()
        return carry

    lax.fori_loop(0, n - 2, relays, 0)
    expand.relay()
    project.relay()

    def place(k):
        owner = t
        for bit in (1, 2):
            turned = flip(owner, bit)
            if isinstance(k, int):
                owner = turned if k & bit else owner
            else:
                owner = jnp.where(lax.rem(lax.div(k, bit), 2) == 1, turned, owner)
        return pl.ds(pl.multiple_of(owner * share, share), share)

    rows = query_sc.shape[1]

    def weight_gradient(part, target):
        value = jnp.dot(part, normed_ref[...], preferred_element_type=F32).T
        for b in range(blocks):
            target[b] = value[b * rows : (b + 1) * rows, :]

    stacked[0:feats, :] = (dq_acc[...] * (1.0 / math.sqrt(HEAD_DIM))).astype(BF16)
    for one in fetches[2:]:
        one.wait()
    weight_gradient(stacked[0:feats, :], query_sc)
    query.x_begin()
    stacked[feats:, PCH:] = own_acc[:, PCH:].astype(BF16)

    def prepare(k, carry):
        value = tok_ref[place(k), :].astype(F32)
        centred = value - jnp.mean(value, axis=-1, keepdims=True)
        inverse = lax.rsqrt(jnp.mean(centred * centred, axis=-1, keepdims=True) + norm_eps)
        xhat_sc[k] = centred * inverse
        inv_sc[k] = jnp.broadcast_to(inverse, (share, 128))
        return carry

    lax.fori_loop(0, 4, prepare, 0)

    @pl.when(has_down)
    def _():
        hop(up_out, up_in, 0, z, up_send, up_recv).wait_recv()
        own_acc[:, 0:PCH] += up_in[0].astype(F32)
    @pl.when(has_up)
    def _():
        hop(down_out, down_in, 0, z, down_send, down_recv).wait_recv()
        own_acc[:, 0:PCH] += down_in[0].astype(F32)
    stacked[feats:, 0:PCH] = own_acc[:, 0:PCH].astype(BF16)

    weight_gradient(stacked[feats:, :], keyval_sc)
    keyval.x_begin()

    def grad_normed(k):
        mix[k] = lax.dot_general(stacked[:, place(k)], wa_ref[...], tn, preferred_element_type=F32)
        return mix[k]

    def core_copy(i):
        return remote(core_out.at[i], core_in.at[i], core_send.at[i], core_recv.at[i], sibling)

    core_out[0] = grad_normed(3).astype(BF16)
    core_copy(0).start()
    last = grad_normed(2)
    core_copy(0).wait_recv()
    y_out[...] = (last + core_in[0].astype(F32)).astype(BF16)
    y_copy = remote(y_out, y_in, y_send.at[1], y_recv.at[1], partner)
    y_copy.start()
    core_out[1] = grad_normed(1).astype(BF16)
    core_copy(1).start()
    query.relay()
    grad_normed(0)

    width = tensor_in.shape[2]
    tensor_in[t, 0:2, :] = jnp.zeros((2, width), F32)
    tensor_in[t, 2:6, :] = early_ref[...]
    tensor_in[t, 6:7, :] = esum_ref[...]
    tensor_in[t, 7:8, :] = jnp.zeros((1, width), F32)
    ones = jnp.ones((8, stacked.shape[1]), BF16)
    tensor_in[t, 7:8, 0 : 3 * feats] = lax.dot_general(ones, stacked[...], nt, preferred_element_type=F32)[0:1]

    def statistics(k, carry):
        tensor_in[t, 0:1, :] += jnp.sum(mix[k] * xhat_sc[k], axis=0, keepdims=True)
        tensor_in[t, 1:2, :] += jnp.sum(mix[k], axis=0, keepdims=True)
        return carry

    lax.fori_loop(0, 4, statistics, 0)

    def seq_copy(target, sender):
        return remote(seq_in.at[z], seq_in.at[sender], seq_send.at[target], seq_recv.at[sender], {"seq": target})

    def tensor_copy(target, sender):
        return remote(
            tensor_in.at[t], tensor_in.at[sender], tensor_send.at[target], tensor_recv.at[sender],
            {"tensor": target},
        )

    def dp_copy(i):
        return remote(dp_out.at[i], dp_in.at[i], dp_send.at[i], dp_recv.at[i], dp_peers[i])

    for d in range(1, 4):
        tensor_copy(lax.rem(t + d, 4), t).start()
    keyval.relay(range(0, 2))
    for d in range(1, 4):
        other = lax.rem(t + d, 4)
        tensor_copy(other, other).wait_recv()
    total = tensor_in[0]
    for i in range(1, 4):
        total = total + tensor_in[i]
    own = tensor_in[t]
    row = lax.broadcasted_iota(jnp.int32, own.shape, 0)
    dp_out[0] = jnp.where(row < 6, total, own)
    dp_copy(0).start()
    keyval.relay(range(2, n))
    for i in range(bits):
        dp_copy(i).wait_recv()
        value = dp_out[i] + dp_in[i]
        if i + 1 < bits:
            dp_out[i + 1] = value
            dp_copy(i + 1).start()
        else:
            seq_in[z] = value
    for d in range(1, n):
        seq_copy(lax.rem(z + d, n), z).start()

    core_copy(1).wait_recv()
    y_copy.wait_recv()
    mixed = mix[0] + core_in[1].astype(F32) + y_in[...].astype(F32)
    e = mixed * gain_ref[0:1, :]
    xhat = xhat_sc[0]
    gtok_ref[...] = (
        ghid_ref[...]
        + inv_sc[0][:, 0:1]
        * (e - jnp.mean(e, axis=-1, keepdims=True) - xhat * jnp.mean(e * xhat, axis=-1, keepdims=True))
    ).astype(BF16)
    far_copy.wait_recv()
    lout_ref[...] = (near_ref[...] + layer_scale * far_in[...].astype(F32)).astype(BF16)
    expand.z_end()
    project.z_end()
    query.z_end()
    for d in range(1, n):
        other = lax.rem(z + d, n)
        seq_copy(other, other).wait_recv()
    summed = seq_in[0]
    for i in range(1, n):
        summed = summed + seq_in[i]
    sums_ref[...] = summed
    keyval.z_end()

    for d in range(1, n):
        @pl.when(z + d < n)
        def _(): hop(up_out, up_in, d - 1, z + 1, up_send, up_recv).wait_send()
        @pl.when(z >= d)
        def _(): hop(down_out, down_in, d - 1, z - 1, down_send, down_recv).wait_send()
    for one in scatters:
        one.drain()
    far_copy.wait_send()
    y_copy.wait_send()
    for i in range(2):
        core_copy(i).wait_send()
    for d in range(1, n):
        seq_copy(lax.rem(z + d, n), z).wait_send()
    for d in range(1, 4):
        tensor_copy(lax.rem(t + d, 4), t).wait_send()
    for i in range(bits):
        dp_copy(i).wait_send()


def finish(
    n, dp_count, layer_scale, q, kv, kv_all, branch, do, of, lse, near, far,
    grad_expand, grad_proj, early, expand_terms, w_attn, normed_one, token_rows,
    grad_hidden, norm_gains,
):
    feats, rows = q.shape
    heads = feats // HEAD_DIM
    share, width = grad_hidden.shape
    blocks = dp_count * n
    bits = len(log_bits(dp_count))
    vm = pl.BlockSpec(memory_space=pltpu.VMEM)
    anywhere = pl.BlockSpec(memory_space=pl.ANY)
    slots = pltpu.VMEM((n - 1, 2 * feats, PCH), BF16)
    shape = jax.ShapeDtypeStruct
    sems = lambda count: pltpu.SemaphoreType.DMA((count,))
    block_rows = width // blocks
    proj_blocks = grad_proj.reshape(blocks, block_rows, feats)
    units = grad_expand.shape[1]
    fetched = [
        near, grad_expand.reshape(blocks, block_rows, units), proj_blocks, early, expand_terms, w_attn, normed_one, token_rows,
        grad_hidden, norm_gains,
    ]
    widths = [units, feats, feats, 2 * feats]
    scatter_scratch = []
    for columns in widths:
        scatter_scratch += scatter_buffers(n, dp_count, block_rows, columns)
    return pl.pallas_call(
        functools.partial(finish_kernel, n, dp_count, heads, layer_scale),
        out_shape=(
            shape((share, width), BF16),
            shape((share, width), BF16),
            *(shape((block_rows, columns), F32) for columns in widths),
            shape((8, width), F32),
        ),
        in_specs=[vm, vm, vm, pl.BlockSpec(memory_space=pltpu.SMEM)] + [vm] * 4 + [anywhere] * len(fetched),
        out_specs=(vm,) * 7,
        scratch_shapes=[
            pltpu.VMEM((feats, rows), F32),
            pltpu.VMEM((2 * feats, rows), F32),
            pltpu.VMEM((n - 1, 2 * feats, PCH), F32),
            pltpu.VMEM((n - 1, 2 * feats, PCH), F32),
            pltpu.VMEM((heads, 1, rows), F32),
            pltpu.VMEM((heads, 1, rows), F32),
            slots, slots, slots, slots,
            *(pltpu.VMEM(one.shape, one.dtype) for one in fetched),
            pltpu.VMEM((3 * feats, rows), BF16),
            pltpu.VMEM((4, share, width), F32),
            pltpu.VMEM((4, share, width), F32),
            pltpu.VMEM((4, share, 128), F32),
            pltpu.VMEM((blocks, block_rows, feats), F32),
            pltpu.VMEM((blocks, block_rows, 2 * feats), F32),
            *scatter_scratch,
            pltpu.VMEM((2, share, width), BF16),
            pltpu.VMEM((2, share, width), BF16),
            pltpu.VMEM((share, width), BF16),
            pltpu.VMEM((share, width), BF16),
            pltpu.VMEM((share, width), BF16),
            pltpu.VMEM((n, 8, width), F32),
            pltpu.VMEM((4, 8, width), F32),
            pltpu.VMEM((bits, 8, width), F32),
            pltpu.VMEM((bits, 8, width), F32),
            sems(n - 1), sems(n - 1), sems(n - 1), sems(n - 1),
            *scatter_sems(n, dp_count, 4),
            sems(2), sems(2), sems(2), sems(2), sems(n), sems(n), sems(4), sems(4), sems(bits), sems(bits),
            sems(len(fetched)),
        ],
        compiler_params=pltpu.CompilerParams(
            collective_id=2, has_side_effects=True, vmem_limit_bytes=60 * 2**20
        ),
        cost_estimate=pl.CostEstimate(flops=4 * 10**10, bytes_accessed=10**7, transcendentals=0),
        name="finish",
    )(q, kv, kv_all, branch, do, of, lse, far, *fetched)


def emit_kernel(
    feats, turned, con, lout, gtok, expand, proj, query, keyval, sums,
    lout_ref, gtok_ref, attn_ref, proj_ref, exp_ref, con_ref, bias_ref, branch_ref, units_ref, gains_ref, shifts_ref,
):
    lout_ref[...] = lout[...]
    gtok_ref[...] = gtok[...]
    attn_ref[0] = query[...]
    attn_ref[1] = keyval[:, 0:feats]
    attn_ref[2] = keyval[:, feats : 2 * feats]
    proj_ref[...] = proj[...].T if turned else proj[...]
    exp_ref[...] = expand[...]
    con_ref[...] = con[...]
    bias_ref[0:1, :] = sums[7:8, 0:feats]
    bias_ref[1:2, :] = sums[7:8, 2 * feats : 3 * feats]
    branch_ref[...] = sums[2:4, :]
    units_ref[...] = sums[6, :]
    for row, late, early in ((gains_ref, 0, 4), (shifts_ref, 1, 5)):
        row[0:1, :] = sums[late : late + 1, :]
        row[1:2, :] = sums[early : early + 1, :]


def emit(con, results):
    lout, gtok, expand, proj, query, keyval, sums = results
    rows, feats = query.shape
    share, width = lout.shape
    turned = rows % 8 == 0
    shape = jax.ShapeDtypeStruct
    vm = pl.BlockSpec(memory_space=pltpu.VMEM)
    outputs = pl.pallas_call(
        functools.partial(emit_kernel, feats, turned),
        out_shape=(
            shape((share, width), BF16), shape((share, width), BF16), shape((3, rows, feats), F32),
            shape((feats, rows) if turned else (rows, feats), F32), shape(expand.shape, F32),
            shape(con.shape, F32), shape((2, feats), F32), shape((2, width), F32),
            shape((expand.shape[1],), F32), shape((2, width), F32), shape((2, width), F32),
        ),
        in_specs=[vm] * 8,
        out_specs=(vm,) * 11,
        compiler_params=pltpu.CompilerParams(vmem_limit_bytes=60 * 2**20),
        name="emit",
    )(con, *results)
    lout, gtok, attn, proj, expand, con, bias, branch, units, gains, shifts = outputs
    whole = (1, 1, share, width)
    return (
        lout.reshape(whole), gtok.reshape(whole), attn, proj if turned else proj.T, expand, con.T,
        bias, branch, units, gains, shifts,
    )


def middle_kernel(
    n, dp_count, layer_scale, o_ref, tok_ref, cot_ref, wp_ref, we_ref, wc_ref, bb_ref, eb_ref, gain_ref, shift_ref,
    ghid_ref, near_ref, far_ref, gatt_ref, gproj_ref, gexp_ref, gcon_ref, sums_ref, esum_ref,
    ga_sc, mix_sc, n2, gm, act, gp, att, own_sc, xhat_sc, inv_sc, proj_sc,
    core_out, core_in, y_out, y_in, con_sc, con_xo, con_xi, con_acc, con_zo, con_zi,
    core_send, core_recv, y_send, y_recv, n2_send, n2_recv, att_send, att_recv, x_send, x_recv, z_send, z_recv,
):
    t = lax.axis_index("tensor")
    y, c = t // 2, t % 2
    sibling = y * 2 + (1 - c)
    partner = (1 - y) * 2 + c
    share = own_sc.shape[0]

    def block(k):
        if isinstance(k, int):
            return ((1 - y) if k >= 2 else y) * 2 + ((1 - c) if k % 2 else c)
        return jnp.where(k >= 2, 1 - y, y) * 2 + jnp.where(k % 2 == 1, 1 - c, c)

    def place(k):
        return pl.ds(pl.multiple_of(block(k) * share, share), share)

    barrier = pltpu.get_barrier_semaphore()
    for to in (sibling, partner):
        pl.semaphore_signal(barrier, inc=1, device_id={"tensor": to}, device_id_type=pl.DeviceIdType.MESH)
    links = Links(n, dp_count, x_send, x_recv, z_send, z_recv)
    peers = [{"seq": lax.rem(links.z + d, n)} for d in range(1, n)]
    peers += [{"dp": flip(links.dp, bit)} for bit in log_bits(dp_count)]
    for peer in peers:
        pl.semaphore_signal(barrier, inc=1, device_id=peer, device_id_type=pl.DeviceIdType.MESH)
    pl.semaphore_wait(barrier, 2 + len(peers))
    weights = Scatter(links, 0, con_sc, con_xo, con_xi, con_acc, con_zo, con_zi, gcon_ref)

    def copy(src, dst, send, recv, to):
        return pltpu.make_async_remote_copy(
            src_ref=src, dst_ref=dst, send_sem=send, recv_sem=recv,
            device_id={"tensor": to}, device_id_type=pl.DeviceIdType.MESH,
        )

    def core_copy(i):
        return copy(core_out.at[i], core_in.at[i], core_send.at[i], core_recv.at[i], sibling)

    def y_copy(i):
        return copy(y_out.at[i], y_in.at[i], y_send.at[i], y_recv.at[i], partner)

    def gather(ref, send, recv):
        return (
            copy(ref.at[0], ref.at[2], send.at[0], recv.at[0], partner),
            copy(ref.at[0], ref.at[1], send.at[1], recv.at[1], sibling),
            copy(ref.at[2], ref.at[3], send.at[2], recv.at[2], sibling),
        )

    tn = (((0,), (0,)), ((), ()))
    nt = (((1,), (1,)), ((), ()))

    def project(k):
        return lax.dot_general(o_ref[:, place(k)], wp_ref[...], tn, preferred_element_type=F32)

    core_out[0] = project(3).astype(BF16)
    core_copy(0).start()
    own_sc[...] = project(2)
    core_out[1] = project(1).astype(BF16)
    core_copy(1).start()
    core_copy(0).wait_recv()
    y_out[0] = (own_sc[...] + core_in[0].astype(F32)).astype(BF16)
    y_copy(0).start()
    own_sc[...] = project(0)

    def before(k, carry):
        g = (cot_ref[place(k), :].astype(F32) * layer_scale).astype(BF16)
        gm[k] = g
        ga_sc[k] = lax.dot_general(g, wc_ref[...], nt, preferred_element_type=F32)
        return carry

    lax.fori_loop(0, 4, before, 0)
    core_copy(1).wait_recv()
    own_sc[...] += core_in[1].astype(F32)
    y_copy(0).wait_recv()

    hidden = tok_ref[place(0), :].astype(F32) + layer_scale * (
        own_sc[...] + y_in[0].astype(F32) + bb_ref[0:1, :]
    )
    near_ref[...] = hidden + layer_scale * bb_ref[1:2, :]
    centred = hidden - jnp.mean(hidden, axis=-1, keepdims=True)
    inverse = lax.rsqrt(jnp.mean(centred * centred, axis=-1, keepdims=True) + norm_eps)
    xhat = centred * inverse
    n2[0] = (xhat * gain_ref[1:2, :] + shift_ref[1:2, :]).astype(BF16)
    across, near, on = gather(n2, n2_send, n2_recv)
    across.start()
    near.start()
    xhat_sc[...] = xhat
    inv_sc[...] = jnp.broadcast_to(inverse, inv_sc.shape)
    esum_ref[...] = jnp.zeros_like(esum_ref)

    def process(k, carry):
        @pl.when(k == 1)
        def _():
            near.wait_recv()

        @pl.when(k == 2)
        def _():
            across.wait_recv()
            on.start()

        @pl.when(k == 3)
        def _():
            on.wait_recv()

        v = jnp.dot(n2[k], we_ref[...], preferred_element_type=F32) + eb_ref[...]
        square = v * v
        th = jnp.tanh(math.sqrt(2.0 / math.pi) * (v + 0.044715 * (v * square)))
        cdf = 0.5 * (1.0 + th)
        act[k] = (v * cdf).astype(BF16)
        slope = cdf + 0.5 * v * (1.0 - th * th) * (
            math.sqrt(2.0 / math.pi) * (1.0 + 3 * 0.044715 * square)
        )
        g = (slope * ga_sc[k]).astype(BF16)
        gp[k] = g
        esum_ref[...] += jnp.sum(g.astype(F32), axis=0, keepdims=True)
        mix_sc[k] = lax.dot_general(g, we_ref[...], nt, preferred_element_type=F32)
        return carry

    lax.fori_loop(0, 4, process, 0)
    core_out[2] = mix_sc[3].astype(BF16)
    core_copy(2).start()
    core_out[3] = mix_sc[1].astype(BF16)
    core_copy(3).start()
    core_copy(2).wait_recv()
    y_out[1] = (mix_sc[2] + core_in[2].astype(F32)).astype(BF16)
    y_copy(1).start()

    rows = 4 * share
    width = gm.shape[2]
    value = lax.dot_general(
        gm[...].reshape(rows, width), act[...].reshape(rows, -1), tn, preferred_element_type=F32
    )
    size = con_sc.shape[1]
    for b in range(con_sc.shape[0]):
        con_sc[b] = value[b * size : (b + 1) * size, :]
    weights.x_begin()
    gexp_ref[...] = lax.dot_general(
        n2[...].reshape(rows, width), gp[...].reshape(rows, -1), tn, preferred_element_type=F32
    )

    def contract(k):
        return jnp.dot(act[k], wc_ref[...], preferred_element_type=F32)

    core_out[4] = contract(3).astype(BF16)
    core_copy(4).start()
    core_out[5] = contract(1).astype(BF16)
    core_copy(5).start()
    near_ref[...] += layer_scale * contract(0)
    last = contract(2)
    core_copy(4).wait_recv()
    far_ref[...] = (last + core_in[4].astype(F32)).astype(BF16)
    core_copy(5).wait_recv()
    near_ref[...] += layer_scale * core_in[5].astype(F32)
    weights.relay(range(0, 1))

    core_copy(3).wait_recv()
    mixed = mix_sc[0] + core_in[3].astype(F32)
    y_copy(1).wait_recv()
    mixed = mixed + y_in[1].astype(F32)
    e = mixed * gain_ref[1:2, :]
    xhat = xhat_sc[...]
    grad_hidden = cot_ref[place(0), :].astype(F32) + inv_sc[:, 0:1] * (
        e - jnp.mean(e, axis=-1, keepdims=True) - xhat * jnp.mean(e * xhat, axis=-1, keepdims=True)
    )
    g = (grad_hidden * layer_scale).astype(BF16)
    att[0] = g
    across_b, near_b, on_b = gather(att, att_send, att_recv)
    across_b.start()
    near_b.start()
    ghid_ref[...] = grad_hidden
    sums_ref[0:1, :] = jnp.sum(g.astype(F32), axis=0, keepdims=True)
    sums_ref[1:2, :] = jnp.sum(gm[0].astype(F32), axis=0, keepdims=True)
    sums_ref[2:3, :] = jnp.sum(mixed * xhat, axis=0, keepdims=True)
    sums_ref[3:4, :] = jnp.sum(mixed, axis=0, keepdims=True)

    proj_sc[...] = jnp.zeros_like(proj_sc)
    weights.relay(range(1, n))

    def after(k, carry):
        @pl.when(k == 1)
        def _():
            near_b.wait_recv()

        @pl.when(k == 2)
        def _():
            across_b.wait_recv()
            on_b.start()

        @pl.when(k == 3)
        def _():
            on_b.wait_recv()

        gatt_ref[:, place(k)] = lax.dot_general(
            wp_ref[...], att[k], nt, preferred_element_type=F32
        ).astype(BF16)
        proj_sc[...] += jnp.dot(o_ref[:, place(k)], att[k], preferred_element_type=F32)
        return carry

    lax.fori_loop(0, 4, after, 0)
    gproj_ref[...] = proj_sc[...].T
    weights.z_end()
    weights.drain()
    for i in range(6):
        core_copy(i).wait_send()
    for i in range(2):
        y_copy(i).wait_send()
    for one in (across, near, on, across_b, near_b, on_b):
        one.wait_send()


def middle(
    n, dp_count, layer_scale, attended, token_rows, cotangent_rows, w_proj, w_expand, w_contract,
    branch_bias, expand_bias, norm_gains, norm_shifts,
):
    rows, width = token_rows.shape
    feats, hidden_units = w_proj.shape[0], w_expand.shape[1]
    share = rows // 4
    size = width // (dp_count * n)
    vm = pl.BlockSpec(memory_space=pltpu.VMEM)
    shape = jax.ShapeDtypeStruct
    slots = lambda columns, kind: pltpu.VMEM((4, share, columns), kind)
    sems = lambda count: pltpu.SemaphoreType.DMA((count,))
    return pl.pallas_call(
        functools.partial(middle_kernel, n, dp_count, layer_scale),
        out_shape=(
            shape((share, width), F32),
            shape((share, width), F32),
            shape((share, width), BF16),
            shape((feats, rows), BF16),
            shape((width, feats), F32),
            shape((width, hidden_units), F32),
            shape((size, hidden_units), F32),
            shape((4, width), F32),
            shape((1, hidden_units), F32),
        ),
        in_specs=[vm] * 10,
        out_specs=(vm,) * 9,
        scratch_shapes=[
            slots(hidden_units, F32),
            slots(width, F32),
            slots(width, BF16),
            slots(width, BF16),
            slots(hidden_units, BF16),
            slots(hidden_units, BF16),
            slots(width, BF16),
            pltpu.VMEM((share, width), F32),
            pltpu.VMEM((share, width), F32),
            pltpu.VMEM((share, 128), F32),
            pltpu.VMEM((feats, width), F32),
            pltpu.VMEM((6, share, width), BF16),
            pltpu.VMEM((6, share, width), BF16),
            pltpu.VMEM((2, share, width), BF16),
            pltpu.VMEM((2, share, width), BF16),
            pltpu.VMEM((dp_count * n, size, hidden_units), F32),
            *scatter_buffers(n, dp_count, size, hidden_units),
            sems(6), sems(6), sems(2), sems(2), sems(3), sems(3), sems(3), sems(3),
            *scatter_sems(n, dp_count, 1),
        ],
        compiler_params=pltpu.CompilerParams(
            collective_id=3, has_side_effects=True, vmem_limit_bytes=56 * 2**20
        ),
        cost_estimate=pl.CostEstimate(flops=5 * 10**10, bytes_accessed=2 * 10**7, transcendentals=0),
        name="middle",
    )(
        attended, token_rows, cotangent_rows, w_proj, w_expand, w_contract,
        branch_bias, expand_bias, norm_gains, norm_shifts,
    )


def shards(
    tokens,
    branch,
    w_attn,
    w_proj,
    w_expand,
    w_contract,
    attn_bias,
    branch_bias,
    expand_bias,
    norm_gains,
    norm_shifts,
    cotangent,
):
    seq_count = lax.axis_size("seq")
    width = tokens.shape[3]
    row_count = tokens.shape[2]
    share = row_count // lax.axis_size("tensor")
    local_width = w_attn.shape[2]
    layer_scale = 1.0 / math.sqrt(LAYERS)

    token_rows = tokens.reshape(row_count, width)
    cotangent_rows = cotangent.reshape(row_count, width)
    w_attn = jnp.transpose(w_attn, (0, 2, 1)).reshape(3 * local_width, width)
    attended, attended_wide, logsum, all_kv, queries, own_kv, normed_one = attend_forward(
        seq_count, token_rows, w_attn, attn_bias, norm_gains, norm_shifts, branch
    )
    (
        grad_hidden, mlp_near, mlp_far, grad_attended,
        grad_proj, grad_expand, grad_contract, early, expand_terms,
    ) = middle(
        seq_count, lax.axis_size("dp"), layer_scale, attended, token_rows, cotangent_rows, w_proj, w_expand, w_contract,
        branch_bias, expand_bias.reshape(1, -1), norm_gains, norm_shifts,
    )
    return emit(grad_contract, finish(
        seq_count, lax.axis_size("dp"), layer_scale, queries, own_kv, all_kv, branch, grad_attended,
        attended_wide, logsum, mlp_near, mlp_far, grad_expand, grad_proj, early,
        expand_terms, w_attn, normed_one, token_rows, grad_hidden, norm_gains,
    ))


def solution(mesh):
    placed = (
        P("dp", "seq", None, None),
        P("dp", "seq"),
        P(None, None, "tensor"),
        P("tensor", None),
        P(None, "tensor"),
        P("tensor", None),
        P(None, "tensor"),
        P(),
        P("tensor"),
        P(),
        P(),
        P("dp", "seq", None, None),
    )
    return jax.shard_map(
        shards,
        mesh=mesh,
        in_specs=placed,
        out_specs=(
            P("dp", "seq", "tensor", None),
            P("dp", "seq", "tensor", None),
            P(None, ("dp", "seq"), "tensor"),
            P("tensor", ("dp", "seq")),
            P(("dp", "seq"), "tensor"),
            P("tensor", ("dp", "seq")),
            P(None, "tensor"),
            P(),
            P("tensor"),
            P(),
            P(),
        ),
        check_vma=False,
    )
```

```python
import functools
import math

import jax
import jax.numpy as jnp
from jax import lax
from jax.experimental import pallas as pl
from jax.experimental.pallas import tpu as pltpu
from jax.sharding import PartitionSpec as P

HEAD_DIM = 64
LAYERS = 12
PCH = 512
CLEN = 512
F32 = jnp.float32
BF16 = jnp.bfloat16


norm_eps = 1e-05
big_negative = -1000000000.0


def layer_norm_parts(value):
    centre = jnp.mean(value, axis=-1, keepdims=True)
    centred = value - centre
    spread = jnp.mean(centred * centred, axis=-1, keepdims=True)
    inverse = lax.rsqrt(spread + norm_eps)
    return centred * inverse, inverse


def forward_kernel(n, heads, tok_ref, wa_ref, bias_ref, gain_ref, shift_ref, branch_ref, o_ref, of_ref, lse_ref, kv_all, q_ref, kv_ref, normed_ref, m_sc, l_sc, acc, up_send, up_recv, down_send, down_recv):
    z = lax.axis_index("seq")
    feats = heads * HEAD_DIM
    barrier = pltpu.get_barrier_semaphore()
    has_up, has_down = z < n - 1, z > 0

    def meet(to):
        pl.semaphore_signal(barrier, inc=1, device_id={"seq": to}, device_id_type=pl.DeviceIdType.MESH)

    @pl.when(has_up)
    def _(): meet(z + 1)
    @pl.when(has_down)
    def _(): meet(z - 1)

    bias = [jnp.broadcast_to(bias_ref[i : i + 1, :], (8, feats)).T[:, 0:1] for i in range(2)]

    def project(first, cols):
        normed = normed_ref[cols, :]
        value = lax.dot_general(
            wa_ref[first * feats :, :] if first else wa_ref[0:feats, :], normed,
            (((1,), (1,)), ((), ())), preferred_element_type=F32,
        )
        return value

    def norm_rows(cols):
        value = layer_norm_parts(tok_ref[cols, :].astype(F32))[0]
        normed_ref[cols, :] = (value * gain_ref[0:1, :] + shift_ref[0:1, :]).astype(BF16)

    def keys_values(cols):
        value = project(1, cols)
        kv_ref[0:feats, cols] = value[0:feats].astype(BF16)
        kv_ref[feats:, cols] = (value[feats:] + bias[1]).astype(BF16)

    prompt_cols, other_cols = slice(0, PCH), slice(PCH, q_ref.shape[1])
    norm_rows(prompt_cols)
    keys_values(prompt_cols)
    pl.semaphore_wait(barrier, has_up.astype(jnp.int32) + has_down.astype(jnp.int32))

    own = kv_ref.at[:, 0:PCH]

    def hop(src, block, step, to, send, recv):
        return pltpu.make_async_remote_copy(src_ref=src, dst_ref=kv_all.at[block], send_sem=send.at[step], recv_sem=recv.at[step], device_id={"seq": to}, device_id_type=pl.DeviceIdType.MESH)

    @pl.when(has_up)
    def _(): hop(own, z, 0, z + 1, up_send, up_recv).start()
    @pl.when(has_down)
    def _(): hop(own, z, 0, z - 1, down_send, down_recv).start()

    norm_rows(other_cols)
    keys_values(other_cols)
    for cols in (prompt_cols, other_cols):
        value = (project(0, cols) + bias[0]).astype(BF16)
        q_ref[:, cols] = value * jnp.asarray(1.0 / math.sqrt(HEAD_DIM), BF16)

    def load_q(h, c):
        return q_ref[pl.ds(pl.multiple_of(h * HEAD_DIM, HEAD_DIM), HEAD_DIM), pl.ds(pl.multiple_of(c * PCH, PCH), PCH)]

    def scores(k, q):
        return lax.dot_general(k, q, (((0,), (0,)), ((), ())), preferred_element_type=F32)

    def diag(i, carry):
        c, h = i // heads, i % heads
        rows = pl.ds(pl.multiple_of(h * HEAD_DIM, HEAD_DIM), HEAD_DIM)
        vrows = pl.ds(pl.multiple_of(feats + h * HEAD_DIM, HEAD_DIM), HEAD_DIM)
        cols = pl.ds(pl.multiple_of(c * PCH, PCH), PCH)
        s = scores(kv_ref[rows, cols], load_q(h, c))
        key = lax.broadcasted_iota(jnp.int32, s.shape, 0)
        query = lax.broadcasted_iota(jnp.int32, s.shape, 1)
        s = jnp.where(key <= query, s, big_negative)
        m = jnp.max(s, axis=0, keepdims=True)
        p = jnp.exp(s - m)
        m_sc[h, :, cols] = m
        l_sc[h, :, cols] = jnp.sum(p, axis=0, keepdims=True)
        acc[rows, cols] = jnp.dot(kv_ref[vrows, cols], p.astype(BF16), preferred_element_type=F32)
        return carry
    lax.fori_loop(0, 2 * heads, diag, 0)

    branch = branch_ref[0, 0]

    def full(source, c, block):
        limit = jnp.where(c == 0, n * PCH, branch) - block * PCH
        def body(h, carry):
            rows = pl.ds(pl.multiple_of(h * HEAD_DIM, HEAD_DIM), HEAD_DIM)
            vrows = pl.ds(pl.multiple_of(feats + h * HEAD_DIM, HEAD_DIM), HEAD_DIM)
            cols = pl.ds(pl.multiple_of(c * PCH, PCH), PCH)
            s = scores(source[rows, :], load_q(h, c))
            key = lax.broadcasted_iota(jnp.int32, (PCH, 1), 0)
            s = s + jnp.where(key < limit, 0.0, big_negative)
            m_old = m_sc[h, :, cols]
            m = jnp.maximum(m_old, jnp.max(s, axis=0, keepdims=True))
            p = jnp.exp(s - m)
            alpha = jnp.exp(m_old - m)
            m_sc[h, :, cols] = m
            l_sc[h, :, cols] = l_sc[h, :, cols] * alpha + jnp.sum(p, axis=0, keepdims=True)
            acc[rows, cols] = acc[rows, cols] * alpha + jnp.dot(source[vrows, :], p.astype(BF16), preferred_element_type=F32)
            return carry
        lax.fori_loop(0, heads, body, 0)

    full(own, 1, z)

    def step_body(step, carry):
        @pl.when(z >= step)
        def _():
            hop(own, z - step, step - 1, z, up_send, up_recv).wait_recv()
            @pl.when(has_up & (step < n - 1))
            def _(): hop(kv_all.at[z - step], z - step, step, z + 1, up_send, up_recv).start()
        @pl.when(z + step < n)
        def _():
            hop(own, z + step, step - 1, z, down_send, down_recv).wait_recv()
            @pl.when(has_down & (step < n - 1))
            def _(): hop(kv_all.at[z + step], z + step, step, z - 1, down_send, down_recv).start()
        @pl.when(z >= step)
        def _():
            def both(c, carry):
                full(kv_all.at[z - step], c, z - step)
                return carry
            lax.fori_loop(0, 2, both, 0)
        @pl.when(z + step < n)
        def _(): full(kv_all.at[z + step], 1, z + step)
        return carry
    lax.fori_loop(1, n, step_body, 0)

    for h in range(heads):
        rows = slice(h * HEAD_DIM, (h + 1) * HEAD_DIM)
        total = l_sc[h]
        out = acc[rows, :] / total
        of_ref[rows, :] = out
        o_ref[rows, :] = out.astype(BF16)
        lse_ref[h:h + 1, :] = m_sc[h] + jnp.log(total)

    for step in range(n - 1):
        @pl.when(has_up & (z >= step))
        def _(): hop(own, z, step, z + 1, up_send, up_recv).wait_send()
        @pl.when(has_down & (z + step < n))
        def _(): hop(own, z, step, z - 1, down_send, down_recv).wait_send()

def attend_forward(n, tokens, w_attn, attn_bias, norm_gains, norm_shifts, branch):
    rows, width = tokens.shape
    feats = attn_bias.shape[1]
    heads = feats // HEAD_DIM
    vm = pl.BlockSpec(memory_space=pltpu.VMEM)
    shape = jax.ShapeDtypeStruct
    sems = pltpu.SemaphoreType.DMA((n - 1,))
    return pl.pallas_call(
        functools.partial(forward_kernel, n, heads),
        out_shape=(
            shape((feats, rows), BF16), shape((feats, rows), F32), shape((heads, rows), F32),
            shape((n, 2 * feats, PCH), BF16), shape((feats, rows), BF16), shape((2 * feats, rows), BF16),
            shape((rows, width), BF16),
        ),
        in_specs=[vm] * 5 + [pl.BlockSpec(memory_space=pltpu.SMEM)],
        out_specs=(vm,) * 7,
        scratch_shapes=[
            pltpu.VMEM((heads, 1, rows), F32),
            pltpu.VMEM((heads, 1, rows), F32),
            pltpu.VMEM((feats, rows), F32),
            sems, sems, sems, sems,
        ],
        compiler_params=pltpu.CompilerParams(collective_id=1, has_side_effects=True, vmem_limit_bytes=60 * 2**20),
        cost_estimate=pl.CostEstimate(flops=4 * 10**10, bytes_accessed=10**7, transcendentals=0),
        name="attend_forward",
    )(tokens, w_attn, attn_bias, norm_gains, norm_shifts, branch)


def flip(index, bit):
    return index + bit * (1 - 2 * lax.rem(lax.div(index, bit), 2))


def log_bits(size):
    return [1 << k for k in range(size.bit_length() - 1)]


class Links:
    def __init__(self, n, dp_count, x_send, x_recv, z_send, z_recv):
        self.z, self.dp = lax.axis_index("seq"), lax.axis_index("dp")
        self.n, self.dp_count, self.bits = n, dp_count, len(log_bits(dp_count))
        self.x_send, self.x_recv, self.z_send, self.z_recv = x_send, x_recv, z_send, z_recv


class Scatter:
    def __init__(self, links, number, source, xo, xi, acc, zo, zi, out):
        self.links, self.number, self.source, self.xo, self.xi = links, number, source, xo, xi
        self.acc, self.zo, self.zi, self.out = acc, zo, zi, out
        self.n, self.bits, self.z = links.n, links.bits, links.z
        self.blocks = links.dp_count * links.n

    def mine(self, s):
        return lax.rem(lax.div(self.links.dp, self.links.dp_count >> (s + 1)), 2)

    def start_of(self, s):
        return self.blocks - (self.blocks >> s)

    def held(self, s):
        return self.source if s == 0 else self.acc

    def x_copy(self, s, j=None):
        half, start, links = self.blocks >> (s + 1), self.start_of(s), self.links
        sem = self.number * (self.bits - 1 + self.n) + (self.n + s if j is None else j)
        part = pl.ds(start, half) if j is None else start + j
        return remote(
            self.xo.at[part], self.xi.at[part], links.x_send.at[sem], links.x_recv.at[sem],
            {"dp": flip(links.dp, links.dp_count >> (s + 1))},
        )

    def x_begin(self, s=0):
        half, start, held = self.blocks >> (s + 1), self.start_of(s), self.held(s)
        other = (1 - self.mine(s)) * half
        if s == self.bits - 1:
            for d in range(self.n):
                j = lax.rem(self.z + 1 + d, self.n)
                self.xo[start + j] = held[other + j].astype(BF16)
                self.x_copy(s, j).start()
            return

        def body(j, carry):
            self.xo[start + j] = held[other + j].astype(BF16)
            return carry

        lax.fori_loop(0, half, body, 0)
        self.x_copy(s).start()

    def relay(self, part=None):
        part = range(self.n) if part is None else part
        if 0 in part:
            for s in range(self.bits - 1):
                half, start, held = self.blocks >> (s + 1), self.start_of(s), self.held(s)
                own = self.mine(s) * half
                self.x_copy(s).wait_recv()

                def body(j, carry):
                    self.acc[j] = held[own + j] + self.xi[start + j].astype(F32)
                    return carry

                lax.fori_loop(0, half, body, 0)
                self.x_begin(s + 1)
        s = self.bits - 1
        own = self.mine(s) * self.n
        for d in part:
            j = lax.rem(self.z + 1 + d, self.n)
            self.x_copy(s, j).wait_recv()
            value = self.held(s)[own + j] + self.xi[self.start_of(s) + j].astype(F32)
            if d < self.n - 1:
                self.zo[j] = value.astype(BF16)
                self.z_copy(j, self.z).start()
            else:
                self.out[...] = value

    def z_copy(self, target, sender):
        base, links = self.number * self.n, self.links
        return remote(
            self.zo.at[target], self.zi.at[sender], links.z_send.at[base + target], links.z_recv.at[base + sender],
            {"seq": target},
        )

    def z_end(self):
        for d in range(1, self.n):
            i = lax.rem(self.z + d, self.n)
            self.z_copy(i, i).wait_recv()
            self.out[...] += self.zi[i].astype(F32)

    def drain(self):
        for s in range(self.bits - 1):
            self.x_copy(s).wait_send()
        for j in range(self.n):
            self.x_copy(self.bits - 1, j).wait_send()
        for d in range(1, self.n):
            self.z_copy(lax.rem(self.z + d, self.n), self.z).wait_send()


def scatter_buffers(n, dp_count, rows, columns):
    blocks = dp_count * n
    return [
        pltpu.VMEM((max(blocks - n, 1), rows, columns), BF16),
        pltpu.VMEM((max(blocks - n, 1), rows, columns), BF16),
        pltpu.VMEM((blocks // 2 if dp_count > 2 else 1, rows, columns), F32),
        pltpu.VMEM((n, rows, columns), BF16),
        pltpu.VMEM((n, rows, columns), BF16),
    ]


def scatter_sems(n, dp_count, count):
    over_dp = pltpu.SemaphoreType.DMA((count * (len(log_bits(dp_count)) - 1 + n),))
    over_seq = pltpu.SemaphoreType.DMA((count * n,))
    return [over_dp, over_dp, over_seq, over_seq]


def remote(src, dst, send, recv, to):
    return pltpu.make_async_remote_copy(
        src_ref=src, dst_ref=dst, send_sem=send, recv_sem=recv, device_id=to,
        device_id_type=pl.DeviceIdType.MESH,
    )


def finish_kernel(
    n, dp_count, heads, layer_scale,
    q_ref, kv_ref, all_ref, branch_ref, do_ref, of_ref, lse_ref, far_ref,
    near_any, exp_any, proj_any, early_any, esum_any, wa_any, normed_any, tok_any, ghid_any, gain_any,
    lout_ref, gtok_ref, exp_out, proj_out, query_out, keyval_out, sums_ref,
    dq_acc, own_acc, far_up, far_down, lse_sc, dot_sc, up_out, up_in, down_out, down_in,
    near_ref, exp_ref, proj_ref, early_ref, esum_ref, wa_ref, normed_ref, tok_ref, ghid_ref, gain_ref,
    stacked, mix, xhat_sc, inv_sc, query_sc, keyval_sc,
    exp_xo, exp_xi, exp_acc, exp_zo, exp_zi,
    proj_xo, proj_xi, proj_acc, proj_zo, proj_zi,
    query_xo, query_xi, query_acc, query_zo, query_zi,
    keyval_xo, keyval_xi, keyval_acc, keyval_zo, keyval_zi,
    core_out, core_in, y_out, y_in, far_in, seq_in, tensor_in, dp_out, dp_in,
    up_send, up_recv, down_send, down_recv, x_send, x_recv, z_send, z_recv,
    core_send, core_recv, y_send, y_recv, seq_send, seq_recv, tensor_send, tensor_recv, dp_send, dp_recv,
    fetch_sem,
):
    z = lax.axis_index("seq")
    t = lax.axis_index("tensor")
    dp = lax.axis_index("dp")
    feats = heads * HEAD_DIM
    share = ghid_ref.shape[0]
    has_up, has_down = z < n - 1, z > 0
    dp_bits = log_bits(dp_count)
    bits = len(dp_bits)
    blocks = dp_count * n
    mesh_ids = pl.DeviceIdType.MESH

    fetches = [
        pltpu.make_async_copy(src, dst, fetch_sem.at[i])
        for i, (src, dst) in enumerate(
            [
                (proj_any, proj_ref), (exp_any, exp_ref), (normed_any, normed_ref), (tok_any, tok_ref),
                (wa_any, wa_ref), (near_any, near_ref), (ghid_any, ghid_ref), (early_any, early_ref),
                (esum_any, esum_ref), (gain_any, gain_ref),
            ]
        )
    ]
    for one in fetches:
        one.start()

    barrier = pltpu.get_barrier_semaphore()
    seq_peers = [{"seq": lax.rem(z + d, n)} for d in range(1, n)]
    tensor_peers = [{"tensor": lax.rem(t + d, 4)} for d in range(1, 4)]
    dp_peers = [{"dp": flip(dp, bit)} for bit in dp_bits]
    for peer in seq_peers + tensor_peers + dp_peers:
        pl.semaphore_signal(barrier, inc=1, device_id=peer, device_id_type=mesh_ids)
    pl.semaphore_wait(barrier, n + 2 + bits)

    links = Links(n, dp_count, x_send, x_recv, z_send, z_recv)
    expand = Scatter(links, 0, exp_ref, exp_xo, exp_xi, exp_acc, exp_zo, exp_zi, exp_out)
    project = Scatter(links, 1, proj_ref, proj_xo, proj_xi, proj_acc, proj_zo, proj_zi, proj_out)
    query = Scatter(links, 2, query_sc, query_xo, query_xi, query_acc, query_zo, query_zi, query_out)
    keyval = Scatter(links, 3, keyval_sc, keyval_xo, keyval_xi, keyval_acc, keyval_zo, keyval_zi, keyval_out)
    scatters = (expand, project, query, keyval)

    sibling, partner = {"tensor": flip(t, 1)}, {"tensor": flip(t, 2)}
    far_copy = remote(far_ref, far_in, y_send.at[0], y_recv.at[0], partner)
    far_copy.start()
    fetches[1].wait()
    expand.x_begin()
    fetches[0].wait()
    project.x_begin()

    def hop(out, inn, d, to, send, recv):
        return remote(out.at[d], inn.at[d], send.at[d], recv.at[d], {"seq": to})

    dq_acc[...] = jnp.zeros_like(dq_acc)
    for h in range(heads):
        rows = slice(h * HEAD_DIM, (h + 1) * HEAD_DIM)
        lse_sc[h] = lse_ref[h:h + 1, :]
        dot_sc[h] = jnp.sum(do_ref[rows, :].astype(F32) * of_ref[rows, :], axis=0, keepdims=True)

    nt = (((1,), (1,)), ((), ()))
    tn = (((0,), (0,)), ((), ()))

    def tile(h, cols, k, v, mask):
        rows = pl.ds(pl.multiple_of(h * HEAD_DIM, HEAD_DIM), HEAD_DIM)
        q, do = q_ref[rows, cols], do_ref[rows, cols]
        s = mask(lax.dot_general(k, q, tn, preferred_element_type=F32))
        p = jnp.exp(s - lse_sc[h, :, cols])
        dp = lax.dot_general(v, do, tn, preferred_element_type=F32)
        ds = (p * (dp - dot_sc[h, :, cols])).astype(BF16)
        p = p.astype(BF16)
        dv = lax.dot_general(do, p, nt, preferred_element_type=F32)
        dk = lax.dot_general(q, ds, nt, preferred_element_type=F32)
        dq_acc[rows, cols] += jnp.dot(k, ds, preferred_element_type=F32)
        return dk, dv

    def head_rows(h):
        return (pl.ds(pl.multiple_of(h * HEAD_DIM, HEAD_DIM), HEAD_DIM),
                pl.ds(pl.multiple_of(feats + h * HEAD_DIM, HEAD_DIM), HEAD_DIM))

    def columns(c):
        return pl.ds(pl.multiple_of(c * PCH, PCH), PCH)

    branch = branch_ref[0, 0]

    def full(source, c, block, total):
        limit = jnp.where(c == 0, n * PCH, branch) - block * PCH
        def mask(s):
            key = lax.broadcasted_iota(jnp.int32, (PCH, 1), 0)
            return s + jnp.where(key < limit, 0.0, big_negative)
        def body(h, carry):
            rows, vrows = head_rows(h)
            dk, dv = tile(h, columns(c), source[rows, :], source[vrows, :], mask)
            total[rows, :] += dk
            total[vrows, :] += dv
            return carry
        lax.fori_loop(0, heads, body, 0)

    def diag(i, carry):
        c, h = i // heads, i % heads
        rows, vrows = head_rows(h)
        cols = columns(c)
        def mask(s):
            key = lax.broadcasted_iota(jnp.int32, s.shape, 0)
            query = lax.broadcasted_iota(jnp.int32, s.shape, 1)
            return jnp.where(key <= query, s, big_negative)
        dk, dv = tile(h, cols, kv_ref[rows, cols], kv_ref[vrows, cols], mask)
        own_acc[rows, cols] = dk
        own_acc[vrows, cols] = dv
        return carry

    def far_blocks(i, carry):
        d = n - 1 - i

        @pl.when(z + d < n)
        def _():
            far_up[d - 1] = jnp.zeros(far_up.shape[1:], F32)
            full(all_ref.at[z + d], 1, z + d, far_up.at[d - 1])
            @pl.when(~has_down | (d == n - 1))
            def _():
                up_out[d - 1] = far_up[d - 1].astype(BF16)
                hop(up_out, up_in, d - 1, z + 1, up_send, up_recv).start()

        @pl.when(z >= d)
        def _():
            far_down[d - 1] = jnp.zeros(far_down.shape[1:], F32)
            def both(c, carry):
                full(all_ref.at[z - d], c, z - d, far_down.at[d - 1])
                return carry
            lax.fori_loop(0, 2, both, 0)
            @pl.when(~has_up | (d == n - 1))
            def _():
                down_out[d - 1] = far_down[d - 1].astype(BF16)
                hop(down_out, down_in, d - 1, z - 1, down_send, down_recv).start()
        return carry

    lax.fori_loop(0, n - 1, far_blocks, 0)

    def relays(i, carry):
        d = n - 2 - i

        @pl.when(d == 1)
        def _():
            lax.fori_loop(0, 2 * heads, diag, 0)
            full(kv_ref.at[:, 0:PCH], 1, z, own_acc.at[:, 0:PCH])

        @pl.when((z + d < n) & has_down)
        def _():
            hop(up_out, up_in, d, z, up_send, up_recv).wait_recv()
            up_out[d - 1] = (far_up[d - 1] + up_in[d].astype(F32)).astype(BF16)
            hop(up_out, up_in, d - 1, z + 1, up_send, up_recv).start()

        @pl.when((z >= d) & has_up)
        def _():
            hop(down_out, down_in, d, z, down_send, down_recv).wait_recv()
            down_out[d - 1] = (far_down[d - 1] + down_in[d].astype(F32)).astype(BF16)
            hop(down_out, down_in, d - 1, z - 1, down_send, down_recv).start()
        return carry

    lax.fori_loop(0, n - 2, relays, 0)
    expand.relay()
    project.relay()

    def place(k):
        owner = t
        for bit in (1, 2):
            turned = flip(owner, bit)
            if isinstance(k, int):
                owner = turned if k & bit else owner
            else:
                owner = jnp.where(lax.rem(lax.div(k, bit), 2) == 1, turned, owner)
        return pl.ds(pl.multiple_of(owner * share, share), share)

    rows = query_sc.shape[1]

    def weight_gradient(part, target):
        value = jnp.dot(part, normed_ref[...], preferred_element_type=F32).T
        for b in range(blocks):
            target[b] = value[b * rows : (b + 1) * rows, :]

    stacked[0:feats, :] = (dq_acc[...] * (1.0 / math.sqrt(HEAD_DIM))).astype(BF16)
    for one in fetches[2:]:
        one.wait()
    weight_gradient(stacked[0:feats, :], query_sc)
    query.x_begin()
    stacked[feats:, PCH:] = own_acc[:, PCH:].astype(BF16)

    def prepare(k, carry):
        value = tok_ref[place(k), :].astype(F32)
        centred = value - jnp.mean(value, axis=-1, keepdims=True)
        inverse = lax.rsqrt(jnp.mean(centred * centred, axis=-1, keepdims=True) + norm_eps)
        xhat_sc[k] = centred * inverse
        inv_sc[k] = jnp.broadcast_to(inverse, (share, 128))
        return carry

    lax.fori_loop(0, 4, prepare, 0)

    @pl.when(has_down)
    def _():
        hop(up_out, up_in, 0, z, up_send, up_recv).wait_recv()
        own_acc[:, 0:PCH] += up_in[0].astype(F32)
    @pl.when(has_up)
    def _():
        hop(down_out, down_in, 0, z, down_send, down_recv).wait_recv()
        own_acc[:, 0:PCH] += down_in[0].astype(F32)
    stacked[feats:, 0:PCH] = own_acc[:, 0:PCH].astype(BF16)

    weight_gradient(stacked[feats:, :], keyval_sc)
    keyval.x_begin()

    def grad_normed(k):
        mix[k] = lax.dot_general(stacked[:, place(k)], wa_ref[...], tn, preferred_element_type=F32)
        return mix[k]

    def core_copy(i):
        return remote(core_out.at[i], core_in.at[i], core_send.at[i], core_recv.at[i], sibling)

    core_out[0] = grad_normed(3).astype(BF16)
    core_copy(0).start()
    last = grad_normed(2)
    core_copy(0).wait_recv()
    y_out[...] = (last + core_in[0].astype(F32)).astype(BF16)
    y_copy = remote(y_out, y_in, y_send.at[1], y_recv.at[1], partner)
    y_copy.start()
    core_out[1] = grad_normed(1).astype(BF16)
    core_copy(1).start()
    query.relay()
    grad_normed(0)

    width = tensor_in.shape[2]
    tensor_in[t, 0:2, :] = jnp.zeros((2, width), F32)
    tensor_in[t, 2:6, :] = early_ref[...]
    tensor_in[t, 6:7, :] = esum_ref[...]
    tensor_in[t, 7:8, :] = jnp.zeros((1, width), F32)
    ones = jnp.ones((8, stacked.shape[1]), BF16)
    tensor_in[t, 7:8, 0 : 3 * feats] = lax.dot_general(ones, stacked[...], nt, preferred_element_type=F32)[0:1]

    def statistics(k, carry):
        tensor_in[t, 0:1, :] += jnp.sum(mix[k] * xhat_sc[k], axis=0, keepdims=True)
        tensor_in[t, 1:2, :] += jnp.sum(mix[k], axis=0, keepdims=True)
        return carry

    lax.fori_loop(0, 4, statistics, 0)

    def seq_copy(target, sender):
        return remote(seq_in.at[z], seq_in.at[sender], seq_send.at[target], seq_recv.at[sender], {"seq": target})

    def tensor_copy(target, sender):
        return remote(
            tensor_in.at[t], tensor_in.at[sender], tensor_send.at[target], tensor_recv.at[sender],
            {"tensor": target},
        )

    def dp_copy(i):
        return remote(dp_out.at[i], dp_in.at[i], dp_send.at[i], dp_recv.at[i], dp_peers[i])

    for d in range(1, 4):
        tensor_copy(lax.rem(t + d, 4), t).start()
    keyval.relay(range(0, 2))
    for d in range(1, 4):
        other = lax.rem(t + d, 4)
        tensor_copy(other, other).wait_recv()
    total = tensor_in[0]
    for i in range(1, 4):
        total = total + tensor_in[i]
    own = tensor_in[t]
    row = lax.broadcasted_iota(jnp.int32, own.shape, 0)
    dp_out[0] = jnp.where(row < 6, total, own)
    dp_copy(0).start()
    keyval.relay(range(2, n))
    for i in range(bits):
        dp_copy(i).wait_recv()
        value = dp_out[i] + dp_in[i]
        if i + 1 < bits:
            dp_out[i + 1] = value
            dp_copy(i + 1).start()
        else:
            seq_in[z] = value
    for d in range(1, n):
        seq_copy(lax.rem(z + d, n), z).start()

    core_copy(1).wait_recv()
    y_copy.wait_recv()
    mixed = mix[0] + core_in[1].astype(F32) + y_in[...].astype(F32)
    e = mixed * gain_ref[0:1, :]
    xhat = xhat_sc[0]
    gtok_ref[...] = (
        ghid_ref[...]
        + inv_sc[0][:, 0:1]
        * (e - jnp.mean(e, axis=-1, keepdims=True) - xhat * jnp.mean(e * xhat, axis=-1, keepdims=True))
    ).astype(BF16)
    far_copy.wait_recv()
    lout_ref[...] = (near_ref[...] + layer_scale * far_in[...].astype(F32)).astype(BF16)
    expand.z_end()
    project.z_end()
    query.z_end()
    for d in range(1, n):
        other = lax.rem(z + d, n)
        seq_copy(other, other).wait_recv()
    summed = seq_in[0]
    for i in range(1, n):
        summed = summed + seq_in[i]
    sums_ref[...] = summed
    keyval.z_end()

    for d in range(1, n):
        @pl.when(z + d < n)
        def _(): hop(up_out, up_in, d - 1, z + 1, up_send, up_recv).wait_send()
        @pl.when(z >= d)
        def _(): hop(down_out, down_in, d - 1, z - 1, down_send, down_recv).wait_send()
    for one in scatters:
        one.drain()
    far_copy.wait_send()
    y_copy.wait_send()
    for i in range(2):
        core_copy(i).wait_send()
    for d in range(1, n):
        seq_copy(lax.rem(z + d, n), z).wait_send()
    for d in range(1, 4):
        tensor_copy(lax.rem(t + d, 4), t).wait_send()
    for i in range(bits):
        dp_copy(i).wait_send()


def finish(
    n, dp_count, layer_scale, q, kv, kv_all, branch, do, of, lse, near, far,
    grad_expand, grad_proj, early, expand_terms, w_attn, normed_one, token_rows,
    grad_hidden, norm_gains,
):
    feats, rows = q.shape
    heads = feats // HEAD_DIM
    share, width = grad_hidden.shape
    blocks = dp_count * n
    bits = len(log_bits(dp_count))
    vm = pl.BlockSpec(memory_space=pltpu.VMEM)
    anywhere = pl.BlockSpec(memory_space=pl.ANY)
    slots = pltpu.VMEM((n - 1, 2 * feats, PCH), BF16)
    shape = jax.ShapeDtypeStruct
    sems = lambda count: pltpu.SemaphoreType.DMA((count,))
    block_rows = width // blocks
    proj_blocks = grad_proj.reshape(blocks, block_rows, feats)
    units = grad_expand.shape[1]
    fetched = [
        near, grad_expand.reshape(blocks, block_rows, units), proj_blocks, early, expand_terms, w_attn, normed_one, token_rows,
        grad_hidden, norm_gains,
    ]
    widths = [units, feats, feats, 2 * feats]
    scatter_scratch = []
    for columns in widths:
        scatter_scratch += scatter_buffers(n, dp_count, block_rows, columns)
    return pl.pallas_call(
        functools.partial(finish_kernel, n, dp_count, heads, layer_scale),
        out_shape=(
            shape((share, width), BF16),
            shape((share, width), BF16),
            *(shape((block_rows, columns), F32) for columns in widths),
            shape((8, width), F32),
        ),
        in_specs=[vm, vm, vm, pl.BlockSpec(memory_space=pltpu.SMEM)] + [vm] * 4 + [anywhere] * len(fetched),
        out_specs=(vm,) * 7,
        scratch_shapes=[
            pltpu.VMEM((feats, rows), F32),
            pltpu.VMEM((2 * feats, rows), F32),
            pltpu.VMEM((n - 1, 2 * feats, PCH), F32),
            pltpu.VMEM((n - 1, 2 * feats, PCH), F32),
            pltpu.VMEM((heads, 1, rows), F32),
            pltpu.VMEM((heads, 1, rows), F32),
            slots, slots, slots, slots,
            *(pltpu.VMEM(one.shape, one.dtype) for one in fetched),
            pltpu.VMEM((3 * feats, rows), BF16),
            pltpu.VMEM((4, share, width), F32),
            pltpu.VMEM((4, share, width), F32),
            pltpu.VMEM((4, share, 128), F32),
            pltpu.VMEM((blocks, block_rows, feats), F32),
            pltpu.VMEM((blocks, block_rows, 2 * feats), F32),
            *scatter_scratch,
            pltpu.VMEM((2, share, width), BF16),
            pltpu.VMEM((2, share, width), BF16),
            pltpu.VMEM((share, width), BF16),
            pltpu.VMEM((share, width), BF16),
            pltpu.VMEM((share, width), BF16),
            pltpu.VMEM((n, 8, width), F32),
            pltpu.VMEM((4, 8, width), F32),
            pltpu.VMEM((bits, 8, width), F32),
            pltpu.VMEM((bits, 8, width), F32),
            sems(n - 1), sems(n - 1), sems(n - 1), sems(n - 1),
            *scatter_sems(n, dp_count, 4),
            sems(2), sems(2), sems(2), sems(2), sems(n), sems(n), sems(4), sems(4), sems(bits), sems(bits),
            sems(len(fetched)),
        ],
        compiler_params=pltpu.CompilerParams(
            collective_id=2, has_side_effects=True, vmem_limit_bytes=60 * 2**20
        ),
        cost_estimate=pl.CostEstimate(flops=4 * 10**10, bytes_accessed=10**7, transcendentals=0),
        name="finish",
    )(q, kv, kv_all, branch, do, of, lse, far, *fetched)


def emit_kernel(
    feats, turned, con, lout, gtok, expand, proj, query, keyval, sums,
    lout_ref, gtok_ref, attn_ref, proj_ref, exp_ref, con_ref, bias_ref, branch_ref, units_ref, gains_ref, shifts_ref,
):
    lout_ref[...] = lout[...]
    gtok_ref[...] = gtok[...]
    attn_ref[0] = query[...]
    attn_ref[1] = keyval[:, 0:feats]
    attn_ref[2] = keyval[:, feats : 2 * feats]
    proj_ref[...] = proj[...].T if turned else proj[...]
    exp_ref[...] = expand[...]
    con_ref[...] = con[...]
    bias_ref[0:1, :] = sums[7:8, 0:feats]
    bias_ref[1:2, :] = sums[7:8, 2 * feats : 3 * feats]
    branch_ref[...] = sums[2:4, :]
    units_ref[...] = sums[6, :]
    for row, late, early in ((gains_ref, 0, 4), (shifts_ref, 1, 5)):
        row[0:1, :] = sums[late : late + 1, :]
        row[1:2, :] = sums[early : early + 1, :]


def emit(con, results):
    lout, gtok, expand, proj, query, keyval, sums = results
    rows, feats = query.shape
    share, width = lout.shape
    turned = rows % 8 == 0
    shape = jax.ShapeDtypeStruct
    vm = pl.BlockSpec(memory_space=pltpu.VMEM)
    outputs = pl.pallas_call(
        functools.partial(emit_kernel, feats, turned),
        out_shape=(
            shape((share, width), BF16), shape((share, width), BF16), shape((3, rows, feats), F32),
            shape((feats, rows) if turned else (rows, feats), F32), shape(expand.shape, F32),
            shape(con.shape, F32), shape((2, feats), F32), shape((2, width), F32),
            shape((expand.shape[1],), F32), shape((2, width), F32), shape((2, width), F32),
        ),
        in_specs=[vm] * 8,
        out_specs=(vm,) * 11,
        compiler_params=pltpu.CompilerParams(vmem_limit_bytes=60 * 2**20),
        name="emit",
    )(con, *results)
    lout, gtok, attn, proj, expand, con, bias, branch, units, gains, shifts = outputs
    whole = (1, 1, share, width)
    return (
        lout.reshape(whole), gtok.reshape(whole), attn, proj if turned else proj.T, expand, con.T,
        bias, branch, units, gains, shifts,
    )


def middle_kernel(
    n, dp_count, layer_scale, o_ref, tok_ref, cot_ref, wp_ref, we_ref, wc_ref, bb_ref, eb_ref, gain_ref, shift_ref,
    ghid_ref, near_ref, far_ref, gatt_ref, gproj_ref, gexp_ref, gcon_ref, sums_ref, esum_ref,
    ga_sc, mix_sc, n2, gm, act, gp, att, own_sc, xhat_sc, inv_sc, proj_sc,
    core_out, core_in, y_out, y_in, con_sc, con_xo, con_xi, con_acc, con_zo, con_zi,
    core_send, core_recv, y_send, y_recv, n2_send, n2_recv, att_send, att_recv, x_send, x_recv, z_send, z_recv,
):
    t = lax.axis_index("tensor")
    y, c = t // 2, t % 2
    sibling = y * 2 + (1 - c)
    partner = (1 - y) * 2 + c
    share = own_sc.shape[0]

    def block(k):
        if isinstance(k, int):
            return ((1 - y) if k >= 2 else y) * 2 + ((1 - c) if k % 2 else c)
        return jnp.where(k >= 2, 1 - y, y) * 2 + jnp.where(k % 2 == 1, 1 - c, c)

    def place(k):
        return pl.ds(pl.multiple_of(block(k) * share, share), share)

    barrier = pltpu.get_barrier_semaphore()
    for to in (sibling, partner):
        pl.semaphore_signal(barrier, inc=1, device_id={"tensor": to}, device_id_type=pl.DeviceIdType.MESH)
    links = Links(n, dp_count, x_send, x_recv, z_send, z_recv)
    peers = [{"seq": lax.rem(links.z + d, n)} for d in range(1, n)]
    peers += [{"dp": flip(links.dp, bit)} for bit in log_bits(dp_count)]
    for peer in peers:
        pl.semaphore_signal(barrier, inc=1, device_id=peer, device_id_type=pl.DeviceIdType.MESH)
    pl.semaphore_wait(barrier, 2 + len(peers))
    weights = Scatter(links, 0, con_sc, con_xo, con_xi, con_acc, con_zo, con_zi, gcon_ref)

    def copy(src, dst, send, recv, to):
        return pltpu.make_async_remote_copy(
            src_ref=src, dst_ref=dst, send_sem=send, recv_sem=recv,
            device_id={"tensor": to}, device_id_type=pl.DeviceIdType.MESH,
        )

    def core_copy(i):
        return copy(core_out.at[i], core_in.at[i], core_send.at[i], core_recv.at[i], sibling)

    part = share // 2
    parts = [slice(h * part, (h + 1) * part) for h in range(2)]

    def own_rows(h):
        return pl.ds(pl.multiple_of(block(0) * share + h * part, part), part)

    def y_copy(i, h):
        rows, sem = pl.ds(h * part, part), 2 * i + h
        return copy(y_out.at[i, rows], y_in.at[i, rows], y_send.at[sem], y_recv.at[sem], partner)

    def gather(ref, send, recv):
        rows = [pl.ds(h * part, part) for h in range(2)]
        return (
            [copy(ref.at[0, rows[h]], ref.at[2, rows[h]], send.at[h], recv.at[h], partner) for h in range(2)],
            copy(ref.at[0], ref.at[1], send.at[2], recv.at[2], sibling),
            [copy(ref.at[2, rows[h]], ref.at[3, rows[h]], send.at[3 + h], recv.at[3 + h], sibling) for h in range(2)],
        )

    tn = (((0,), (0,)), ((), ()))
    nt = (((1,), (1,)), ((), ()))

    def project(k):
        return lax.dot_general(o_ref[:, place(k)], wp_ref[...], tn, preferred_element_type=F32)

    core_out[0] = project(3).astype(BF16)
    core_copy(0).start()
    own_sc[...] = project(2)
    core_out[1] = project(1).astype(BF16)
    core_copy(1).start()
    core_copy(0).wait_recv()
    for h in range(2):
        y_out[0, parts[h], :] = (own_sc[parts[h], :] + core_in[0, parts[h], :].astype(F32)).astype(BF16)
        y_copy(0, h).start()
    own_sc[...] = project(0)

    def before(k, carry):
        g = (cot_ref[place(k), :].astype(F32) * layer_scale).astype(BF16)
        gm[k] = g
        ga_sc[k] = lax.dot_general(g, wc_ref[...], nt, preferred_element_type=F32)
        return carry

    lax.fori_loop(0, 4, before, 0)
    core_copy(1).wait_recv()
    own_sc[...] += core_in[1].astype(F32)
    across, near, on = gather(n2, n2_send, n2_recv)
    for h in range(2):
        rows = parts[h]
        y_copy(0, h).wait_recv()
        hidden = tok_ref[own_rows(h), :].astype(F32) + layer_scale * (
            own_sc[rows, :] + y_in[0, rows, :].astype(F32) + bb_ref[0:1, :]
        )
        centred = hidden - jnp.mean(hidden, axis=-1, keepdims=True)
        inverse = lax.rsqrt(jnp.mean(centred * centred, axis=-1, keepdims=True) + norm_eps)
        xhat = centred * inverse
        n2[0, rows, :] = (xhat * gain_ref[1:2, :] + shift_ref[1:2, :]).astype(BF16)
        across[h].start()
        near_ref[rows, :] = hidden + layer_scale * bb_ref[1:2, :]
        xhat_sc[rows, :] = xhat
        inv_sc[rows, :] = jnp.broadcast_to(inverse, (part, inv_sc.shape[1]))
    near.start()
    esum_ref[...] = jnp.zeros_like(esum_ref)

    def process(k, carry):
        @pl.when(k == 1)
        def _():
            near.wait_recv()

        @pl.when(k == 2)
        def _():
            for h in range(2):
                across[h].wait_recv()
                on[h].start()

        @pl.when(k == 3)
        def _():
            for h in range(2):
                on[h].wait_recv()

        v = jnp.dot(n2[k], we_ref[...], preferred_element_type=F32) + eb_ref[...]
        square = v * v
        th = jnp.tanh(math.sqrt(2.0 / math.pi) * (v + 0.044715 * (v * square)))
        cdf = 0.5 * (1.0 + th)
        act[k] = (v * cdf).astype(BF16)
        slope = cdf + 0.5 * v * (1.0 - th * th) * (
            math.sqrt(2.0 / math.pi) * (1.0 + 3 * 0.044715 * square)
        )
        g = (slope * ga_sc[k]).astype(BF16)
        gp[k] = g
        esum_ref[...] += jnp.sum(g.astype(F32), axis=0, keepdims=True)
        mix_sc[k] = lax.dot_general(g, we_ref[...], nt, preferred_element_type=F32)
        return carry

    lax.fori_loop(0, 4, process, 0)
    core_out[2] = mix_sc[3].astype(BF16)
    core_copy(2).start()
    core_out[3] = mix_sc[1].astype(BF16)
    core_copy(3).start()
    core_copy(2).wait_recv()
    for h in range(2):
        y_out[1, parts[h], :] = (mix_sc[2, parts[h], :] + core_in[2, parts[h], :].astype(F32)).astype(BF16)
        y_copy(1, h).start()

    rows = 4 * share
    width = gm.shape[2]
    value = lax.dot_general(
        gm[...].reshape(rows, width), act[...].reshape(rows, -1), tn, preferred_element_type=F32
    )
    size = con_sc.shape[1]
    for b in range(con_sc.shape[0]):
        con_sc[b] = value[b * size : (b + 1) * size, :]
    weights.x_begin()
    gexp_ref[...] = lax.dot_general(
        n2[...].reshape(rows, width), gp[...].reshape(rows, -1), tn, preferred_element_type=F32
    )

    def contract(k):
        return jnp.dot(act[k], wc_ref[...], preferred_element_type=F32)

    core_out[4] = contract(3).astype(BF16)
    core_copy(4).start()
    core_out[5] = contract(1).astype(BF16)
    core_copy(5).start()
    near_ref[...] += layer_scale * contract(0)
    last = contract(2)
    core_copy(4).wait_recv()
    far_ref[...] = (last + core_in[4].astype(F32)).astype(BF16)
    core_copy(5).wait_recv()
    near_ref[...] += layer_scale * core_in[5].astype(F32)
    weights.relay(range(0, 1))

    core_copy(3).wait_recv()
    across_b, near_b, on_b = gather(att, att_send, att_recv)
    sums_ref[1:2, :] = jnp.sum(gm[0].astype(F32), axis=0, keepdims=True)
    for h in range(2):
        rows = parts[h]
        y_copy(1, h).wait_recv()
        mixed = mix_sc[0, rows, :] + core_in[3, rows, :].astype(F32) + y_in[1, rows, :].astype(F32)
        e = mixed * gain_ref[1:2, :]
        xhat = xhat_sc[rows, :]
        grad_hidden = cot_ref[own_rows(h), :].astype(F32) + inv_sc[rows, 0:1] * (
            e - jnp.mean(e, axis=-1, keepdims=True) - xhat * jnp.mean(e * xhat, axis=-1, keepdims=True)
        )
        g = (grad_hidden * layer_scale).astype(BF16)
        att[0, rows, :] = g
        across_b[h].start()
        ghid_ref[rows, :] = grad_hidden
        for row, terms in ((0, g.astype(F32)), (2, mixed * xhat), (3, mixed)):
            term = jnp.sum(terms, axis=0, keepdims=True)
            if h == 0:
                sums_ref[row : row + 1, :] = term
            else:
                sums_ref[row : row + 1, :] += term
    near_b.start()

    proj_sc[...] = jnp.zeros_like(proj_sc)
    weights.relay(range(1, n))

    def after(k, carry):
        @pl.when(k == 1)
        def _():
            near_b.wait_recv()

        @pl.when(k == 2)
        def _():
            for h in range(2):
                across_b[h].wait_recv()
                on_b[h].start()

        @pl.when(k == 3)
        def _():
            for h in range(2):
                on_b[h].wait_recv()

        gatt_ref[:, place(k)] = lax.dot_general(
            wp_ref[...], att[k], nt, preferred_element_type=F32
        ).astype(BF16)
        proj_sc[...] += jnp.dot(o_ref[:, place(k)], att[k], preferred_element_type=F32)
        return carry

    lax.fori_loop(0, 4, after, 0)
    gproj_ref[...] = proj_sc[...].T
    weights.z_end()
    weights.drain()
    for i in range(6):
        core_copy(i).wait_send()
    for i in range(2):
        for h in range(2):
            y_copy(i, h).wait_send()
    for one in (*across, near, *on, *across_b, near_b, *on_b):
        one.wait_send()


def middle(
    n, dp_count, layer_scale, attended, token_rows, cotangent_rows, w_proj, w_expand, w_contract,
    branch_bias, expand_bias, norm_gains, norm_shifts,
):
    rows, width = token_rows.shape
    feats, hidden_units = w_proj.shape[0], w_expand.shape[1]
    share = rows // 4
    size = width // (dp_count * n)
    vm = pl.BlockSpec(memory_space=pltpu.VMEM)
    shape = jax.ShapeDtypeStruct
    slots = lambda columns, kind: pltpu.VMEM((4, share, columns), kind)
    sems = lambda count: pltpu.SemaphoreType.DMA((count,))
    return pl.pallas_call(
        functools.partial(middle_kernel, n, dp_count, layer_scale),
        out_shape=(
            shape((share, width), F32),
            shape((share, width), F32),
            shape((share, width), BF16),
            shape((feats, rows), BF16),
            shape((width, feats), F32),
            shape((width, hidden_units), F32),
            shape((size, hidden_units), F32),
            shape((4, width), F32),
            shape((1, hidden_units), F32),
        ),
        in_specs=[vm] * 10,
        out_specs=(vm,) * 9,
        scratch_shapes=[
            slots(hidden_units, F32),
            slots(width, F32),
            slots(width, BF16),
            slots(width, BF16),
            slots(hidden_units, BF16),
            slots(hidden_units, BF16),
            slots(width, BF16),
            pltpu.VMEM((share, width), F32),
            pltpu.VMEM((share, width), F32),
            pltpu.VMEM((share, 128), F32),
            pltpu.VMEM((feats, width), F32),
            pltpu.VMEM((6, share, width), BF16),
            pltpu.VMEM((6, share, width), BF16),
            pltpu.VMEM((2, share, width), BF16),
            pltpu.VMEM((2, share, width), BF16),
            pltpu.VMEM((dp_count * n, size, hidden_units), F32),
            *scatter_buffers(n, dp_count, size, hidden_units),
            sems(6), sems(6), sems(4), sems(4), sems(5), sems(5), sems(5), sems(5),
            *scatter_sems(n, dp_count, 1),
        ],
        compiler_params=pltpu.CompilerParams(
            collective_id=3, has_side_effects=True, vmem_limit_bytes=56 * 2**20
        ),
        cost_estimate=pl.CostEstimate(flops=5 * 10**10, bytes_accessed=2 * 10**7, transcendentals=0),
        name="middle",
    )(
        attended, token_rows, cotangent_rows, w_proj, w_expand, w_contract,
        branch_bias, expand_bias, norm_gains, norm_shifts,
    )


def shards(
    tokens,
    branch,
    w_attn,
    w_proj,
    w_expand,
    w_contract,
    attn_bias,
    branch_bias,
    expand_bias,
    norm_gains,
    norm_shifts,
    cotangent,
):
    seq_count = lax.axis_size("seq")
    width = tokens.shape[3]
    row_count = tokens.shape[2]
    share = row_count // lax.axis_size("tensor")
    local_width = w_attn.shape[2]
    layer_scale = 1.0 / math.sqrt(LAYERS)

    token_rows = tokens.reshape(row_count, width)
    cotangent_rows = cotangent.reshape(row_count, width)
    w_attn = jnp.transpose(w_attn, (0, 2, 1)).reshape(3 * local_width, width)
    attended, attended_wide, logsum, all_kv, queries, own_kv, normed_one = attend_forward(
        seq_count, token_rows, w_attn, attn_bias, norm_gains, norm_shifts, branch
    )
    (
        grad_hidden, mlp_near, mlp_far, grad_attended,
        grad_proj, grad_expand, grad_contract, early, expand_terms,
    ) = middle(
        seq_count, lax.axis_size("dp"), layer_scale, attended, token_rows, cotangent_rows, w_proj, w_expand, w_contract,
        branch_bias, expand_bias.reshape(1, -1), norm_gains, norm_shifts,
    )
    return emit(grad_contract, finish(
        seq_count, lax.axis_size("dp"), layer_scale, queries, own_kv, all_kv, branch, grad_attended,
        attended_wide, logsum, mlp_near, mlp_far, grad_expand, grad_proj, early,
        expand_terms, w_attn, normed_one, token_rows, grad_hidden, norm_gains,
    ))


def solution(mesh):
    placed = (
        P("dp", "seq", None, None),
        P("dp", "seq"),
        P(None, None, "tensor"),
        P("tensor", None),
        P(None, "tensor"),
        P("tensor", None),
        P(None, "tensor"),
        P(),
        P("tensor"),
        P(),
        P(),
        P("dp", "seq", None, None),
    )
    return jax.shard_map(
        shards,
        mesh=mesh,
        in_specs=placed,
        out_specs=(
            P("dp", "seq", "tensor", None),
            P("dp", "seq", "tensor", None),
            P(None, ("dp", "seq"), "tensor"),
            P("tensor", ("dp", "seq")),
            P(("dp", "seq"), "tensor"),
            P("tensor", ("dp", "seq")),
            P(None, "tensor"),
            P(),
            P("tensor"),
            P(),
            P(),
        ),
        check_vma=False,
    )
```
